32 devices in a mesh: cells: 2 (over x), fh: 16 (over z, y, core).
Axes of the slice: x: 2, y: 2, z: 4, core: 2. Of those that a mesh axis runs over, the one named last changes fastest.
Arguments:
- received_time_rows: bfloat16 [4096, 3, 2, 4096], P(('cells', 'fh')), parts along dimension 0, may hold values from -24 to 24
- pilots: int32 [128], P('cells'), parts along dimension 0, may hold values from 0 to 63, as said below
- active_users: int32 [128], P('cells'), parts along dimension 0, may hold values 0 or 1
- allocation: int32 [256, 64], P(('cells', 'fh')), parts along dimension 0, may hold values 0 or 1
- loading: float32 [128], P('cells'), parts along dimension 0, may hold values from 0.25 to 4
Outputs:
- equalized: float32 [128, 1, 2, 4096], P(('cells', 'fh')), parts along dimension 0
The draws below stay inside these ranges and needn't reach their ends.
There are 2 independent parts, one for each index of `cells`. The reference program is written for one: setup_inputs(seed, part) draws one part's arguments, and reference() takes and returns one part's arrays. A program takes and returns all parts, laid end to end along the dimension named above; each array names one. Nothing has to cross between parts.
Inputs may be any that keep to these rules, and one draw needn't show every extreme that they name: `pilots`: the 64 pilot sequences of a cell are distinct.
All inputs are finite; a program needn't handle non-finite values. No bound on the sum of `allocation` on one device may be relied on, other than what follows from the above.
Results may differ from the reference program's by a relative error of at most 0.0076.
Values may be sent and summed in bfloat16 or wider, within the bound.
No kernel may reach another device: no remote copies, remote signals or barrier semaphores. Data moves between devices by JAX's collectives and lax.ppermute only.
A program may use at most 128 MiB of HBM per device.

```python
import math
import jax
import jax.numpy as jnp
from jax import lax

SUBCARRIER_COUNT = 4096
K = 64
ANTENNAS_LOCAL = 128
PSYM = 2
DSYM = 1
B = 32
FA = 16
FB = 256
SYMBOLS_TOTAL = 3
BLOCKS = 128
ANTENNA_COUNT = 2048


def draw_received_time_rows(key, part):
    gain_random_key, noise_random_key = jax.random.split(key, 2)
    channel_gain_rows = jnp.exp(jax.random.uniform(gain_random_key, (ANTENNA_COUNT, 1, 1, 1), jnp.float32, math.log(0.4), math.log(4.0)))
    noise_portion = jnp.clip(jax.random.normal(noise_random_key, (ANTENNA_COUNT, SYMBOLS_TOTAL, 2, SUBCARRIER_COUNT), jnp.float32), -6.0, 6.0)
    values = channel_gain_rows * noise_portion
    return values.astype(jnp.bfloat16)


def draw_pilots(key, part):
    return jax.random.permutation(key, PSYM * B)[:K].astype(jnp.int32)


def with_ends(entries, key, least, largest):
    index_at = [jax.random.randint(jax.random.fold_in(key, axis), (), 0, length) for axis, length in enumerate(entries.shape)]
    main_axis = entries.shape.index(max(entries.shape))
    neighbour = index_at[:main_axis] + [(index_at[main_axis] + 1) % entries.shape[main_axis]] + index_at[main_axis + 1:]
    return entries.at[tuple(index_at)].set(least).at[tuple(neighbour)].set(largest)


def setup_inputs(seed: int = 0, part: int = 0) -> dict:
    streams_of = jax.random.split(jax.random.key(seed), 6)
    part_keys = jax.random.split(jax.random.fold_in(streams_of[5], part), 6)
    received_time_rows = draw_received_time_rows(jax.random.fold_in(jax.random.fold_in(streams_of[5], part), 71), part)
    pilots = draw_pilots(jax.random.fold_in(jax.random.fold_in(streams_of[5], part), 71), part)
    active_users = with_ends((jax.random.randint(part_keys[2], (K,), 0, 4) < 3).astype(jnp.int32), jax.random.fold_in(part_keys[2], 1), 0, 1)
    allocation = with_ends((jax.random.randint(part_keys[3], (BLOCKS, K), 0, 4) < 3).astype(jnp.int32), jax.random.fold_in(part_keys[3], 1), 0, 1)
    loading = jnp.clip(jnp.exp(jax.random.uniform(part_keys[4], (K,), jnp.float32, math.log(0.25), math.log(4.0))), 0.25, 4.0)
    return {"received_time_rows": received_time_rows, "pilots": pilots, "active_users": active_users, "allocation": allocation, "loading": loading}


def product(form, left, right):
    return jnp.einsum(form, left.astype(jnp.float32), right.astype(jnp.float32))

def dft_table(length):
    indices = jnp.arange(length, dtype=jnp.int32)
    phase_index = indices[:, None] * indices[None, :] % length
    angles = phase_index.astype(jnp.float32) * (2.0 * math.pi / length)
    cos_part = jnp.cos(angles)
    sin_part = jnp.sin(angles)
    layout = jnp.stack([jnp.stack([cos_part, -sin_part], 1), jnp.stack([sin_part, cos_part], 1)], 0)
    return layout.astype(jnp.bfloat16)

def twiddle_parts():
    inner_idx = jnp.arange(FA, dtype=jnp.int32)
    outer_idx = jnp.arange(FB, dtype=jnp.int32)
    phase_index = inner_idx[:, None] * outer_idx[None, :] % SUBCARRIER_COUNT
    angles = phase_index.astype(jnp.float32) * (2.0 * math.pi / SUBCARRIER_COUNT)
    factor = 1.0 / math.sqrt(SUBCARRIER_COUNT)
    return (jnp.cos(angles) * factor, jnp.sin(angles) * factor)

def spectra(samples):
    antennas_here = samples.shape[0]
    symbol_count = samples.shape[1]
    shaped = samples.reshape(antennas_here, symbol_count, 2, FA, FB)
    section_one = product('ascnm,cndk->sdkma', shaped, dft_table(FA))
    cos_part, sin_part = twiddle_parts()
    cos_part = cos_part[:, :, None]
    sin_part = sin_part[:, :, None]
    real_part = section_one[:, 0] * cos_part + section_one[:, 1] * sin_part
    imag_part = section_one[:, 1] * cos_part - section_one[:, 0] * sin_part
    section_one = jnp.stack([real_part, imag_part], 1).astype(jnp.bfloat16)
    section_two = product('sckma,cmdj->sdkja', section_one, dft_table(FB))
    return section_two.astype(jnp.bfloat16)

def split_blocks(spectrum):
    width_b = B // FA
    shape_in = spectrum.shape
    return spectrum.reshape(shape_in[0], 2, FA, shape_in[3] // width_b, width_b, shape_in[4])

def code_table(pilots):
    width_b = B // FA
    position = jnp.arange(PSYM, dtype=jnp.int32)[:, None, None] * B + jnp.arange(FA, dtype=jnp.int32)[None, :, None] + FA * jnp.arange(width_b, dtype=jnp.int32)[None, None, :]
    phase_index = pilots[:, None, None, None] * position[None] % (PSYM * B)
    angles = phase_index.astype(jnp.float32) * (2.0 * math.pi / (PSYM * B))
    factor = 1.0 / math.sqrt(PSYM * B)
    cos_part = jnp.cos(angles) * factor
    sin_part = jnp.sin(angles) * factor
    rows_real = jnp.stack([cos_part, sin_part], 2)
    rows_imag = jnp.stack([-sin_part, cos_part], 2)
    return jnp.stack([rows_real, rows_imag], 0).astype(jnp.bfloat16)

def block_terms(pilot_part, data_part, code_rows):
    channel = product('tcarbm,dktcab->rdkm', pilot_part, code_rows).astype(jnp.bfloat16)
    gram = product('rdkm,relm->rdkel', channel, channel)
    gram_real = gram[:, 0, :, 0] + gram[:, 1, :, 1]
    gram_imag = gram[:, 0, :, 1] - gram[:, 1, :, 0]
    matched = product('rdkm,tcarbm->rdktcab', channel, data_part)
    matched_real = matched[:, 0, :, :, 0] + matched[:, 1, :, :, 1]
    matched_imag = matched[:, 0, :, :, 1] - matched[:, 1, :, :, 0]
    blocks = matched_real.shape[0]
    user_count = matched_real.shape[1]
    matched_real = matched_real.reshape(blocks, user_count, -1)
    matched_imag = matched_imag.reshape(blocks, user_count, -1)
    left_half = jnp.stack([gram_real, gram_imag], 1)
    right_half = jnp.stack([matched_real, matched_imag], 1)
    return jnp.concatenate([left_half, right_half], 3)

def mmse_equalizer(packed_layout, served_users, loading, antennas):
    user_count = served_users.shape[1]
    pair_mask = served_users[:, :, None] * served_users[:, None, :]
    diagonal = jnp.eye(user_count, dtype=jnp.float32) * loading[None, :]
    sys_real = pair_mask * packed_layout[:, 0, :, :user_count] / antennas + diagonal[None]
    sys_imag = pair_mask * packed_layout[:, 1, :, :user_count] / antennas
    root_count = math.sqrt(antennas)
    side_real = served_users[:, :, None] * packed_layout[:, 0, :, user_count:] / root_count
    side_imag = served_users[:, :, None] * packed_layout[:, 1, :, user_count:] / root_count
    matrix = jnp.concatenate([jnp.concatenate([sys_real, -sys_imag], 2), jnp.concatenate([sys_imag, sys_real], 2)], 1)
    right_side = jnp.concatenate([side_real, side_imag], 1)
    factor_low = jnp.linalg.cholesky(matrix)
    solved = jax.scipy.linalg.cho_solve((factor_low, True), right_side)
    blocks = solved.shape[0]
    solved = solved.reshape(blocks, 2, user_count, -1, FA, B // FA)
    solved = jnp.transpose(solved, (2, 3, 1, 0, 5, 4))
    return solved.reshape(user_count, solved.shape[1], 2, -1)

def reference(received_time_rows, pilots, active_users, allocation, loading):
    code_rows = code_table(pilots)
    antenna_groups = received_time_rows.reshape(ANTENNA_COUNT // ANTENNAS_LOCAL, ANTENNAS_LOCAL, SYMBOLS_TOTAL, 2, SUBCARRIER_COUNT)

    def accumulate(running, samples):
        spectrum = spectra(samples)
        update = block_terms(split_blocks(spectrum[:PSYM]), split_blocks(spectrum[PSYM:]), code_rows)
        return (running + update, None)
    initial = jnp.zeros((BLOCKS, 2, K, K + DSYM * B), jnp.float32)
    packed_layout, unused = lax.scan(accumulate, initial, antenna_groups)
    served_users = active_users.astype(jnp.float32)[None, :] * allocation.astype(jnp.float32)
    return mmse_equalizer(packed_layout, served_users, loading, ANTENNA_COUNT)
```

```python
import math

import jax
import jax.numpy as jnp
from jax import lax
from jax.experimental import pallas as pl
from jax.experimental.pallas import tpu as pltpu
from jax.sharding import PartitionSpec as P

SUBCARRIER_COUNT = 4096
PSYM = 2
B = 32
FA = 16
FB = 256

PANEL = 8
PREC = lax.Precision.HIGHEST


def _solve_body(a_ref, b_ref, x_ref, s_ref, lt_ref, l_ref):
    nb, n, _ = a_ref.shape
    s_ref[...] = a_ref[...]
    x_ref[...] = b_ref[...]
    lane = lax.broadcasted_iota(jnp.int32, (1, n), 1)

    def panel(p, carry):
        j0 = pl.multiple_of(p * PANEL, PANEL)
        rows = [s_ref[b, pl.ds(j0, PANEL), :] for b in range(nb)]
        xts = [x_ref[b] for b in range(nb)]
        factors = [[] for b in range(nb)]
        for t in range(PANEL):
            j = j0 + t
            hit = lane == j
            keep = lane >= j
            after = lane > j
            for b in range(nb):
                d = jnp.sum(jnp.where(hit, rows[b][t:t + 1, :], 0.0), axis=1, keepdims=True)
                inv = 1.0 / jnp.sqrt(d)
                l = jnp.where(keep, rows[b][t:t + 1, :], 0.0) * inv
                col = jnp.sum(jnp.where(hit, rows[b], 0.0), axis=1, keepdims=True) * inv
                rows[b] = rows[b] - col * l
                y = jnp.sum(jnp.where(hit, xts[b], 0.0), axis=1, keepdims=True) * inv
                xts[b] = jnp.where(hit, y, xts[b] - y * jnp.where(after, l, 0.0))
                factors[b].append(l)
        for b in range(nb):
            block = jnp.concatenate(factors[b], axis=0)
            lt_ref[b, pl.ds(j0, PANEL), :] = block
            x_ref[b] = xts[b]
            update = lax.dot_general(
                block, block, (((0,), (0,)), ((), ())),
                precision=PREC, preferred_element_type=jnp.float32)
            s_ref[b] = s_ref[b] - update
        return carry

    lax.fori_loop(0, n // PANEL, panel, 0)
    for b in range(nb):
        l_ref[b] = jnp.transpose(lt_ref[b])

    def backward(t, carry):
        i = n - 1 - t
        for b in range(nb):
            lrow = l_ref[b, pl.ds(i, 1), :]
            lii = jnp.sum(jnp.where(lane == i, lrow, 0.0), axis=1, keepdims=True)
            yt = x_ref[b]
            xi = jnp.sum(jnp.where(lane == i, yt, 0.0), axis=1, keepdims=True) / lii
            x_ref[b] = jnp.where(lane == i, xi, yt - xi * jnp.where(lane < i, lrow, 0.0))
        return carry

    lax.fori_loop(0, n, backward, 0)


def spd_solve_t(matrix, rhs_t):
    nb, n, _ = matrix.shape
    return pl.pallas_call(
        _solve_body,
        out_shape=jax.ShapeDtypeStruct(rhs_t.shape, jnp.float32),
        scratch_shapes=[
            pltpu.VMEM((nb, n, n), jnp.float32),
            pltpu.VMEM((nb, n, n), jnp.float32),
            pltpu.VMEM((nb, n, n), jnp.float32),
        ],
    )(matrix, rhs_t)


def dft_table(length):
    indices = jnp.arange(length, dtype=jnp.int32)
    phase_index = indices[:, None] * indices[None, :] % length
    angles = phase_index.astype(jnp.float32) * (2.0 * math.pi / length)
    cos_part = jnp.cos(angles)
    sin_part = jnp.sin(angles)
    layout = jnp.stack([jnp.stack([cos_part, -sin_part], 1), jnp.stack([sin_part, cos_part], 1)], 0)
    return layout.astype(jnp.bfloat16)


def twiddle_parts():
    inner_idx = jnp.arange(FA, dtype=jnp.int32)
    outer_idx = jnp.arange(FB, dtype=jnp.int32)
    phase_index = inner_idx[:, None] * outer_idx[None, :] % SUBCARRIER_COUNT
    angles = phase_index.astype(jnp.float32) * (2.0 * math.pi / SUBCARRIER_COUNT)
    factor = 1.0 / math.sqrt(SUBCARRIER_COUNT)
    return (jnp.cos(angles) * factor, jnp.sin(angles) * factor)


def spectra(samples):
    antennas_here = samples.shape[0]
    symbol_count = samples.shape[1]
    shaped = samples.reshape(antennas_here, symbol_count, 2, FA, FB)
    section_one = jnp.einsum(
        "ascnm,cndk->sdkma", shaped, dft_table(FA), preferred_element_type=jnp.float32
    )
    cos_part, sin_part = twiddle_parts()
    cos_part = cos_part[:, :, None]
    sin_part = sin_part[:, :, None]
    real_part = section_one[:, 0] * cos_part + section_one[:, 1] * sin_part
    imag_part = section_one[:, 1] * cos_part - section_one[:, 0] * sin_part
    section_one = jnp.stack([real_part, imag_part], 1).astype(jnp.bfloat16)
    section_two = jnp.einsum(
        "sckma,cmdj->sdkja", section_one, dft_table(FB), preferred_element_type=jnp.float32
    )
    return section_two.astype(jnp.bfloat16)


def split_blocks(spectrum):
    width_b = B // FA
    shape_in = spectrum.shape
    return spectrum.reshape(shape_in[0], 2, FA, shape_in[3] // width_b, width_b, shape_in[4])


def code_table(pilots):
    width_b = B // FA
    position = (
        jnp.arange(PSYM, dtype=jnp.int32)[:, None, None] * B
        + jnp.arange(FA, dtype=jnp.int32)[None, :, None]
        + FA * jnp.arange(width_b, dtype=jnp.int32)[None, None, :]
    )
    phase_index = pilots[:, None, None, None] * position[None] % (PSYM * B)
    angles = phase_index.astype(jnp.float32) * (2.0 * math.pi / (PSYM * B))
    factor = 1.0 / math.sqrt(PSYM * B)
    cos_part = jnp.cos(angles) * factor
    sin_part = jnp.sin(angles) * factor
    rows_real = jnp.stack([cos_part, sin_part], 2)
    rows_imag = jnp.stack([-sin_part, cos_part], 2)
    return jnp.stack([rows_real, rows_imag], 0).astype(jnp.bfloat16)


def block_terms(pilot_part, data_part, code_rows):
    channel = jnp.einsum(
        "tcarbm,dktcab->rdkm", pilot_part, code_rows, preferred_element_type=jnp.float32
    ).astype(jnp.bfloat16)
    gram = jnp.einsum("rdkm,relm->rdkel", channel, channel, preferred_element_type=jnp.float32)
    gram_real = gram[:, 0, :, 0] + gram[:, 1, :, 1]
    gram_imag = gram[:, 0, :, 1] - gram[:, 1, :, 0]
    matched = jnp.einsum(
        "rdkm,tcarbm->rdktcab", channel, data_part, preferred_element_type=jnp.float32
    )
    matched_real = matched[:, 0, :, :, 0] + matched[:, 1, :, :, 1]
    matched_imag = matched[:, 0, :, :, 1] - matched[:, 1, :, :, 0]
    blocks = matched_real.shape[0]
    user_count = matched_real.shape[1]
    matched_real = matched_real.reshape(blocks, user_count, -1)
    matched_imag = matched_imag.reshape(blocks, user_count, -1)
    left_half = jnp.stack([gram_real, gram_imag], 1)
    right_half = jnp.stack([matched_real, matched_imag], 1)
    return jnp.concatenate([left_half, right_half], 3)


def mmse_equalizer(packed_layout, served_users, loading, antennas):
    user_count = served_users.shape[1]
    pair_mask = served_users[:, :, None] * served_users[:, None, :]
    diagonal = jnp.eye(user_count, dtype=jnp.float32) * loading[None, :]
    sys_real = pair_mask * packed_layout[:, 0, :, :user_count] / antennas + diagonal[None]
    sys_imag = pair_mask * packed_layout[:, 1, :, :user_count] / antennas
    root_count = math.sqrt(antennas)
    side_real = served_users[:, :, None] * packed_layout[:, 0, :, user_count:] / root_count
    side_imag = served_users[:, :, None] * packed_layout[:, 1, :, user_count:] / root_count
    matrix = jnp.concatenate(
        [jnp.concatenate([sys_real, -sys_imag], 2), jnp.concatenate([sys_imag, sys_real], 2)], 1
    )
    right_side = jnp.concatenate([side_real, side_imag], 1)
    solved = jnp.swapaxes(spd_solve_t(matrix, jnp.swapaxes(right_side, 1, 2)), 1, 2)
    blocks = solved.shape[0]
    solved = solved.reshape(blocks, 2, user_count, -1, FA, B // FA)
    solved = jnp.transpose(solved, (2, 3, 1, 0, 5, 4))
    return solved.reshape(user_count, solved.shape[1], 2, -1)


def on_device(received_time_rows, pilots, active_users, allocation, loading):
    spectrum = spectra(received_time_rows)
    code_rows = code_table(pilots)
    pilot_part = lax.all_to_all(spectrum[:PSYM], "fh", split_axis=3, concat_axis=4, tiled=True)
    data_part = lax.all_to_all(spectrum[PSYM:], "fh", split_axis=3, concat_axis=4, tiled=True)
    antenna_total = pilot_part.shape[4]
    packed_layout = block_terms(split_blocks(pilot_part), split_blocks(data_part), code_rows)
    served_users = active_users.astype(jnp.float32)[None, :] * allocation.astype(jnp.float32)
    result = mmse_equalizer(packed_layout, served_users, loading, antenna_total)
    return lax.all_to_all(result, "fh", split_axis=0, concat_axis=3, tiled=True)


def solution(mesh):
    return jax.shard_map(
        on_device,
        mesh=mesh,
        in_specs=(
            P(("cells", "fh"), None, None, None),
            P("cells"),
            P("cells"),
            P(("cells", "fh"), None),
            P("cells"),
        ),
        out_specs=P(("cells", "fh"), None, None, None),
        check_vma=False,
    )
```

```python
import functools
import math

import jax
import jax.numpy as jnp
from jax import lax
from jax.experimental import pallas as pl
from jax.experimental.pallas import tpu as pltpu
from jax.sharding import PartitionSpec as P

SUBCARRIER_COUNT = 4096
PSYM = 2
B = 32
FA = 16
FB = 256

PANEL = 8
PREC = lax.Precision.HIGHEST


def _solve_body(a_ref, b_ref, x_ref, s_ref, lt_ref, l_ref):
    nb, n, _ = a_ref.shape
    s_ref[...] = a_ref[...]
    x_ref[...] = b_ref[...]
    lane = lax.broadcasted_iota(jnp.int32, (1, n), 1)

    def panel(p, carry):
        j0 = pl.multiple_of(p * PANEL, PANEL)
        rows = [s_ref[b, pl.ds(j0, PANEL), :] for b in range(nb)]
        xts = [x_ref[b] for b in range(nb)]
        factors = [[] for b in range(nb)]
        for t in range(PANEL):
            j = j0 + t
            hit = lane == j
            keep = lane >= j
            after = lane > j
            for b in range(nb):
                d = jnp.sum(jnp.where(hit, rows[b][t:t + 1, :], 0.0), axis=1, keepdims=True)
                inv = 1.0 / jnp.sqrt(d)
                l = jnp.where(keep, rows[b][t:t + 1, :], 0.0) * inv
                col = jnp.sum(jnp.where(hit, rows[b], 0.0), axis=1, keepdims=True) * inv
                rows[b] = rows[b] - col * l
                y = jnp.sum(jnp.where(hit, xts[b], 0.0), axis=1, keepdims=True) * inv
                xts[b] = jnp.where(hit, y, xts[b] - y * jnp.where(after, l, 0.0))
                factors[b].append(l)
        for b in range(nb):
            block = jnp.concatenate(factors[b], axis=0)
            lt_ref[b, pl.ds(j0, PANEL), :] = block
            x_ref[b] = xts[b]
            update = lax.dot_general(
                block, block, (((0,), (0,)), ((), ())),
                precision=PREC, preferred_element_type=jnp.float32)
            s_ref[b] = s_ref[b] - update
        return carry

    lax.fori_loop(0, n // PANEL, panel, 0)
    for b in range(nb):
        l_ref[b] = jnp.transpose(lt_ref[b])

    def backward(t, carry):
        i = n - 1 - t
        for b in range(nb):
            lrow = l_ref[b, pl.ds(i, 1), :]
            lii = jnp.sum(jnp.where(lane == i, lrow, 0.0), axis=1, keepdims=True)
            yt = x_ref[b]
            xi = jnp.sum(jnp.where(lane == i, yt, 0.0), axis=1, keepdims=True) / lii
            x_ref[b] = jnp.where(lane == i, xi, yt - xi * jnp.where(lane < i, lrow, 0.0))
        return carry

    lax.fori_loop(0, n, backward, 0)


def spd_solve_t(matrix, rhs_t):
    nb, n, _ = matrix.shape
    return pl.pallas_call(
        _solve_body,
        out_shape=jax.ShapeDtypeStruct(rhs_t.shape, jnp.float32),
        scratch_shapes=[
            pltpu.VMEM((nb, n, n), jnp.float32),
            pltpu.VMEM((nb, n, n), jnp.float32),
            pltpu.VMEM((nb, n, n), jnp.float32),
        ],
    )(matrix, rhs_t)


def dft_table(length):
    indices = jnp.arange(length, dtype=jnp.int32)
    phase_index = indices[:, None] * indices[None, :] % length
    angles = phase_index.astype(jnp.float32) * (2.0 * math.pi / length)
    cos_part = jnp.cos(angles)
    sin_part = jnp.sin(angles)
    layout = jnp.stack([jnp.stack([cos_part, -sin_part], 1), jnp.stack([sin_part, cos_part], 1)], 0)
    return layout.astype(jnp.bfloat16)


def twiddle_parts():
    inner_idx = jnp.arange(FA, dtype=jnp.int32)
    outer_idx = jnp.arange(FB, dtype=jnp.int32)
    phase_index = inner_idx[:, None] * outer_idx[None, :] % SUBCARRIER_COUNT
    angles = phase_index.astype(jnp.float32) * (2.0 * math.pi / SUBCARRIER_COUNT)
    factor = 1.0 / math.sqrt(SUBCARRIER_COUNT)
    return (jnp.cos(angles) * factor, jnp.sin(angles) * factor)


def spectra(samples):
    antennas_here = samples.shape[0]
    symbol_count = samples.shape[1]
    shaped = samples.reshape(antennas_here, symbol_count, 2, FA, FB)
    section_one = jnp.einsum(
        "ascnm,cndk->sdkma", shaped, dft_table(FA), preferred_element_type=jnp.float32
    )
    cos_part, sin_part = twiddle_parts()
    cos_part = cos_part[:, :, None]
    sin_part = sin_part[:, :, None]
    real_part = section_one[:, 0] * cos_part + section_one[:, 1] * sin_part
    imag_part = section_one[:, 1] * cos_part - section_one[:, 0] * sin_part
    section_one = jnp.stack([real_part, imag_part], 1).astype(jnp.bfloat16)
    section_two = jnp.einsum(
        "sckma,cmdj->sdkja", section_one, dft_table(FB), preferred_element_type=jnp.float32
    )
    return section_two.astype(jnp.bfloat16)


def split_blocks(spectrum):
    width_b = B // FA
    shape_in = spectrum.shape
    return spectrum.reshape(shape_in[0], 2, FA, shape_in[3] // width_b, width_b, shape_in[4])


def code_table(pilots):
    width_b = B // FA
    position = (
        jnp.arange(PSYM, dtype=jnp.int32)[:, None, None] * B
        + jnp.arange(FA, dtype=jnp.int32)[None, :, None]
        + FA * jnp.arange(width_b, dtype=jnp.int32)[None, None, :]
    )
    phase_index = pilots[:, None, None, None] * position[None] % (PSYM * B)
    angles = phase_index.astype(jnp.float32) * (2.0 * math.pi / (PSYM * B))
    factor = 1.0 / math.sqrt(PSYM * B)
    cos_part = jnp.cos(angles) * factor
    sin_part = jnp.sin(angles) * factor
    rows_real = jnp.stack([cos_part, sin_part], 2)
    rows_imag = jnp.stack([-sin_part, cos_part], 2)
    return jnp.stack([rows_real, rows_imag], 0).astype(jnp.bfloat16)


def block_terms(pilot_part, data_part, code_rows):
    channel = jnp.einsum(
        "tcarbm,dktcab->rdkm", pilot_part, code_rows, preferred_element_type=jnp.float32
    ).astype(jnp.bfloat16)
    gram = jnp.einsum("rdkm,relm->rdkel", channel, channel, preferred_element_type=jnp.float32)
    gram_real = gram[:, 0, :, 0] + gram[:, 1, :, 1]
    gram_imag = gram[:, 0, :, 1] - gram[:, 1, :, 0]
    matched = jnp.einsum(
        "rdkm,tcarbm->rdktcab", channel, data_part, preferred_element_type=jnp.float32
    )
    matched_real = matched[:, 0, :, :, 0] + matched[:, 1, :, :, 1]
    matched_imag = matched[:, 0, :, :, 1] - matched[:, 1, :, :, 0]
    blocks = matched_real.shape[0]
    user_count = matched_real.shape[1]
    matched_real = matched_real.reshape(blocks, user_count, -1)
    matched_imag = matched_imag.reshape(blocks, user_count, -1)
    left_half = jnp.stack([gram_real, gram_imag], 1)
    right_half = jnp.stack([matched_real, matched_imag], 1)
    return jnp.concatenate([left_half, right_half], 3)


def mmse_equalizer(packed_layout, served_users, loading, antennas):
    user_count = served_users.shape[1]
    pair_mask = served_users[:, :, None] * served_users[:, None, :]
    diagonal = jnp.eye(user_count, dtype=jnp.float32) * loading[None, :]
    sys_real = pair_mask * packed_layout[:, 0, :, :user_count] / antennas + diagonal[None]
    sys_imag = pair_mask * packed_layout[:, 1, :, :user_count] / antennas
    root_count = math.sqrt(antennas)
    side_real = served_users[:, :, None] * packed_layout[:, 0, :, user_count:] / root_count
    side_imag = served_users[:, :, None] * packed_layout[:, 1, :, user_count:] / root_count
    matrix = jnp.concatenate(
        [jnp.concatenate([sys_real, -sys_imag], 2), jnp.concatenate([sys_imag, sys_real], 2)], 1
    )
    right_side = jnp.concatenate([side_real, side_imag], 1)
    solved = jnp.swapaxes(spd_solve_t(matrix, jnp.swapaxes(right_side, 1, 2)), 1, 2)
    blocks = solved.shape[0]
    solved = solved.reshape(blocks, 2, user_count, -1, FA, B // FA)
    solved = jnp.transpose(solved, (2, 3, 1, 0, 5, 4))
    return solved.reshape(user_count, solved.shape[1], 2, -1)


def packed_terms(pilot_part, data_part, code_rows):
    channel = jnp.einsum(
        "tcarbm,dktcab->rdkm", pilot_part, code_rows, preferred_element_type=jnp.float32
    ).astype(jnp.bfloat16)
    gram = jnp.einsum("rdkm,relm->rdkel", channel, channel, preferred_element_type=jnp.float32)
    gram_real = gram[:, 0, :, 0] + gram[:, 1, :, 1]
    gram_imag = gram[:, 0, :, 1] - gram[:, 1, :, 0]
    user_count = gram_real.shape[1]
    row = lax.broadcasted_iota(jnp.int32, (user_count, user_count), 0)
    col = lax.broadcasted_iota(jnp.int32, (user_count, user_count), 1)
    packed = jnp.where(row <= col, gram_real, gram_imag)
    matched = jnp.einsum(
        "rdkm,tcarbm->rdktcab", channel, data_part, preferred_element_type=jnp.float32
    )
    matched_real = matched[:, 0, :, :, 0] + matched[:, 1, :, :, 1]
    matched_imag = matched[:, 0, :, :, 1] - matched[:, 1, :, :, 0]
    blocks = matched_real.shape[0]
    matched_real = matched_real.reshape(blocks, user_count, -1)
    matched_imag = matched_imag.reshape(blocks, user_count, -1)
    return jnp.concatenate([packed, matched_real, matched_imag], 2)


def unpack_terms(terms, user_count):
    packed = terms[:, :, :user_count]
    mirrored = jnp.swapaxes(packed, 1, 2)
    row = lax.broadcasted_iota(jnp.int32, (user_count, user_count), 0)
    col = lax.broadcasted_iota(jnp.int32, (user_count, user_count), 1)
    gram_real = jnp.where(row <= col, packed, mirrored)
    gram_imag = jnp.where(row > col, packed, jnp.where(row < col, -mirrored, 0.0))
    width = (terms.shape[2] - user_count) // 2
    matched_real = terms[:, :, user_count:user_count + width]
    matched_imag = terms[:, :, user_count + width:]
    left_half = jnp.stack([gram_real, gram_imag], 1)
    right_half = jnp.stack([matched_real, matched_imag], 1)
    return jnp.concatenate([left_half, right_half], 3)


def on_device(received_time_rows, pilots, active_users, allocation, loading, fh_size):
    spectrum = spectra(received_time_rows)
    code_rows = code_table(pilots)
    terms = packed_terms(split_blocks(spectrum[:PSYM]), split_blocks(spectrum[PSYM:]), code_rows)
    terms = lax.psum_scatter(terms, "fh", scatter_dimension=0, tiled=True)
    antenna_total = received_time_rows.shape[0] * fh_size
    packed_layout = unpack_terms(terms, pilots.shape[0])
    served_users = active_users.astype(jnp.float32)[None, :] * allocation.astype(jnp.float32)
    result = mmse_equalizer(packed_layout, served_users, loading, antenna_total)
    return lax.all_to_all(result, "fh", split_axis=0, concat_axis=3, tiled=True)


def solution(mesh):
    return jax.shard_map(
        functools.partial(on_device, fh_size=mesh.shape["fh"]),
        mesh=mesh,
        in_specs=(
            P(("cells", "fh"), None, None, None),
            P("cells"),
            P("cells"),
            P(("cells", "fh"), None),
            P("cells"),
        ),
        out_specs=P(("cells", "fh"), None, None, None),
        check_vma=False,
    )
```

```python
import functools
import math

import jax
import jax.numpy as jnp
from jax import lax
from jax.experimental import pallas as pl
from jax.experimental.pallas import tpu as pltpu
from jax.sharding import PartitionSpec as P

SUBCARRIER_COUNT = 4096
PSYM = 2
B = 32
FA = 16
FB = 256

PANEL = 8
PREC = lax.Precision.HIGHEST


def _solve_body(a_ref, b_ref, x_ref, s_ref, lt_ref, l_ref):
    nb, n, _ = a_ref.shape
    s_ref[...] = a_ref[...]
    x_ref[...] = b_ref[...]
    lane = lax.broadcasted_iota(jnp.int32, (1, n), 1)

    def panel(p, carry):
        j0 = pl.multiple_of(p * PANEL, PANEL)
        rows = [s_ref[b, pl.ds(j0, PANEL), :] for b in range(nb)]
        xts = [x_ref[b] for b in range(nb)]
        factors = [[] for b in range(nb)]
        for t in range(PANEL):
            j = j0 + t
            hit = lane == j
            keep = lane >= j
            after = lane > j
            for b in range(nb):
                d = jnp.sum(jnp.where(hit, rows[b][t:t + 1, :], 0.0), axis=1, keepdims=True)
                inv = 1.0 / jnp.sqrt(d)
                l = jnp.where(keep, rows[b][t:t + 1, :], 0.0) * inv
                col = jnp.sum(jnp.where(hit, rows[b], 0.0), axis=1, keepdims=True) * inv
                rows[b] = rows[b] - col * l
                y = jnp.sum(jnp.where(hit, xts[b], 0.0), axis=1, keepdims=True) * inv
                xts[b] = jnp.where(hit, y, xts[b] - y * jnp.where(after, l, 0.0))
                factors[b].append(l)
        for b in range(nb):
            block = jnp.concatenate(factors[b], axis=0)
            lt_ref[b, pl.ds(j0, PANEL), :] = block
            x_ref[b] = xts[b]
            update = lax.dot_general(
                block, block, (((0,), (0,)), ((), ())),
                precision=PREC, preferred_element_type=jnp.float32)
            s_ref[b] = s_ref[b] - update
        return carry

    lax.fori_loop(0, n // PANEL, panel, 0)
    for b in range(nb):
        l_ref[b] = jnp.transpose(lt_ref[b])

    def backward(t, carry):
        i = n - 1 - t
        for b in range(nb):
            lrow = l_ref[b, pl.ds(i, 1), :]
            lii = jnp.sum(jnp.where(lane == i, lrow, 0.0), axis=1, keepdims=True)
            yt = x_ref[b]
            xi = jnp.sum(jnp.where(lane == i, yt, 0.0), axis=1, keepdims=True) / lii
            x_ref[b] = jnp.where(lane == i, xi, yt - xi * jnp.where(lane < i, lrow, 0.0))
        return carry

    lax.fori_loop(0, n, backward, 0)


def spd_solve_t(matrix, rhs_t):
    nb, n, _ = matrix.shape
    return pl.pallas_call(
        _solve_body,
        out_shape=jax.ShapeDtypeStruct(rhs_t.shape, jnp.float32),
        scratch_shapes=[
            pltpu.VMEM((nb, n, n), jnp.float32),
            pltpu.VMEM((nb, n, n), jnp.float32),
            pltpu.VMEM((nb, n, n), jnp.float32),
        ],
    )(matrix, rhs_t)


def dft_table(length):
    indices = jnp.arange(length, dtype=jnp.int32)
    phase_index = indices[:, None] * indices[None, :] % length
    angles = phase_index.astype(jnp.float32) * (2.0 * math.pi / length)
    cos_part = jnp.cos(angles)
    sin_part = jnp.sin(angles)
    layout = jnp.stack([jnp.stack([cos_part, -sin_part], 1), jnp.stack([sin_part, cos_part], 1)], 0)
    return layout.astype(jnp.bfloat16)


def twiddle_parts():
    inner_idx = jnp.arange(FA, dtype=jnp.int32)
    outer_idx = jnp.arange(FB, dtype=jnp.int32)
    phase_index = inner_idx[:, None] * outer_idx[None, :] % SUBCARRIER_COUNT
    angles = phase_index.astype(jnp.float32) * (2.0 * math.pi / SUBCARRIER_COUNT)
    factor = 1.0 / math.sqrt(SUBCARRIER_COUNT)
    return (jnp.cos(angles) * factor, jnp.sin(angles) * factor)


def spectra(samples):
    antennas_here = samples.shape[0]
    symbol_count = samples.shape[1]
    shaped = samples.reshape(antennas_here, symbol_count, 2, FA, FB)
    section_one = jnp.einsum(
        "ascnm,cndk->sdkma", shaped, dft_table(FA), preferred_element_type=jnp.float32
    )
    cos_part, sin_part = twiddle_parts()
    cos_part = cos_part[:, :, None]
    sin_part = sin_part[:, :, None]
    real_part = section_one[:, 0] * cos_part + section_one[:, 1] * sin_part
    imag_part = section_one[:, 1] * cos_part - section_one[:, 0] * sin_part
    section_one = jnp.stack([real_part, imag_part], 1).astype(jnp.bfloat16)
    section_two = jnp.einsum(
        "sckma,cmdj->sdkja", section_one, dft_table(FB), preferred_element_type=jnp.float32
    )
    return section_two.astype(jnp.bfloat16)


def split_blocks(spectrum):
    width_b = B // FA
    shape_in = spectrum.shape
    return spectrum.reshape(shape_in[0], 2, FA, shape_in[3] // width_b, width_b, shape_in[4])


def code_table(pilots):
    width_b = B // FA
    position = (
        jnp.arange(PSYM, dtype=jnp.int32)[:, None, None] * B
        + jnp.arange(FA, dtype=jnp.int32)[None, :, None]
        + FA * jnp.arange(width_b, dtype=jnp.int32)[None, None, :]
    )
    phase_index = pilots[:, None, None, None] * position[None] % (PSYM * B)
    angles = phase_index.astype(jnp.float32) * (2.0 * math.pi / (PSYM * B))
    factor = 1.0 / math.sqrt(PSYM * B)
    cos_part = jnp.cos(angles) * factor
    sin_part = jnp.sin(angles) * factor
    rows_real = jnp.stack([cos_part, sin_part], 2)
    rows_imag = jnp.stack([-sin_part, cos_part], 2)
    return jnp.stack([rows_real, rows_imag], 0).astype(jnp.bfloat16)


def block_terms(pilot_part, data_part, code_rows):
    channel = jnp.einsum(
        "tcarbm,dktcab->rdkm", pilot_part, code_rows, preferred_element_type=jnp.float32
    ).astype(jnp.bfloat16)
    gram = jnp.einsum("rdkm,relm->rdkel", channel, channel, preferred_element_type=jnp.float32)
    gram_real = gram[:, 0, :, 0] + gram[:, 1, :, 1]
    gram_imag = gram[:, 0, :, 1] - gram[:, 1, :, 0]
    matched = jnp.einsum(
        "rdkm,tcarbm->rdktcab", channel, data_part, preferred_element_type=jnp.float32
    )
    matched_real = matched[:, 0, :, :, 0] + matched[:, 1, :, :, 1]
    matched_imag = matched[:, 0, :, :, 1] - matched[:, 1, :, :, 0]
    blocks = matched_real.shape[0]
    user_count = matched_real.shape[1]
    matched_real = matched_real.reshape(blocks, user_count, -1)
    matched_imag = matched_imag.reshape(blocks, user_count, -1)
    left_half = jnp.stack([gram_real, gram_imag], 1)
    right_half = jnp.stack([matched_real, matched_imag], 1)
    return jnp.concatenate([left_half, right_half], 3)


def mmse_equalizer(packed_layout, served_users, loading, antennas):
    user_count = served_users.shape[1]
    pair_mask = served_users[:, :, None] * served_users[:, None, :]
    diagonal = jnp.eye(user_count, dtype=jnp.float32) * loading[None, :]
    sys_real = pair_mask * packed_layout[:, 0, :, :user_count] / antennas + diagonal[None]
    sys_imag = pair_mask * packed_layout[:, 1, :, :user_count] / antennas
    root_count = math.sqrt(antennas)
    side_real = served_users[:, :, None] * packed_layout[:, 0, :, user_count:] / root_count
    side_imag = served_users[:, :, None] * packed_layout[:, 1, :, user_count:] / root_count
    matrix = jnp.concatenate(
        [jnp.concatenate([sys_real, -sys_imag], 2), jnp.concatenate([sys_imag, sys_real], 2)], 1
    )
    right_side = jnp.concatenate([side_real, side_imag], 1)
    solved = jnp.swapaxes(spd_solve_t(matrix, jnp.swapaxes(right_side, 1, 2)), 1, 2)
    blocks = solved.shape[0]
    solved = solved.reshape(blocks, 2, user_count, -1, FA, B // FA)
    solved = jnp.transpose(solved, (2, 3, 1, 0, 5, 4))
    return solved.reshape(user_count, solved.shape[1], 2, -1)


def packed_terms(pilot_part, data_part, code_rows):
    channel = jnp.einsum(
        "tcarbm,dktcab->rdkm", pilot_part, code_rows, preferred_element_type=jnp.float32
    ).astype(jnp.bfloat16)
    gram = jnp.einsum("rdkm,relm->rdkel", channel, channel, preferred_element_type=jnp.float32)
    gram_real = gram[:, 0, :, 0] + gram[:, 1, :, 1]
    gram_imag = gram[:, 0, :, 1] - gram[:, 1, :, 0]
    user_count = gram_real.shape[1]
    row = lax.broadcasted_iota(jnp.int32, (user_count, user_count), 0)
    col = lax.broadcasted_iota(jnp.int32, (user_count, user_count), 1)
    packed = jnp.where(row <= col, gram_real, gram_imag)
    matched = jnp.einsum(
        "rdkm,tcarbm->rdktcab", channel, data_part, preferred_element_type=jnp.float32
    )
    matched_real = matched[:, 0, :, :, 0] + matched[:, 1, :, :, 1]
    matched_imag = matched[:, 0, :, :, 1] - matched[:, 1, :, :, 0]
    blocks = matched_real.shape[0]
    matched_real = matched_real.reshape(blocks, user_count, -1)
    matched_imag = matched_imag.reshape(blocks, user_count, -1)
    return jnp.concatenate([packed, matched_real, matched_imag], 2)


def unpack_terms(terms, user_count):
    packed = terms[:, :, :user_count]
    mirrored = jnp.swapaxes(packed, 1, 2)
    row = lax.broadcasted_iota(jnp.int32, (user_count, user_count), 0)
    col = lax.broadcasted_iota(jnp.int32, (user_count, user_count), 1)
    gram_real = jnp.where(row <= col, packed, mirrored)
    gram_imag = jnp.where(row > col, packed, jnp.where(row < col, -mirrored, 0.0))
    width = (terms.shape[2] - user_count) // 2
    matched_real = terms[:, :, user_count:user_count + width]
    matched_imag = terms[:, :, user_count + width:]
    left_half = jnp.stack([gram_real, gram_imag], 1)
    right_half = jnp.stack([matched_real, matched_imag], 1)
    return jnp.concatenate([left_half, right_half], 3)


def halving_reduce_scatter(terms, fh_size):
    position = lax.axis_index("fh")
    parts = terms.reshape(fh_size, -1, *terms.shape[1:])
    bit = 0
    while (1 << bit) < fh_size:
        paired = parts.reshape(parts.shape[0] // 2, 2, *parts.shape[1:])
        mine = (position >> bit) & 1
        keep = lax.dynamic_index_in_dim(paired, mine, axis=1, keepdims=False)
        send = lax.dynamic_index_in_dim(paired, 1 - mine, axis=1, keepdims=False)
        pairs = [(i, i ^ (1 << bit)) for i in range(fh_size)]
        parts = keep + lax.ppermute(send, "fh", perm=pairs)
        bit += 1
    return parts.reshape(-1, *terms.shape[1:])


def on_device(received_time_rows, pilots, active_users, allocation, loading, fh_size):
    spectrum = spectra(received_time_rows)
    code_rows = code_table(pilots)
    terms = packed_terms(split_blocks(spectrum[:PSYM]), split_blocks(spectrum[PSYM:]), code_rows)
    terms = halving_reduce_scatter(terms, fh_size)
    antenna_total = received_time_rows.shape[0] * fh_size
    packed_layout = unpack_terms(terms, pilots.shape[0])
    served_users = active_users.astype(jnp.float32)[None, :] * allocation.astype(jnp.float32)
    result = mmse_equalizer(packed_layout, served_users, loading, antenna_total)
    return lax.all_to_all(result, "fh", split_axis=0, concat_axis=3, tiled=True)


def solution(mesh):
    return jax.shard_map(
        functools.partial(on_device, fh_size=mesh.shape["fh"]),
        mesh=mesh,
        in_specs=(
            P(("cells", "fh"), None, None, None),
            P("cells"),
            P("cells"),
            P(("cells", "fh"), None),
            P("cells"),
        ),
        out_specs=P(("cells", "fh"), None, None, None),
        check_vma=False,
    )
```

```python
import functools
import math

import jax
import jax.numpy as jnp
from jax import lax
from jax.experimental import pallas as pl
from jax.experimental.pallas import tpu as pltpu
from jax.sharding import PartitionSpec as P

SUBCARRIER_COUNT = 4096
PSYM = 2
B = 32
FA = 16
FB = 256

PANEL = 8
PREC = lax.Precision.HIGHEST


def _solve_body(a_ref, b_ref, x_ref, s_ref, lt_ref, l_ref):
    nb, n, _ = a_ref.shape
    s_ref[...] = a_ref[...]
    x_ref[...] = b_ref[...]
    lane = lax.broadcasted_iota(jnp.int32, (1, n), 1)

    def panel(p, carry):
        j0 = pl.multiple_of(p * PANEL, PANEL)
        rows = [s_ref[b, pl.ds(j0, PANEL), :] for b in range(nb)]
        xts = [x_ref[b] for b in range(nb)]
        factors = [[] for b in range(nb)]
        for t in range(PANEL):
            j = j0 + t
            hit = lane == j
            keep = lane >= j
            after = lane > j
            for b in range(nb):
                d = jnp.sum(jnp.where(hit, rows[b][t:t + 1, :], 0.0), axis=1, keepdims=True)
                inv = 1.0 / jnp.sqrt(d)
                l = jnp.where(keep, rows[b][t:t + 1, :], 0.0) * inv
                col = jnp.sum(jnp.where(hit, rows[b], 0.0), axis=1, keepdims=True) * inv
                rows[b] = rows[b] - col * l
                y = jnp.sum(jnp.where(hit, xts[b], 0.0), axis=1, keepdims=True) * inv
                xts[b] = jnp.where(hit, y, xts[b] - y * jnp.where(after, l, 0.0))
                factors[b].append(l)
        for b in range(nb):
            block = jnp.concatenate(factors[b], axis=0)
            lt_ref[b, pl.ds(j0, PANEL), :] = block
            x_ref[b] = xts[b]
            update = lax.dot_general(
                block, block, (((0,), (0,)), ((), ())),
                precision=PREC, preferred_element_type=jnp.float32)
            s_ref[b] = s_ref[b] - update
        return carry

    lax.fori_loop(0, n // PANEL, panel, 0)
    for b in range(nb):
        l_ref[b] = jnp.transpose(lt_ref[b])

    def backward(t, carry):
        i = n - 1 - t
        for b in range(nb):
            lrow = l_ref[b, pl.ds(i, 1), :]
            lii = jnp.sum(jnp.where(lane == i, lrow, 0.0), axis=1, keepdims=True)
            yt = x_ref[b]
            xi = jnp.sum(jnp.where(lane == i, yt, 0.0), axis=1, keepdims=True) / lii
            x_ref[b] = jnp.where(lane == i, xi, yt - xi * jnp.where(lane < i, lrow, 0.0))
        return carry

    lax.fori_loop(0, n, backward, 0)


def spd_solve_t(matrix, rhs_t):
    nb, n, _ = matrix.shape
    return pl.pallas_call(
        _solve_body,
        out_shape=jax.ShapeDtypeStruct(rhs_t.shape, jnp.float32),
        scratch_shapes=[
            pltpu.VMEM((nb, n, n), jnp.float32),
            pltpu.VMEM((nb, n, n), jnp.float32),
            pltpu.VMEM((nb, n, n), jnp.float32),
        ],
    )(matrix, rhs_t)


def dft_table(length):
    indices = jnp.arange(length, dtype=jnp.int32)
    phase_index = indices[:, None] * indices[None, :] % length
    angles = phase_index.astype(jnp.float32) * (2.0 * math.pi / length)
    cos_part = jnp.cos(angles)
    sin_part = jnp.sin(angles)
    layout = jnp.stack([jnp.stack([cos_part, -sin_part], 1), jnp.stack([sin_part, cos_part], 1)], 0)
    return layout.astype(jnp.bfloat16)


def twiddle_parts():
    inner_idx = jnp.arange(FA, dtype=jnp.int32)
    outer_idx = jnp.arange(FB, dtype=jnp.int32)
    phase_index = inner_idx[:, None] * outer_idx[None, :] % SUBCARRIER_COUNT
    angles = phase_index.astype(jnp.float32) * (2.0 * math.pi / SUBCARRIER_COUNT)
    factor = 1.0 / math.sqrt(SUBCARRIER_COUNT)
    return (jnp.cos(angles) * factor, jnp.sin(angles) * factor)


def spectra(samples):
    antennas_here = samples.shape[0]
    symbol_count = samples.shape[1]
    shaped = samples.reshape(antennas_here, symbol_count, 2, FA, FB)
    section_one = jnp.einsum(
        "ascnm,cndk->sdkma", shaped, dft_table(FA), preferred_element_type=jnp.float32
    )
    cos_part, sin_part = twiddle_parts()
    cos_part = cos_part[:, :, None]
    sin_part = sin_part[:, :, None]
    real_part = section_one[:, 0] * cos_part + section_one[:, 1] * sin_part
    imag_part = section_one[:, 1] * cos_part - section_one[:, 0] * sin_part
    section_one = jnp.stack([real_part, imag_part], 1).astype(jnp.bfloat16)
    section_two = jnp.einsum(
        "sckma,cmdj->sdkja", section_one, dft_table(FB), preferred_element_type=jnp.float32
    )
    return section_two.astype(jnp.bfloat16)


def split_blocks(spectrum):
    width_b = B // FA
    shape_in = spectrum.shape
    return spectrum.reshape(shape_in[0], 2, FA, shape_in[3] // width_b, width_b, shape_in[4])


def code_table(pilots):
    width_b = B // FA
    position = (
        jnp.arange(PSYM, dtype=jnp.int32)[:, None, None] * B
        + jnp.arange(FA, dtype=jnp.int32)[None, :, None]
        + FA * jnp.arange(width_b, dtype=jnp.int32)[None, None, :]
    )
    phase_index = pilots[:, None, None, None] * position[None] % (PSYM * B)
    angles = phase_index.astype(jnp.float32) * (2.0 * math.pi / (PSYM * B))
    factor = 1.0 / math.sqrt(PSYM * B)
    cos_part = jnp.cos(angles) * factor
    sin_part = jnp.sin(angles) * factor
    rows_real = jnp.stack([cos_part, sin_part], 2)
    rows_imag = jnp.stack([-sin_part, cos_part], 2)
    return jnp.stack([rows_real, rows_imag], 0).astype(jnp.bfloat16)


def block_terms(pilot_part, data_part, code_rows):
    channel = jnp.einsum(
        "tcarbm,dktcab->rdkm", pilot_part, code_rows, preferred_element_type=jnp.float32
    ).astype(jnp.bfloat16)
    gram = jnp.einsum("rdkm,relm->rdkel", channel, channel, preferred_element_type=jnp.float32)
    gram_real = gram[:, 0, :, 0] + gram[:, 1, :, 1]
    gram_imag = gram[:, 0, :, 1] - gram[:, 1, :, 0]
    matched = jnp.einsum(
        "rdkm,tcarbm->rdktcab", channel, data_part, preferred_element_type=jnp.float32
    )
    matched_real = matched[:, 0, :, :, 0] + matched[:, 1, :, :, 1]
    matched_imag = matched[:, 0, :, :, 1] - matched[:, 1, :, :, 0]
    blocks = matched_real.shape[0]
    user_count = matched_real.shape[1]
    matched_real = matched_real.reshape(blocks, user_count, -1)
    matched_imag = matched_imag.reshape(blocks, user_count, -1)
    left_half = jnp.stack([gram_real, gram_imag], 1)
    right_half = jnp.stack([matched_real, matched_imag], 1)
    return jnp.concatenate([left_half, right_half], 3)


def mmse_equalizer(packed_layout, served_users, loading, antennas):
    user_count = served_users.shape[1]
    pair_mask = served_users[:, :, None] * served_users[:, None, :]
    diagonal = jnp.eye(user_count, dtype=jnp.float32) * loading[None, :]
    sys_real = pair_mask * packed_layout[:, 0, :, :user_count] / antennas + diagonal[None]
    sys_imag = pair_mask * packed_layout[:, 1, :, :user_count] / antennas
    root_count = math.sqrt(antennas)
    side_real = served_users[:, :, None] * packed_layout[:, 0, :, user_count:] / root_count
    side_imag = served_users[:, :, None] * packed_layout[:, 1, :, user_count:] / root_count
    matrix = jnp.concatenate(
        [jnp.concatenate([sys_real, -sys_imag], 2), jnp.concatenate([sys_imag, sys_real], 2)], 1
    )
    right_side = jnp.concatenate([side_real, side_imag], 1)
    solved = jnp.swapaxes(spd_solve_t(matrix, jnp.swapaxes(right_side, 1, 2)), 1, 2)
    blocks = solved.shape[0]
    solved = solved.reshape(blocks, 2, user_count, -1, FA, B // FA)
    solved = jnp.transpose(solved, (2, 3, 1, 0, 5, 4))
    return solved.reshape(user_count, solved.shape[1], 2, -1)


def channel_estimate(pilot_part, code_rows):
    return jnp.einsum(
        "tcarbm,dktcab->rdkm", pilot_part, code_rows, preferred_element_type=jnp.float32
    ).astype(jnp.bfloat16)


def gram_terms(channel):
    gram = jnp.einsum("rdkm,relm->rdkel", channel, channel, preferred_element_type=jnp.float32)
    gram_real = gram[:, 0, :, 0] + gram[:, 1, :, 1]
    gram_imag = gram[:, 0, :, 1] - gram[:, 1, :, 0]
    user_count = gram_real.shape[1]
    row = lax.broadcasted_iota(jnp.int32, (user_count, user_count), 0)
    col = lax.broadcasted_iota(jnp.int32, (user_count, user_count), 1)
    return jnp.where(row <= col, gram_real, gram_imag)


def matched_terms(channel, data_part):
    matched = jnp.einsum(
        "rdkm,tcarbm->rdktcab", channel, data_part, preferred_element_type=jnp.float32
    )
    matched_real = matched[:, 0, :, :, 0] + matched[:, 1, :, :, 1]
    matched_imag = matched[:, 0, :, :, 1] - matched[:, 1, :, :, 0]
    blocks = matched_real.shape[0]
    user_count = matched_real.shape[1]
    matched_real = matched_real.reshape(blocks, user_count, -1)
    matched_imag = matched_imag.reshape(blocks, user_count, -1)
    return jnp.concatenate([matched_real, matched_imag], 2)


def unpack_terms(terms, user_count):
    packed = terms[:, :, :user_count]
    mirrored = jnp.swapaxes(packed, 1, 2)
    row = lax.broadcasted_iota(jnp.int32, (user_count, user_count), 0)
    col = lax.broadcasted_iota(jnp.int32, (user_count, user_count), 1)
    gram_real = jnp.where(row <= col, packed, mirrored)
    gram_imag = jnp.where(row > col, packed, jnp.where(row < col, -mirrored, 0.0))
    width = (terms.shape[2] - user_count) // 2
    matched_real = terms[:, :, user_count:user_count + width]
    matched_imag = terms[:, :, user_count + width:]
    left_half = jnp.stack([gram_real, gram_imag], 1)
    right_half = jnp.stack([matched_real, matched_imag], 1)
    return jnp.concatenate([left_half, right_half], 3)


def halving_reduce_scatter(terms, fh_size):
    position = lax.axis_index("fh")
    parts = terms.reshape(fh_size, -1, *terms.shape[1:])
    bit = 0
    while (1 << bit) < fh_size:
        paired = parts.reshape(parts.shape[0] // 2, 2, *parts.shape[1:])
        mine = (position >> bit) & 1
        keep = lax.dynamic_index_in_dim(paired, mine, axis=1, keepdims=False)
        send = lax.dynamic_index_in_dim(paired, 1 - mine, axis=1, keepdims=False)
        pairs = [(i, i ^ (1 << bit)) for i in range(fh_size)]
        parts = keep + lax.ppermute(send, "fh", perm=pairs)
        bit += 1
    return parts.reshape(-1, *terms.shape[1:])


def on_device(received_time_rows, pilots, active_users, allocation, loading, fh_size):
    code_rows = code_table(pilots)
    channel = channel_estimate(split_blocks(spectra(received_time_rows[:, :PSYM])), code_rows)
    gram = halving_reduce_scatter(gram_terms(channel), fh_size)
    matched = matched_terms(channel, split_blocks(spectra(received_time_rows[:, PSYM:])))
    matched = halving_reduce_scatter(matched, fh_size)
    terms = jnp.concatenate([gram, matched], 2)
    antenna_total = received_time_rows.shape[0] * fh_size
    packed_layout = unpack_terms(terms, pilots.shape[0])
    served_users = active_users.astype(jnp.float32)[None, :] * allocation.astype(jnp.float32)
    result = mmse_equalizer(packed_layout, served_users, loading, antenna_total)
    return lax.all_to_all(result, "fh", split_axis=0, concat_axis=3, tiled=True)


def solution(mesh):
    return jax.shard_map(
        functools.partial(on_device, fh_size=mesh.shape["fh"]),
        mesh=mesh,
        in_specs=(
            P(("cells", "fh"), None, None, None),
            P("cells"),
            P("cells"),
            P(("cells", "fh"), None),
            P("cells"),
        ),
        out_specs=P(("cells", "fh"), None, None, None),
        check_vma=False,
    )
```

```python
import functools
import math

import jax
import jax.numpy as jnp
from jax import lax
from jax.experimental import pallas as pl
from jax.experimental.pallas import tpu as pltpu
from jax.sharding import PartitionSpec as P

SUBCARRIER_COUNT = 4096
PSYM = 2
B = 32
FA = 16
FB = 256

PANEL = 8
PREC = lax.Precision.HIGH


def _solve_body(a_ref, b_ref, x_ref, s_ref, r_ref, lt_ref, y_ref):
    nb, n, _ = a_ref.shape
    panels = n // PANEL
    s_ref[...] = a_ref[...]
    r_ref[...] = b_ref[...]
    lane = lax.broadcasted_iota(jnp.int32, (1, n), 1)
    sub = lax.broadcasted_iota(jnp.int32, (PANEL, 1), 0)

    def forward(p, carry):
        j0 = pl.multiple_of(p * PANEL, PANEL)
        rows = [s_ref[b, pl.ds(j0, PANEL), :] for b in range(nb)]
        sides = [r_ref[b, pl.ds(j0, PANEL), :] for b in range(nb)]
        factors = [[] for _ in range(nb)]
        solved = [[] for _ in range(nb)]
        for t in range(PANEL):
            j = j0 + t
            hit = lane == j
            keep = lane >= j
            for b in range(nb):
                pivot_row = rows[b][t:t + 1, :]
                d = jnp.sum(jnp.where(hit, pivot_row, 0.0), axis=1, keepdims=True)
                inv = 1.0 / jnp.sqrt(d)
                l = jnp.where(keep, pivot_row, 0.0) * inv
                col = jnp.sum(jnp.where(hit, rows[b], 0.0), axis=1, keepdims=True) * inv
                rows[b] = rows[b] - col * l
                y = sides[b][t:t + 1, :] * inv
                sides[b] = sides[b] - col * y
                factors[b].append(l)
                solved[b].append(y)
        for b in range(nb):
            block = jnp.concatenate(factors[b], axis=0)
            ys = jnp.concatenate(solved[b], axis=0)
            lt_ref[b, pl.ds(j0, PANEL), :] = block
            y_ref[b, pl.ds(j0, PANEL), :] = ys
            update = lax.dot_general(
                block, jnp.concatenate([block, ys], axis=1), (((0,), (0,)), ((), ())),
                precision=PREC, preferred_element_type=jnp.float32)
            s_ref[b] = s_ref[b] - update[:, :n]
            r_ref[b] = r_ref[b] - update[:, n:]
        return carry

    lax.fori_loop(0, panels, forward, 0)
    x_ref[...] = jnp.zeros(x_ref.shape, jnp.float32)

    def backward(q, carry):
        j0 = pl.multiple_of((panels - 1 - q) * PANEL, PANEL)
        blocks = []
        rests = []
        diags = []
        for b in range(nb):
            block = lt_ref[b, pl.ds(j0, PANEL), :]
            rest = y_ref[b, pl.ds(j0, PANEL), :] - jnp.dot(
                block, x_ref[b], precision=PREC, preferred_element_type=jnp.float32)
            blocks.append(block)
            rests.append(rest)
            diags.append(jnp.sum(jnp.where(lane == j0 + sub, block, 0.0), axis=1, keepdims=True))
        outs = [[None] * PANEL for _ in range(nb)]
        for t in reversed(range(PANEL)):
            hit = lane == j0 + t
            for b in range(nb):
                xt = rests[b][t:t + 1, :] / diags[b][t:t + 1, :]
                col = jnp.sum(jnp.where(hit, blocks[b], 0.0), axis=1, keepdims=True)
                rests[b] = rests[b] - col * xt
                outs[b][t] = xt
        for b in range(nb):
            x_ref[b, pl.ds(j0, PANEL), :] = jnp.concatenate(outs[b], axis=0)
        return carry

    lax.fori_loop(0, panels, backward, 0)


def spd_solve(matrix, rhs):
    nb, n, _ = matrix.shape
    return pl.pallas_call(
        _solve_body,
        out_shape=jax.ShapeDtypeStruct(rhs.shape, jnp.float32),
        scratch_shapes=[
            pltpu.VMEM((nb, n, n), jnp.float32),
            pltpu.VMEM(rhs.shape, jnp.float32),
            pltpu.VMEM((nb, n, n), jnp.float32),
            pltpu.VMEM(rhs.shape, jnp.float32),
        ],
    )(matrix, rhs)


def dft_table(length):
    indices = jnp.arange(length, dtype=jnp.int32)
    phase_index = indices[:, None] * indices[None, :] % length
    angles = phase_index.astype(jnp.float32) * (2.0 * math.pi / length)
    cos_part = jnp.cos(angles)
    sin_part = jnp.sin(angles)
    layout = jnp.stack([jnp.stack([cos_part, -sin_part], 1), jnp.stack([sin_part, cos_part], 1)], 0)
    return layout.astype(jnp.bfloat16)


def twiddle_parts():
    inner_idx = jnp.arange(FA, dtype=jnp.int32)
    outer_idx = jnp.arange(FB, dtype=jnp.int32)
    phase_index = inner_idx[:, None] * outer_idx[None, :] % SUBCARRIER_COUNT
    angles = phase_index.astype(jnp.float32) * (2.0 * math.pi / SUBCARRIER_COUNT)
    factor = 1.0 / math.sqrt(SUBCARRIER_COUNT)
    return (jnp.cos(angles) * factor, jnp.sin(angles) * factor)


def spectra(samples):
    antennas_here = samples.shape[0]
    symbol_count = samples.shape[1]
    shaped = samples.reshape(antennas_here, symbol_count, 2, FA, FB)
    section_one = jnp.einsum(
        "ascnm,cndk->sdkma", shaped, dft_table(FA), preferred_element_type=jnp.float32
    )
    cos_part, sin_part = twiddle_parts()
    cos_part = cos_part[:, :, None]
    sin_part = sin_part[:, :, None]
    real_part = section_one[:, 0] * cos_part + section_one[:, 1] * sin_part
    imag_part = section_one[:, 1] * cos_part - section_one[:, 0] * sin_part
    section_one = jnp.stack([real_part, imag_part], 1).astype(jnp.bfloat16)
    section_two = jnp.einsum(
        "sckma,cmdj->sdkja", section_one, dft_table(FB), preferred_element_type=jnp.float32
    )
    return section_two.astype(jnp.bfloat16)


def split_blocks(spectrum):
    width_b = B // FA
    shape_in = spectrum.shape
    return spectrum.reshape(shape_in[0], 2, FA, shape_in[3] // width_b, width_b, shape_in[4])


def code_table(pilots):
    width_b = B // FA
    position = (
        jnp.arange(PSYM, dtype=jnp.int32)[:, None, None] * B
        + jnp.arange(FA, dtype=jnp.int32)[None, :, None]
        + FA * jnp.arange(width_b, dtype=jnp.int32)[None, None, :]
    )
    phase_index = pilots[:, None, None, None] * position[None] % (PSYM * B)
    angles = phase_index.astype(jnp.float32) * (2.0 * math.pi / (PSYM * B))
    factor = 1.0 / math.sqrt(PSYM * B)
    cos_part = jnp.cos(angles) * factor
    sin_part = jnp.sin(angles) * factor
    rows_real = jnp.stack([cos_part, sin_part], 2)
    rows_imag = jnp.stack([-sin_part, cos_part], 2)
    return jnp.stack([rows_real, rows_imag], 0).astype(jnp.bfloat16)


def block_terms(pilot_part, data_part, code_rows):
    channel = jnp.einsum(
        "tcarbm,dktcab->rdkm", pilot_part, code_rows, preferred_element_type=jnp.float32
    ).astype(jnp.bfloat16)
    gram = jnp.einsum("rdkm,relm->rdkel", channel, channel, preferred_element_type=jnp.float32)
    gram_real = gram[:, 0, :, 0] + gram[:, 1, :, 1]
    gram_imag = gram[:, 0, :, 1] - gram[:, 1, :, 0]
    matched = jnp.einsum(
        "rdkm,tcarbm->rdktcab", channel, data_part, preferred_element_type=jnp.float32
    )
    matched_real = matched[:, 0, :, :, 0] + matched[:, 1, :, :, 1]
    matched_imag = matched[:, 0, :, :, 1] - matched[:, 1, :, :, 0]
    blocks = matched_real.shape[0]
    user_count = matched_real.shape[1]
    matched_real = matched_real.reshape(blocks, user_count, -1)
    matched_imag = matched_imag.reshape(blocks, user_count, -1)
    left_half = jnp.stack([gram_real, gram_imag], 1)
    right_half = jnp.stack([matched_real, matched_imag], 1)
    return jnp.concatenate([left_half, right_half], 3)


def mmse_equalizer(packed_layout, served_users, loading, antennas):
    user_count = served_users.shape[1]
    pair_mask = served_users[:, :, None] * served_users[:, None, :]
    diagonal = jnp.eye(user_count, dtype=jnp.float32) * loading[None, :]
    sys_real = pair_mask * packed_layout[:, 0, :, :user_count] / antennas + diagonal[None]
    sys_imag = pair_mask * packed_layout[:, 1, :, :user_count] / antennas
    root_count = math.sqrt(antennas)
    side_real = served_users[:, :, None] * packed_layout[:, 0, :, user_count:] / root_count
    side_imag = served_users[:, :, None] * packed_layout[:, 1, :, user_count:] / root_count
    matrix = jnp.concatenate(
        [jnp.concatenate([sys_real, -sys_imag], 2), jnp.concatenate([sys_imag, sys_real], 2)], 1
    )
    right_side = jnp.concatenate([side_real, side_imag], 1)
    solved = spd_solve(matrix, right_side)
    blocks = solved.shape[0]
    solved = solved.reshape(blocks, 2, user_count, -1, FA, B // FA)
    solved = jnp.transpose(solved, (2, 3, 1, 0, 5, 4))
    return solved.reshape(user_count, solved.shape[1], 2, -1)


def packed_terms(pilot_part, data_part, code_rows):
    channel = jnp.einsum(
        "tcarbm,dktcab->rdkm", pilot_part, code_rows, preferred_element_type=jnp.float32
    ).astype(jnp.bfloat16)
    gram = jnp.einsum("rdkm,relm->rdkel", channel, channel, preferred_element_type=jnp.float32)
    gram_real = gram[:, 0, :, 0] + gram[:, 1, :, 1]
    gram_imag = gram[:, 0, :, 1] - gram[:, 1, :, 0]
    user_count = gram_real.shape[1]
    row = lax.broadcasted_iota(jnp.int32, (user_count, user_count), 0)
    col = lax.broadcasted_iota(jnp.int32, (user_count, user_count), 1)
    packed = jnp.where(row <= col, gram_real, gram_imag)
    matched = jnp.einsum(
        "rdkm,tcarbm->rdktcab", channel, data_part, preferred_element_type=jnp.float32
    )
    matched_real = matched[:, 0, :, :, 0] + matched[:, 1, :, :, 1]
    matched_imag = matched[:, 0, :, :, 1] - matched[:, 1, :, :, 0]
    blocks = matched_real.shape[0]
    matched_real = matched_real.reshape(blocks, user_count, -1)
    matched_imag = matched_imag.reshape(blocks, user_count, -1)
    return jnp.concatenate([packed, matched_real, matched_imag], 2)


def unpack_terms(terms, user_count):
    packed = terms[:, :, :user_count]
    mirrored = jnp.swapaxes(packed, 1, 2)
    row = lax.broadcasted_iota(jnp.int32, (user_count, user_count), 0)
    col = lax.broadcasted_iota(jnp.int32, (user_count, user_count), 1)
    gram_real = jnp.where(row <= col, packed, mirrored)
    gram_imag = jnp.where(row > col, packed, jnp.where(row < col, -mirrored, 0.0))
    width = (terms.shape[2] - user_count) // 2
    matched_real = terms[:, :, user_count:user_count + width]
    matched_imag = terms[:, :, user_count + width:]
    left_half = jnp.stack([gram_real, gram_imag], 1)
    right_half = jnp.stack([matched_real, matched_imag], 1)
    return jnp.concatenate([left_half, right_half], 3)


def halving_reduce_scatter(terms, fh_size):
    position = lax.axis_index("fh")
    parts = terms.reshape(fh_size, -1, *terms.shape[1:])
    bit = 0
    while (1 << bit) < fh_size:
        paired = parts.reshape(parts.shape[0] // 2, 2, *parts.shape[1:])
        mine = (position >> bit) & 1
        keep = lax.dynamic_index_in_dim(paired, mine, axis=1, keepdims=False)
        send = lax.dynamic_index_in_dim(paired, 1 - mine, axis=1, keepdims=False)
        pairs = [(i, i ^ (1 << bit)) for i in range(fh_size)]
        parts = keep + lax.ppermute(send, "fh", perm=pairs)
        bit += 1
    return parts.reshape(-1, *terms.shape[1:])


def on_device(received_time_rows, pilots, active_users, allocation, loading, fh_size):
    spectrum = spectra(received_time_rows)
    code_rows = code_table(pilots)
    terms = packed_terms(split_blocks(spectrum[:PSYM]), split_blocks(spectrum[PSYM:]), code_rows)
    terms = halving_reduce_scatter(terms, fh_size)
    antenna_total = received_time_rows.shape[0] * fh_size
    packed_layout = unpack_terms(terms, pilots.shape[0])
    served_users = active_users.astype(jnp.float32)[None, :] * allocation.astype(jnp.float32)
    result = mmse_equalizer(packed_layout, served_users, loading, antenna_total)
    return lax.all_to_all(result, "fh", split_axis=0, concat_axis=3, tiled=True)


def solution(mesh):
    return jax.shard_map(
        functools.partial(on_device, fh_size=mesh.shape["fh"]),
        mesh=mesh,
        in_specs=(
            P(("cells", "fh"), None, None, None),
            P("cells"),
            P("cells"),
            P(("cells", "fh"), None),
            P("cells"),
        ),
        out_specs=P(("cells", "fh"), None, None, None),
        check_vma=False,
    )
```

```python
import functools
import math

import jax
import jax.numpy as jnp
from jax import lax
from jax.experimental import pallas as pl
from jax.experimental.pallas import tpu as pltpu
from jax.sharding import PartitionSpec as P

SUBCARRIER_COUNT = 4096
PSYM = 2
B = 32
FA = 16
FB = 256

PANEL = 8
PREC = lax.Precision.HIGH


def _solve_body(a_ref, b_ref, x_ref, s_ref, r_ref, lt_ref, y_ref):
    nb, n, _ = a_ref.shape
    panels = n // PANEL
    s_ref[...] = a_ref[...]
    r_ref[...] = b_ref[...]
    lane = lax.broadcasted_iota(jnp.int32, (1, n), 1)
    sub = lax.broadcasted_iota(jnp.int32, (PANEL, 1), 0)

    def forward(p, carry):
        j0 = pl.multiple_of(p * PANEL, PANEL)
        rows = [s_ref[b, pl.ds(j0, PANEL), :] for b in range(nb)]
        sides = [r_ref[b, pl.ds(j0, PANEL), :] for b in range(nb)]
        factors = [[] for _ in range(nb)]
        solved = [[] for _ in range(nb)]
        for t in range(PANEL):
            j = j0 + t
            hit = lane == j
            keep = lane >= j
            for b in range(nb):
                pivot_row = rows[b][t:t + 1, :]
                d = jnp.sum(jnp.where(hit, pivot_row, 0.0), axis=1, keepdims=True)
                inv = 1.0 / jnp.sqrt(d)
                l = jnp.where(keep, pivot_row, 0.0) * inv
                col = jnp.sum(jnp.where(hit, rows[b], 0.0), axis=1, keepdims=True) * inv
                rows[b] = rows[b] - col * l
                y = sides[b][t:t + 1, :] * inv
                sides[b] = sides[b] - col * y
                factors[b].append(l)
                solved[b].append(y)
        for b in range(nb):
            block = jnp.concatenate(factors[b], axis=0)
            ys = jnp.concatenate(solved[b], axis=0)
            lt_ref[b, pl.ds(j0, PANEL), :] = block
            y_ref[b, pl.ds(j0, PANEL), :] = ys
            update = lax.dot_general(
                block, jnp.concatenate([block, ys], axis=1), (((0,), (0,)), ((), ())),
                precision=PREC, preferred_element_type=jnp.float32)
            s_ref[b] = s_ref[b] - update[:, :n]
            r_ref[b] = r_ref[b] - update[:, n:]
        return carry

    lax.fori_loop(0, panels, forward, 0)
    x_ref[...] = jnp.zeros(x_ref.shape, jnp.float32)

    def backward(q, carry):
        j0 = pl.multiple_of((panels - 1 - q) * PANEL, PANEL)
        blocks = []
        rests = []
        diags = []
        for b in range(nb):
            block = lt_ref[b, pl.ds(j0, PANEL), :]
            rest = y_ref[b, pl.ds(j0, PANEL), :] - jnp.dot(
                block, x_ref[b], precision=PREC, preferred_element_type=jnp.float32)
            blocks.append(block)
            rests.append(rest)
            diags.append(jnp.sum(jnp.where(lane == j0 + sub, block, 0.0), axis=1, keepdims=True))
        outs = [[None] * PANEL for _ in range(nb)]
        for t in reversed(range(PANEL)):
            hit = lane == j0 + t
            for b in range(nb):
                xt = rests[b][t:t + 1, :] / diags[b][t:t + 1, :]
                col = jnp.sum(jnp.where(hit, blocks[b], 0.0), axis=1, keepdims=True)
                rests[b] = rests[b] - col * xt
                outs[b][t] = xt
        for b in range(nb):
            x_ref[b, pl.ds(j0, PANEL), :] = jnp.concatenate(outs[b], axis=0)
        return carry

    lax.fori_loop(0, panels, backward, 0)


def spd_solve(matrix, rhs):
    nb, n, _ = matrix.shape
    return pl.pallas_call(
        _solve_body,
        out_shape=jax.ShapeDtypeStruct(rhs.shape, jnp.float32),
        scratch_shapes=[
            pltpu.VMEM((nb, n, n), jnp.float32),
            pltpu.VMEM(rhs.shape, jnp.float32),
            pltpu.VMEM((nb, n, n), jnp.float32),
            pltpu.VMEM(rhs.shape, jnp.float32),
        ],
    )(matrix, rhs)


def dft_table(length):
    indices = jnp.arange(length, dtype=jnp.int32)
    phase_index = indices[:, None] * indices[None, :] % length
    angles = phase_index.astype(jnp.float32) * (2.0 * math.pi / length)
    cos_part = jnp.cos(angles)
    sin_part = jnp.sin(angles)
    layout = jnp.stack([jnp.stack([cos_part, -sin_part], 1), jnp.stack([sin_part, cos_part], 1)], 0)
    return layout.astype(jnp.bfloat16)


def twiddle_parts():
    inner_idx = jnp.arange(FA, dtype=jnp.int32)
    outer_idx = jnp.arange(FB, dtype=jnp.int32)
    phase_index = inner_idx[:, None] * outer_idx[None, :] % SUBCARRIER_COUNT
    angles = phase_index.astype(jnp.float32) * (2.0 * math.pi / SUBCARRIER_COUNT)
    factor = 1.0 / math.sqrt(SUBCARRIER_COUNT)
    return (jnp.cos(angles) * factor, jnp.sin(angles) * factor)


def spectra(samples):
    antennas_here = samples.shape[0]
    symbol_count = samples.shape[1]
    shaped = samples.reshape(antennas_here, symbol_count, 2, FA, FB)
    section_one = jnp.einsum(
        "ascnm,cndk->sdkma", shaped, dft_table(FA), preferred_element_type=jnp.float32
    )
    cos_part, sin_part = twiddle_parts()
    cos_part = cos_part[:, :, None]
    sin_part = sin_part[:, :, None]
    real_part = section_one[:, 0] * cos_part + section_one[:, 1] * sin_part
    imag_part = section_one[:, 1] * cos_part - section_one[:, 0] * sin_part
    section_one = jnp.stack([real_part, imag_part], 1).astype(jnp.bfloat16)
    section_two = jnp.einsum(
        "sckma,cmdj->sdkja", section_one, dft_table(FB), preferred_element_type=jnp.float32
    )
    return section_two.astype(jnp.bfloat16)


def split_blocks(spectrum):
    width_b = B // FA
    shape_in = spectrum.shape
    return spectrum.reshape(shape_in[0], 2, FA, shape_in[3] // width_b, width_b, shape_in[4])


def code_table(pilots):
    width_b = B // FA
    position = (
        jnp.arange(PSYM, dtype=jnp.int32)[:, None, None] * B
        + jnp.arange(FA, dtype=jnp.int32)[None, :, None]
        + FA * jnp.arange(width_b, dtype=jnp.int32)[None, None, :]
    )
    phase_index = pilots[:, None, None, None] * position[None] % (PSYM * B)
    angles = phase_index.astype(jnp.float32) * (2.0 * math.pi / (PSYM * B))
    factor = 1.0 / math.sqrt(PSYM * B)
    cos_part = jnp.cos(angles) * factor
    sin_part = jnp.sin(angles) * factor
    rows_real = jnp.stack([cos_part, sin_part], 2)
    rows_imag = jnp.stack([-sin_part, cos_part], 2)
    return jnp.stack([rows_real, rows_imag], 0).astype(jnp.bfloat16)


def block_terms(pilot_part, data_part, code_rows):
    channel = jnp.einsum(
        "tcarbm,dktcab->rdkm", pilot_part, code_rows, preferred_element_type=jnp.float32
    ).astype(jnp.bfloat16)
    gram = jnp.einsum("rdkm,relm->rdkel", channel, channel, preferred_element_type=jnp.float32)
    gram_real = gram[:, 0, :, 0] + gram[:, 1, :, 1]
    gram_imag = gram[:, 0, :, 1] - gram[:, 1, :, 0]
    matched = jnp.einsum(
        "rdkm,tcarbm->rdktcab", channel, data_part, preferred_element_type=jnp.float32
    )
    matched_real = matched[:, 0, :, :, 0] + matched[:, 1, :, :, 1]
    matched_imag = matched[:, 0, :, :, 1] - matched[:, 1, :, :, 0]
    blocks = matched_real.shape[0]
    user_count = matched_real.shape[1]
    matched_real = matched_real.reshape(blocks, user_count, -1)
    matched_imag = matched_imag.reshape(blocks, user_count, -1)
    left_half = jnp.stack([gram_real, gram_imag], 1)
    right_half = jnp.stack([matched_real, matched_imag], 1)
    return jnp.concatenate([left_half, right_half], 3)


def mmse_equalizer(packed_layout, served_users, loading, antennas):
    user_count = served_users.shape[1]
    pair_mask = served_users[:, :, None] * served_users[:, None, :]
    diagonal = jnp.eye(user_count, dtype=jnp.float32) * loading[None, :]
    sys_real = pair_mask * packed_layout[:, 0, :, :user_count] / antennas + diagonal[None]
    sys_imag = pair_mask * packed_layout[:, 1, :, :user_count] / antennas
    root_count = math.sqrt(antennas)
    side_real = served_users[:, :, None] * packed_layout[:, 0, :, user_count:] / root_count
    side_imag = served_users[:, :, None] * packed_layout[:, 1, :, user_count:] / root_count
    matrix = jnp.concatenate(
        [jnp.concatenate([sys_real, -sys_imag], 2), jnp.concatenate([sys_imag, sys_real], 2)], 1
    )
    right_side = jnp.concatenate([side_real, side_imag], 1)
    solved = spd_solve(matrix, right_side)
    blocks = solved.shape[0]
    solved = solved.reshape(blocks, 2, user_count, -1, FA, B // FA)
    solved = jnp.transpose(solved, (2, 3, 1, 0, 5, 4))
    return solved.reshape(user_count, solved.shape[1], 2, -1)


def packed_terms(pilot_spectrum, data_spectrum, code_rows):
    channel = jnp.einsum(
        "tcarbm,dktcab->rkdm", split_blocks(pilot_spectrum), code_rows,
        preferred_element_type=jnp.float32,
    ).astype(jnp.bfloat16)
    blocks, user_count, _, antennas = channel.shape
    rows = channel.reshape(blocks, user_count, 2 * antennas)
    turned = jnp.concatenate([channel[:, :, 1], -channel[:, :, 0]], axis=2)
    data = data_spectrum[0].reshape(2, FA, blocks, B // FA, antennas)
    real_side = jnp.stack([data[0], data[1]], axis=3)
    imag_side = jnp.stack([data[1], -data[0]], axis=3)
    sides = jnp.stack([real_side, imag_side], axis=0)
    sides = jnp.transpose(sides, (2, 0, 1, 3, 4, 5)).reshape(blocks, -1, 2 * antennas)
    partners = jnp.concatenate([rows, turned, sides], axis=1)
    products = jnp.einsum("rkx,rlx->rkl", rows, partners, preferred_element_type=jnp.float32)
    row = lax.broadcasted_iota(jnp.int32, (user_count, user_count), 0)
    col = lax.broadcasted_iota(jnp.int32, (user_count, user_count), 1)
    packed = jnp.where(row <= col, products[:, :, :user_count], products[:, :, user_count:2 * user_count])
    return jnp.concatenate([packed, products[:, :, 2 * user_count:]], 2)


def unpack_terms(terms, user_count):
    packed = terms[:, :, :user_count]
    mirrored = jnp.swapaxes(packed, 1, 2)
    row = lax.broadcasted_iota(jnp.int32, (user_count, user_count), 0)
    col = lax.broadcasted_iota(jnp.int32, (user_count, user_count), 1)
    gram_real = jnp.where(row <= col, packed, mirrored)
    gram_imag = jnp.where(row > col, packed, jnp.where(row < col, -mirrored, 0.0))
    width = (terms.shape[2] - user_count) // 2
    matched_real = terms[:, :, user_count:user_count + width]
    matched_imag = terms[:, :, user_count + width:]
    left_half = jnp.stack([gram_real, gram_imag], 1)
    right_half = jnp.stack([matched_real, matched_imag], 1)
    return jnp.concatenate([left_half, right_half], 3)


def halving_reduce_scatter(terms, fh_size):
    position = lax.axis_index("fh")
    parts = terms.reshape(fh_size, -1, *terms.shape[1:])
    bit = 0
    while (1 << bit) < fh_size:
        paired = parts.reshape(parts.shape[0] // 2, 2, *parts.shape[1:])
        mine = (position >> bit) & 1
        keep = lax.dynamic_index_in_dim(paired, mine, axis=1, keepdims=False)
        send = lax.dynamic_index_in_dim(paired, 1 - mine, axis=1, keepdims=False)
        pairs = [(i, i ^ (1 << bit)) for i in range(fh_size)]
        parts = keep + lax.ppermute(send, "fh", perm=pairs)
        bit += 1
    return parts.reshape(-1, *terms.shape[1:])


def on_device(received_time_rows, pilots, active_users, allocation, loading, fh_size):
    spectrum = spectra(received_time_rows)
    code_rows = code_table(pilots)
    terms = packed_terms(spectrum[:PSYM], spectrum[PSYM:], code_rows)
    terms = halving_reduce_scatter(terms, fh_size)
    antenna_total = received_time_rows.shape[0] * fh_size
    packed_layout = unpack_terms(terms, pilots.shape[0])
    served_users = active_users.astype(jnp.float32)[None, :] * allocation.astype(jnp.float32)
    result = mmse_equalizer(packed_layout, served_users, loading, antenna_total)
    return lax.all_to_all(result, "fh", split_axis=0, concat_axis=3, tiled=True)


def solution(mesh):
    return jax.shard_map(
        functools.partial(on_device, fh_size=mesh.shape["fh"]),
        mesh=mesh,
        in_specs=(
            P(("cells", "fh"), None, None, None),
            P("cells"),
            P("cells"),
            P(("cells", "fh"), None),
            P("cells"),
        ),
        out_specs=P(("cells", "fh"), None, None, None),
        check_vma=False,
    )
```

```python
import functools
import math

import jax
import jax.numpy as jnp
from jax import lax
from jax.experimental import pallas as pl
from jax.experimental.pallas import tpu as pltpu
from jax.sharding import PartitionSpec as P

SUBCARRIER_COUNT = 4096
PSYM = 2
B = 32
FA = 16
FB = 256

PANEL = 8
PREC = lax.Precision.HIGH


def _solve_body(a_ref, b_ref, x_ref, s_ref, r_ref, lt_ref, y_ref):
    nb, n, _ = a_ref.shape
    panels = n // PANEL
    s_ref[...] = a_ref[...]
    r_ref[...] = b_ref[...]
    lane = lax.broadcasted_iota(jnp.int32, (1, n), 1)
    sub = lax.broadcasted_iota(jnp.int32, (PANEL, 1), 0)

    def forward(p, carry):
        j0 = pl.multiple_of(p * PANEL, PANEL)
        rows = [s_ref[b, pl.ds(j0, PANEL), :] for b in range(nb)]
        sides = [r_ref[b, pl.ds(j0, PANEL), :] for b in range(nb)]
        factors = [[] for _ in range(nb)]
        solved = [[] for _ in range(nb)]
        for t in range(PANEL):
            j = j0 + t
            hit = lane == j
            keep = lane >= j
            for b in range(nb):
                pivot_row = rows[b][t:t + 1, :]
                column = jnp.sum(jnp.where(hit, rows[b], 0.0), axis=1, keepdims=True)
                inv = 1.0 / jnp.sqrt(column[t:t + 1, :])
                l = jnp.where(keep, pivot_row, 0.0) * inv
                col = column * inv
                rows[b] = rows[b] - col * l
                y = sides[b][t:t + 1, :] * inv
                sides[b] = sides[b] - col * y
                factors[b].append(l)
                solved[b].append(y)
        for b in range(nb):
            block = jnp.concatenate(factors[b], axis=0)
            ys = jnp.concatenate(solved[b], axis=0)
            lt_ref[b, pl.ds(j0, PANEL), :] = block
            y_ref[b, pl.ds(j0, PANEL), :] = ys
            update = lax.dot_general(
                block, jnp.concatenate([block, ys], axis=1), (((0,), (0,)), ((), ())),
                precision=PREC, preferred_element_type=jnp.float32)
            s_ref[b] = s_ref[b] - update[:, :n]
            r_ref[b] = r_ref[b] - update[:, n:]
        return carry

    lax.fori_loop(0, panels, forward, 0)
    x_ref[...] = jnp.zeros(x_ref.shape, jnp.float32)

    def backward(q, carry):
        j0 = pl.multiple_of((panels - 1 - q) * PANEL, PANEL)
        blocks = []
        rests = []
        diags = []
        for b in range(nb):
            block = lt_ref[b, pl.ds(j0, PANEL), :]
            rest = y_ref[b, pl.ds(j0, PANEL), :] - jnp.dot(
                block, x_ref[b], precision=PREC, preferred_element_type=jnp.float32)
            blocks.append(block)
            rests.append(rest)
            diags.append(1.0 / jnp.sum(jnp.where(lane == j0 + sub, block, 0.0), axis=1, keepdims=True))
        outs = [[None] * PANEL for _ in range(nb)]
        for t in reversed(range(PANEL)):
            hit = lane == j0 + t
            for b in range(nb):
                xt = rests[b][t:t + 1, :] * diags[b][t:t + 1, :]
                col = jnp.sum(jnp.where(hit, blocks[b], 0.0), axis=1, keepdims=True)
                rests[b] = rests[b] - col * xt
                outs[b][t] = xt
        for b in range(nb):
            x_ref[b, pl.ds(j0, PANEL), :] = jnp.concatenate(outs[b], axis=0)
        return carry

    lax.fori_loop(0, panels, backward, 0)


def spd_solve(matrix, rhs):
    nb, n, _ = matrix.shape
    return pl.pallas_call(
        _solve_body,
        out_shape=jax.ShapeDtypeStruct(rhs.shape, jnp.float32),
        scratch_shapes=[
            pltpu.VMEM((nb, n, n), jnp.float32),
            pltpu.VMEM(rhs.shape, jnp.float32),
            pltpu.VMEM((nb, n, n), jnp.float32),
            pltpu.VMEM(rhs.shape, jnp.float32),
        ],
    )(matrix, rhs)


def dft_table(length):
    indices = jnp.arange(length, dtype=jnp.int32)
    phase_index = indices[:, None] * indices[None, :] % length
    angles = phase_index.astype(jnp.float32) * (2.0 * math.pi / length)
    cos_part = jnp.cos(angles)
    sin_part = jnp.sin(angles)
    layout = jnp.stack([jnp.stack([cos_part, -sin_part], 1), jnp.stack([sin_part, cos_part], 1)], 0)
    return layout.astype(jnp.bfloat16)


def twiddle_parts():
    inner_idx = jnp.arange(FA, dtype=jnp.int32)
    outer_idx = jnp.arange(FB, dtype=jnp.int32)
    phase_index = inner_idx[:, None] * outer_idx[None, :] % SUBCARRIER_COUNT
    angles = phase_index.astype(jnp.float32) * (2.0 * math.pi / SUBCARRIER_COUNT)
    factor = 1.0 / math.sqrt(SUBCARRIER_COUNT)
    return (jnp.cos(angles) * factor, jnp.sin(angles) * factor)


def spectra(samples):
    antennas_here = samples.shape[0]
    symbol_count = samples.shape[1]
    shaped = samples.reshape(antennas_here, symbol_count, 2, FA, FB)
    section_one = jnp.einsum(
        "ascnm,cndk->sdkma", shaped, dft_table(FA), preferred_element_type=jnp.float32
    )
    cos_part, sin_part = twiddle_parts()
    cos_part = cos_part[:, :, None]
    sin_part = sin_part[:, :, None]
    real_part = section_one[:, 0] * cos_part + section_one[:, 1] * sin_part
    imag_part = section_one[:, 1] * cos_part - section_one[:, 0] * sin_part
    section_one = jnp.stack([real_part, imag_part], 1).astype(jnp.bfloat16)
    section_two = jnp.einsum(
        "sckma,cmdj->sdkja", section_one, dft_table(FB), preferred_element_type=jnp.float32
    )
    return section_two.astype(jnp.bfloat16)


def split_blocks(spectrum):
    width_b = B // FA
    shape_in = spectrum.shape
    return spectrum.reshape(shape_in[0], 2, FA, shape_in[3] // width_b, width_b, shape_in[4])


def code_table(pilots):
    width_b = B // FA
    position = (
        jnp.arange(PSYM, dtype=jnp.int32)[:, None, None] * B
        + jnp.arange(FA, dtype=jnp.int32)[None, :, None]
        + FA * jnp.arange(width_b, dtype=jnp.int32)[None, None, :]
    )
    phase_index = pilots[:, None, None, None] * position[None] % (PSYM * B)
    angles = phase_index.astype(jnp.float32) * (2.0 * math.pi / (PSYM * B))
    factor = 1.0 / math.sqrt(PSYM * B)
    cos_part = jnp.cos(angles) * factor
    sin_part = jnp.sin(angles) * factor
    rows_real = jnp.stack([cos_part, sin_part], 2)
    rows_imag = jnp.stack([-sin_part, cos_part], 2)
    return jnp.stack([rows_real, rows_imag], 0).astype(jnp.bfloat16)


def block_terms(pilot_part, data_part, code_rows):
    channel = jnp.einsum(
        "tcarbm,dktcab->rdkm", pilot_part, code_rows, preferred_element_type=jnp.float32
    ).astype(jnp.bfloat16)
    gram = jnp.einsum("rdkm,relm->rdkel", channel, channel, preferred_element_type=jnp.float32)
    gram_real = gram[:, 0, :, 0] + gram[:, 1, :, 1]
    gram_imag = gram[:, 0, :, 1] - gram[:, 1, :, 0]
    matched = jnp.einsum(
        "rdkm,tcarbm->rdktcab", channel, data_part, preferred_element_type=jnp.float32
    )
    matched_real = matched[:, 0, :, :, 0] + matched[:, 1, :, :, 1]
    matched_imag = matched[:, 0, :, :, 1] - matched[:, 1, :, :, 0]
    blocks = matched_real.shape[0]
    user_count = matched_real.shape[1]
    matched_real = matched_real.reshape(blocks, user_count, -1)
    matched_imag = matched_imag.reshape(blocks, user_count, -1)
    left_half = jnp.stack([gram_real, gram_imag], 1)
    right_half = jnp.stack([matched_real, matched_imag], 1)
    return jnp.concatenate([left_half, right_half], 3)


def mmse_equalizer(packed_layout, served_users, loading, antennas):
    user_count = served_users.shape[1]
    pair_mask = served_users[:, :, None] * served_users[:, None, :]
    diagonal = jnp.eye(user_count, dtype=jnp.float32) * loading[None, :]
    sys_real = pair_mask * packed_layout[:, 0, :, :user_count] / antennas + diagonal[None]
    sys_imag = pair_mask * packed_layout[:, 1, :, :user_count] / antennas
    root_count = math.sqrt(antennas)
    side_real = served_users[:, :, None] * packed_layout[:, 0, :, user_count:] / root_count
    side_imag = served_users[:, :, None] * packed_layout[:, 1, :, user_count:] / root_count
    matrix = jnp.concatenate(
        [jnp.concatenate([sys_real, -sys_imag], 2), jnp.concatenate([sys_imag, sys_real], 2)], 1
    )
    right_side = jnp.concatenate([side_real, side_imag], 1)
    solved = spd_solve(matrix, right_side)
    blocks = solved.shape[0]
    solved = solved.reshape(blocks, 2, user_count, -1, FA, B // FA)
    solved = jnp.transpose(solved, (2, 3, 1, 0, 5, 4))
    return solved.reshape(user_count, solved.shape[1], 2, -1)


def packed_terms(pilot_part, data_part, code_rows):
    channel = jnp.einsum(
        "tcarbm,dktcab->rdkm", pilot_part, code_rows, preferred_element_type=jnp.float32
    ).astype(jnp.bfloat16)
    gram = jnp.einsum("rdkm,relm->rdkel", channel, channel, preferred_element_type=jnp.float32)
    gram_real = gram[:, 0, :, 0] + gram[:, 1, :, 1]
    gram_imag = gram[:, 0, :, 1] - gram[:, 1, :, 0]
    user_count = gram_real.shape[1]
    row = lax.broadcasted_iota(jnp.int32, (user_count, user_count), 0)
    col = lax.broadcasted_iota(jnp.int32, (user_count, user_count), 1)
    packed = jnp.where(row <= col, gram_real, gram_imag)
    matched = jnp.einsum(
        "rdkm,tcarbm->rdktcab", channel, data_part, preferred_element_type=jnp.float32
    )
    matched_real = matched[:, 0, :, :, 0] + matched[:, 1, :, :, 1]
    matched_imag = matched[:, 0, :, :, 1] - matched[:, 1, :, :, 0]
    blocks = matched_real.shape[0]
    matched_real = matched_real.reshape(blocks, user_count, -1)
    matched_imag = matched_imag.reshape(blocks, user_count, -1)
    return jnp.concatenate([packed, matched_real, matched_imag], 2)


def unpack_terms(terms, user_count):
    packed = terms[:, :, :user_count]
    mirrored = jnp.swapaxes(packed, 1, 2)
    row = lax.broadcasted_iota(jnp.int32, (user_count, user_count), 0)
    col = lax.broadcasted_iota(jnp.int32, (user_count, user_count), 1)
    gram_real = jnp.where(row <= col, packed, mirrored)
    gram_imag = jnp.where(row > col, packed, jnp.where(row < col, -mirrored, 0.0))
    width = (terms.shape[2] - user_count) // 2
    matched_real = terms[:, :, user_count:user_count + width]
    matched_imag = terms[:, :, user_count + width:]
    left_half = jnp.stack([gram_real, gram_imag], 1)
    right_half = jnp.stack([matched_real, matched_imag], 1)
    return jnp.concatenate([left_half, right_half], 3)


def halving_reduce_scatter(terms, fh_size):
    position = lax.axis_index("fh")
    parts = terms.reshape(fh_size, -1, *terms.shape[1:])
    bit = 0
    while (1 << bit) < fh_size:
        paired = parts.reshape(parts.shape[0] // 2, 2, *parts.shape[1:])
        mine = (position >> bit) & 1
        keep = lax.dynamic_index_in_dim(paired, mine, axis=1, keepdims=False)
        send = lax.dynamic_index_in_dim(paired, 1 - mine, axis=1, keepdims=False)
        pairs = [(i, i ^ (1 << bit)) for i in range(fh_size)]
        parts = keep + lax.ppermute(send, "fh", perm=pairs)
        bit += 1
    return parts.reshape(-1, *terms.shape[1:])


def on_device(received_time_rows, pilots, active_users, allocation, loading, fh_size):
    spectrum = spectra(received_time_rows)
    code_rows = code_table(pilots)
    terms = packed_terms(split_blocks(spectrum[:PSYM]), split_blocks(spectrum[PSYM:]), code_rows)
    terms = halving_reduce_scatter(terms, fh_size)
    antenna_total = received_time_rows.shape[0] * fh_size
    packed_layout = unpack_terms(terms, pilots.shape[0])
    served_users = active_users.astype(jnp.float32)[None, :] * allocation.astype(jnp.float32)
    result = mmse_equalizer(packed_layout, served_users, loading, antenna_total)
    return lax.all_to_all(result, "fh", split_axis=0, concat_axis=3, tiled=True)


def solution(mesh):
    return jax.shard_map(
        functools.partial(on_device, fh_size=mesh.shape["fh"]),
        mesh=mesh,
        in_specs=(
            P(("cells", "fh"), None, None, None),
            P("cells"),
            P("cells"),
            P(("cells", "fh"), None),
            P("cells"),
        ),
        out_specs=P(("cells", "fh"), None, None, None),
        check_vma=False,
    )
```

```python
import functools
import math

import jax
import jax.numpy as jnp
from jax import lax
from jax.experimental import pallas as pl
from jax.experimental.pallas import tpu as pltpu
from jax.sharding import PartitionSpec as P

SUBCARRIER_COUNT = 4096
PSYM = 2
B = 32
FA = 16
FB = 256

PANEL = 8
PREC = lax.Precision.HIGH


def _solve_body(a_ref, b_ref, x_ref, s_ref, r_ref, lt_ref, y_ref):
    nb, n, _ = a_ref.shape
    panels = n // PANEL
    s_ref[...] = a_ref[...]
    r_ref[...] = b_ref[...]
    lane = lax.broadcasted_iota(jnp.int32, (1, n), 1)
    sub = lax.broadcasted_iota(jnp.int32, (PANEL, 1), 0)

    def forward(p, carry):
        j0 = pl.multiple_of(p * PANEL, PANEL)
        rows = [s_ref[b, pl.ds(j0, PANEL), :] for b in range(nb)]
        sides = [r_ref[b, pl.ds(j0, PANEL), :] for b in range(nb)]
        factors = [[] for _ in range(nb)]
        solved = [[] for _ in range(nb)]
        for t in range(PANEL):
            j = j0 + t
            hit = lane == j
            keep = lane >= j
            for b in range(nb):
                pivot_row = rows[b][t:t + 1, :]
                column = jnp.sum(jnp.where(hit, rows[b], 0.0), axis=1, keepdims=True)
                inv = 1.0 / jnp.sqrt(column[t:t + 1, :])
                l = jnp.where(keep, pivot_row, 0.0) * inv
                col = column * inv
                rows[b] = rows[b] - col * l
                y = sides[b][t:t + 1, :] * inv
                sides[b] = sides[b] - col * y
                factors[b].append(l)
                solved[b].append(y)
        for b in range(nb):
            block = jnp.concatenate(factors[b], axis=0)
            ys = jnp.concatenate(solved[b], axis=0)
            lt_ref[b, pl.ds(j0, PANEL), :] = block
            y_ref[b, pl.ds(j0, PANEL), :] = ys
            update = lax.dot_general(
                block, jnp.concatenate([block, ys], axis=1), (((0,), (0,)), ((), ())),
                precision=PREC, preferred_element_type=jnp.float32)
            s_ref[b] = s_ref[b] - update[:, :n]
            r_ref[b] = r_ref[b] - update[:, n:]
        return carry

    lax.fori_loop(0, panels, forward, 0)
    x_ref[...] = jnp.zeros(x_ref.shape, jnp.float32)

    def backward(q, carry):
        j0 = pl.multiple_of((panels - 1 - q) * PANEL, PANEL)
        blocks = []
        rests = []
        diags = []
        for b in range(nb):
            block = lt_ref[b, pl.ds(j0, PANEL), :]
            rest = y_ref[b, pl.ds(j0, PANEL), :] - jnp.dot(
                block, x_ref[b], precision=PREC, preferred_element_type=jnp.float32)
            blocks.append(block)
            rests.append(rest)
            diags.append(1.0 / jnp.sum(jnp.where(lane == j0 + sub, block, 0.0), axis=1, keepdims=True))
        outs = [[None] * PANEL for _ in range(nb)]
        for t in reversed(range(PANEL)):
            hit = lane == j0 + t
            for b in range(nb):
                xt = rests[b][t:t + 1, :] * diags[b][t:t + 1, :]
                col = jnp.sum(jnp.where(hit, blocks[b], 0.0), axis=1, keepdims=True)
                rests[b] = rests[b] - col * xt
                outs[b][t] = xt
        for b in range(nb):
            x_ref[b, pl.ds(j0, PANEL), :] = jnp.concatenate(outs[b], axis=0)
        return carry

    lax.fori_loop(0, panels, backward, 0)


def spd_solve(matrix, rhs):
    nb, n, _ = matrix.shape
    return pl.pallas_call(
        _solve_body,
        out_shape=jax.ShapeDtypeStruct(rhs.shape, jnp.float32),
        scratch_shapes=[
            pltpu.VMEM((nb, n, n), jnp.float32),
            pltpu.VMEM(rhs.shape, jnp.float32),
            pltpu.VMEM((nb, n, n), jnp.float32),
            pltpu.VMEM(rhs.shape, jnp.float32),
        ],
    )(matrix, rhs)


def dft_table(length):
    indices = jnp.arange(length, dtype=jnp.int32)
    phase_index = indices[:, None] * indices[None, :] % length
    angles = phase_index.astype(jnp.float32) * (2.0 * math.pi / length)
    cos_part = jnp.cos(angles)
    sin_part = jnp.sin(angles)
    layout = jnp.stack([jnp.stack([cos_part, -sin_part], 1), jnp.stack([sin_part, cos_part], 1)], 0)
    return layout.astype(jnp.bfloat16)


def twiddle_parts():
    inner_idx = jnp.arange(FA, dtype=jnp.int32)
    outer_idx = jnp.arange(FB, dtype=jnp.int32)
    phase_index = inner_idx[:, None] * outer_idx[None, :] % SUBCARRIER_COUNT
    angles = phase_index.astype(jnp.float32) * (2.0 * math.pi / SUBCARRIER_COUNT)
    factor = 1.0 / math.sqrt(SUBCARRIER_COUNT)
    return (jnp.cos(angles) * factor, jnp.sin(angles) * factor)


def spectra(samples):
    antennas_here = samples.shape[0]
    symbol_count = samples.shape[1]
    shaped = samples.reshape(antennas_here, symbol_count, 2, FA, FB)
    section_one = jnp.einsum(
        "ascnm,cndk->sdkma", shaped, dft_table(FA), preferred_element_type=jnp.float32
    )
    cos_part, sin_part = twiddle_parts()
    cos_part = cos_part[:, :, None]
    sin_part = sin_part[:, :, None]
    real_part = section_one[:, 0] * cos_part + section_one[:, 1] * sin_part
    imag_part = section_one[:, 1] * cos_part - section_one[:, 0] * sin_part
    section_one = jnp.stack([real_part, imag_part], 1).astype(jnp.bfloat16)
    section_two = jnp.einsum(
        "sckma,cmdj->sdkja", section_one, dft_table(FB), preferred_element_type=jnp.float32
    )
    return section_two.astype(jnp.bfloat16)


def split_blocks(spectrum):
    width_b = B // FA
    shape_in = spectrum.shape
    return spectrum.reshape(shape_in[0], 2, FA, shape_in[3] // width_b, width_b, shape_in[4])


def code_table(pilots):
    width_b = B // FA
    position = (
        jnp.arange(PSYM, dtype=jnp.int32)[:, None, None] * B
        + jnp.arange(FA, dtype=jnp.int32)[None, :, None]
        + FA * jnp.arange(width_b, dtype=jnp.int32)[None, None, :]
    )
    phase_index = pilots[:, None, None, None] * position[None] % (PSYM * B)
    angles = phase_index.astype(jnp.float32) * (2.0 * math.pi / (PSYM * B))
    factor = 1.0 / math.sqrt(PSYM * B)
    cos_part = jnp.cos(angles) * factor
    sin_part = jnp.sin(angles) * factor
    rows_real = jnp.stack([cos_part, sin_part], 2)
    rows_imag = jnp.stack([-sin_part, cos_part], 2)
    return jnp.stack([rows_real, rows_imag], 0).astype(jnp.bfloat16)


def block_terms(pilot_part, data_part, code_rows):
    channel = jnp.einsum(
        "tcarbm,dktcab->rdkm", pilot_part, code_rows, preferred_element_type=jnp.float32
    ).astype(jnp.bfloat16)
    gram = jnp.einsum("rdkm,relm->rdkel", channel, channel, preferred_element_type=jnp.float32)
    gram_real = gram[:, 0, :, 0] + gram[:, 1, :, 1]
    gram_imag = gram[:, 0, :, 1] - gram[:, 1, :, 0]
    matched = jnp.einsum(
        "rdkm,tcarbm->rdktcab", channel, data_part, preferred_element_type=jnp.float32
    )
    matched_real = matched[:, 0, :, :, 0] + matched[:, 1, :, :, 1]
    matched_imag = matched[:, 0, :, :, 1] - matched[:, 1, :, :, 0]
    blocks = matched_real.shape[0]
    user_count = matched_real.shape[1]
    matched_real = matched_real.reshape(blocks, user_count, -1)
    matched_imag = matched_imag.reshape(blocks, user_count, -1)
    left_half = jnp.stack([gram_real, gram_imag], 1)
    right_half = jnp.stack([matched_real, matched_imag], 1)
    return jnp.concatenate([left_half, right_half], 3)


def mmse_equalizer(packed_layout, served_users, loading, antennas):
    user_count = served_users.shape[1]
    pair_mask = served_users[:, :, None] * served_users[:, None, :]
    diagonal = jnp.eye(user_count, dtype=jnp.float32) * loading[None, :]
    sys_real = pair_mask * packed_layout[:, 0, :, :user_count] / antennas + diagonal[None]
    sys_imag = pair_mask * packed_layout[:, 1, :, :user_count] / antennas
    root_count = math.sqrt(antennas)
    side_real = served_users[:, :, None] * packed_layout[:, 0, :, user_count:] / root_count
    side_imag = served_users[:, :, None] * packed_layout[:, 1, :, user_count:] / root_count
    matrix = jnp.concatenate(
        [jnp.concatenate([sys_real, -sys_imag], 2), jnp.concatenate([sys_imag, sys_real], 2)], 1
    )
    right_side = jnp.concatenate([side_real, side_imag], 1)
    solved = spd_solve(matrix, right_side)
    blocks = solved.shape[0]
    solved = solved.reshape(blocks, 2, user_count, -1, FA, B // FA)
    solved = jnp.transpose(solved, (2, 3, 1, 0, 5, 4))
    return solved.reshape(user_count, solved.shape[1], 2, -1)


def packed_terms(pilot_part, data_part, code_rows):
    channel = jnp.einsum(
        "tcarbm,dktcab->rdkm", pilot_part, code_rows, preferred_element_type=jnp.float32
    ).astype(jnp.bfloat16)
    gram = jnp.einsum("rdkm,relm->rdkel", channel, channel, preferred_element_type=jnp.float32)
    gram_real = gram[:, 0, :, 0] + gram[:, 1, :, 1]
    gram_imag = gram[:, 0, :, 1] - gram[:, 1, :, 0]
    user_count = gram_real.shape[1]
    row = lax.broadcasted_iota(jnp.int32, (user_count, user_count), 0)
    col = lax.broadcasted_iota(jnp.int32, (user_count, user_count), 1)
    packed = jnp.where(row <= col, gram_real, gram_imag)
    matched = jnp.einsum(
        "rdkm,tcarbm->rdktcab", channel, data_part, preferred_element_type=jnp.float32
    )
    matched_real = matched[:, 0, :, :, 0] + matched[:, 1, :, :, 1]
    matched_imag = matched[:, 0, :, :, 1] - matched[:, 1, :, :, 0]
    blocks = matched_real.shape[0]
    matched_real = matched_real.reshape(blocks, user_count, -1)
    matched_imag = matched_imag.reshape(blocks, user_count, -1)
    return jnp.concatenate([packed, matched_real, matched_imag], 2)


def unpack_terms(terms, user_count):
    packed = terms[:, :, :user_count]
    mirrored = jnp.swapaxes(packed, 1, 2)
    row = lax.broadcasted_iota(jnp.int32, (user_count, user_count), 0)
    col = lax.broadcasted_iota(jnp.int32, (user_count, user_count), 1)
    gram_real = jnp.where(row <= col, packed, mirrored)
    gram_imag = jnp.where(row > col, packed, jnp.where(row < col, -mirrored, 0.0))
    width = (terms.shape[2] - user_count) // 2
    matched_real = terms[:, :, user_count:user_count + width]
    matched_imag = terms[:, :, user_count + width:]
    left_half = jnp.stack([gram_real, gram_imag], 1)
    right_half = jnp.stack([matched_real, matched_imag], 1)
    return jnp.concatenate([left_half, right_half], 3)


def halve(parts, bits, bit, position, fh_size):
    axis = bits.index(bit)
    mine = (position >> bit) & 1
    keep = lax.dynamic_index_in_dim(parts, mine, axis=axis, keepdims=False)
    send = lax.dynamic_index_in_dim(parts, 1 - mine, axis=axis, keepdims=False)
    pairs = [(i, i ^ (1 << bit)) for i in range(fh_size)]
    return keep + lax.ppermute(send, "fh", perm=pairs), bits[:axis] + bits[axis + 1:]


def halving_reduce_scatter(terms, fh_size):
    position = lax.axis_index("fh")
    count = fh_size.bit_length() - 1
    bits = list(reversed(range(count)))
    parts = terms.reshape(*([2] * count), -1, *terms.shape[1:])
    share = parts.shape[count]
    if count < 3 or share % 2:
        for bit in range(count):
            parts, bits = halve(parts, bits, bit, position, fh_size)
        return parts.reshape(-1, *terms.shape[1:])
    parts, bits = halve(parts, bits, 0, position, fh_size)
    first = lax.slice_in_dim(parts, 0, share // 2, axis=count - 1)
    second = lax.slice_in_dim(parts, share // 2, share, axis=count - 1)
    bits_first = bits_second = bits
    order_first = list(range(1, count))
    order_second = [2, 1] + list(range(3, count))
    for bit_first, bit_second in zip(order_first, order_second):
        first, bits_first = halve(first, bits_first, bit_first, position, fh_size)
        second, bits_second = halve(second, bits_second, bit_second, position, fh_size)
    return jnp.concatenate([first, second], axis=0).reshape(-1, *terms.shape[1:])


def on_device(received_time_rows, pilots, active_users, allocation, loading, fh_size):
    spectrum = spectra(received_time_rows)
    code_rows = code_table(pilots)
    terms = packed_terms(split_blocks(spectrum[:PSYM]), split_blocks(spectrum[PSYM:]), code_rows)
    terms = halving_reduce_scatter(terms, fh_size)
    antenna_total = received_time_rows.shape[0] * fh_size
    packed_layout = unpack_terms(terms, pilots.shape[0])
    served_users = active_users.astype(jnp.float32)[None, :] * allocation.astype(jnp.float32)
    result = mmse_equalizer(packed_layout, served_users, loading, antenna_total)
    return lax.all_to_all(result, "fh", split_axis=0, concat_axis=3, tiled=True)


def solution(mesh):
    return jax.shard_map(
        functools.partial(on_device, fh_size=mesh.shape["fh"]),
        mesh=mesh,
        in_specs=(
            P(("cells", "fh"), None, None, None),
            P("cells"),
            P("cells"),
            P(("cells", "fh"), None),
            P("cells"),
        ),
        out_specs=P(("cells", "fh"), None, None, None),
        check_vma=False,
    )
```

```python
import functools
import math

import jax
import jax.numpy as jnp
from jax import lax
from jax.experimental import pallas as pl
from jax.experimental.pallas import tpu as pltpu
from jax.sharding import PartitionSpec as P

SUBCARRIER_COUNT = 4096
PSYM = 2
B = 32
FA = 16
FB = 256

PANEL = 8
PREC = lax.Precision.HIGH


def _solve_body(a_ref, b_ref, x_ref, s_ref, r_ref, lt_ref, y_ref):
    nb, n, _ = a_ref.shape
    panels = n // PANEL
    s_ref[...] = a_ref[...]
    r_ref[...] = b_ref[...]
    lane = lax.broadcasted_iota(jnp.int32, (1, n), 1)
    sub = lax.broadcasted_iota(jnp.int32, (PANEL, 1), 0)

    def forward(p, carry):
        j0 = pl.multiple_of(p * PANEL, PANEL)
        rows = [s_ref[b, pl.ds(j0, PANEL), :] for b in range(nb)]
        sides = [r_ref[b, pl.ds(j0, PANEL), :] for b in range(nb)]
        factors = [[] for _ in range(nb)]
        solved = [[] for _ in range(nb)]
        for t in range(PANEL):
            j = j0 + t
            hit = lane == j
            keep = lane >= j
            for b in range(nb):
                pivot_row = rows[b][t:t + 1, :]
                column = jnp.sum(jnp.where(hit, rows[b], 0.0), axis=1, keepdims=True)
                inv = 1.0 / jnp.sqrt(column[t:t + 1, :])
                l = jnp.where(keep, pivot_row, 0.0) * inv
                col = column * inv
                rows[b] = rows[b] - col * l
                y = sides[b][t:t + 1, :] * inv
                sides[b] = sides[b] - col * y
                factors[b].append(l)
                solved[b].append(y)
        for b in range(nb):
            block = jnp.concatenate(factors[b], axis=0)
            ys = jnp.concatenate(solved[b], axis=0)
            lt_ref[b, pl.ds(j0, PANEL), :] = block
            y_ref[b, pl.ds(j0, PANEL), :] = ys
            update = lax.dot_general(
                block, jnp.concatenate([block, ys], axis=1), (((0,), (0,)), ((), ())),
                precision=PREC, preferred_element_type=jnp.float32)
            s_ref[b] = s_ref[b] - update[:, :n]
            r_ref[b] = r_ref[b] - update[:, n:]
        return carry

    lax.fori_loop(0, panels, forward, 0)
    x_ref[...] = jnp.zeros(x_ref.shape, jnp.float32)

    def backward(q, carry):
        j0 = pl.multiple_of((panels - 1 - q) * PANEL, PANEL)
        blocks = []
        rests = []
        diags = []
        for b in range(nb):
            block = lt_ref[b, pl.ds(j0, PANEL), :]
            rest = y_ref[b, pl.ds(j0, PANEL), :] - jnp.dot(
                block, x_ref[b], precision=PREC, preferred_element_type=jnp.float32)
            blocks.append(block)
            rests.append(rest)
            diags.append(1.0 / jnp.sum(jnp.where(lane == j0 + sub, block, 0.0), axis=1, keepdims=True))
        outs = [[None] * PANEL for _ in range(nb)]
        for t in reversed(range(PANEL)):
            hit = lane == j0 + t
            for b in range(nb):
                xt = rests[b][t:t + 1, :] * diags[b][t:t + 1, :]
                col = jnp.sum(jnp.where(hit, blocks[b], 0.0), axis=1, keepdims=True)
                rests[b] = rests[b] - col * xt
                outs[b][t] = xt
        for b in range(nb):
            x_ref[b, pl.ds(j0, PANEL), :] = jnp.concatenate(outs[b], axis=0)
        return carry

    lax.fori_loop(0, panels, backward, 0)


def spd_solve(matrix, rhs):
    nb, n, _ = matrix.shape
    return pl.pallas_call(
        _solve_body,
        out_shape=jax.ShapeDtypeStruct(rhs.shape, jnp.float32),
        scratch_shapes=[
            pltpu.VMEM((nb, n, n), jnp.float32),
            pltpu.VMEM(rhs.shape, jnp.float32),
            pltpu.VMEM((nb, n, n), jnp.float32),
            pltpu.VMEM(rhs.shape, jnp.float32),
        ],
    )(matrix, rhs)


def dft_table(length):
    indices = jnp.arange(length, dtype=jnp.int32)
    phase_index = indices[:, None] * indices[None, :] % length
    angles = phase_index.astype(jnp.float32) * (2.0 * math.pi / length)
    cos_part = jnp.cos(angles)
    sin_part = jnp.sin(angles)
    layout = jnp.stack([jnp.stack([cos_part, -sin_part], 1), jnp.stack([sin_part, cos_part], 1)], 0)
    return layout.astype(jnp.bfloat16)


def twiddle_parts():
    inner_idx = jnp.arange(FA, dtype=jnp.int32)
    outer_idx = jnp.arange(FB, dtype=jnp.int32)
    phase_index = inner_idx[:, None] * outer_idx[None, :] % SUBCARRIER_COUNT
    angles = phase_index.astype(jnp.float32) * (2.0 * math.pi / SUBCARRIER_COUNT)
    factor = 1.0 / math.sqrt(SUBCARRIER_COUNT)
    return (jnp.cos(angles) * factor, jnp.sin(angles) * factor)


def spectra(samples):
    antennas_here = samples.shape[0]
    symbol_count = samples.shape[1]
    shaped = samples.reshape(antennas_here, symbol_count, 2, FA, FB)
    section_one = jnp.einsum(
        "ascnm,cndk->sdkma", shaped, dft_table(FA), preferred_element_type=jnp.float32
    )
    cos_part, sin_part = twiddle_parts()
    cos_part = cos_part[:, :, None]
    sin_part = sin_part[:, :, None]
    real_part = section_one[:, 0] * cos_part + section_one[:, 1] * sin_part
    imag_part = section_one[:, 1] * cos_part - section_one[:, 0] * sin_part
    section_one = jnp.stack([real_part, imag_part], 1).astype(jnp.bfloat16)
    section_two = jnp.einsum(
        "sckma,cmdj->sdkja", section_one, dft_table(FB), preferred_element_type=jnp.float32
    )
    return section_two.astype(jnp.bfloat16)


def split_blocks(spectrum):
    width_b = B // FA
    shape_in = spectrum.shape
    return spectrum.reshape(shape_in[0], 2, FA, shape_in[3] // width_b, width_b, shape_in[4])


def code_table(pilots):
    width_b = B // FA
    position = (
        jnp.arange(PSYM, dtype=jnp.int32)[:, None, None] * B
        + jnp.arange(FA, dtype=jnp.int32)[None, :, None]
        + FA * jnp.arange(width_b, dtype=jnp.int32)[None, None, :]
    )
    phase_index = pilots[:, None, None, None] * position[None] % (PSYM * B)
    angles = phase_index.astype(jnp.float32) * (2.0 * math.pi / (PSYM * B))
    factor = 1.0 / math.sqrt(PSYM * B)
    cos_part = jnp.cos(angles) * factor
    sin_part = jnp.sin(angles) * factor
    rows_real = jnp.stack([cos_part, sin_part], 2)
    rows_imag = jnp.stack([-sin_part, cos_part], 2)
    return jnp.stack([rows_real, rows_imag], 0).astype(jnp.bfloat16)


def block_terms(pilot_part, data_part, code_rows):
    channel = jnp.einsum(
        "tcarbm,dktcab->rdkm", pilot_part, code_rows, preferred_element_type=jnp.float32
    ).astype(jnp.bfloat16)
    gram = jnp.einsum("rdkm,relm->rdkel", channel, channel, preferred_element_type=jnp.float32)
    gram_real = gram[:, 0, :, 0] + gram[:, 1, :, 1]
    gram_imag = gram[:, 0, :, 1] - gram[:, 1, :, 0]
    matched = jnp.einsum(
        "rdkm,tcarbm->rdktcab", channel, data_part, preferred_element_type=jnp.float32
    )
    matched_real = matched[:, 0, :, :, 0] + matched[:, 1, :, :, 1]
    matched_imag = matched[:, 0, :, :, 1] - matched[:, 1, :, :, 0]
    blocks = matched_real.shape[0]
    user_count = matched_real.shape[1]
    matched_real = matched_real.reshape(blocks, user_count, -1)
    matched_imag = matched_imag.reshape(blocks, user_count, -1)
    left_half = jnp.stack([gram_real, gram_imag], 1)
    right_half = jnp.stack([matched_real, matched_imag], 1)
    return jnp.concatenate([left_half, right_half], 3)


def mmse_equalizer(packed_layout, served_users, loading, antennas):
    user_count = served_users.shape[1]
    pair_mask = served_users[:, :, None] * served_users[:, None, :]
    diagonal = jnp.eye(user_count, dtype=jnp.float32) * loading[None, :]
    sys_real = pair_mask * packed_layout[:, 0, :, :user_count] / antennas + diagonal[None]
    sys_imag = pair_mask * packed_layout[:, 1, :, :user_count] / antennas
    root_count = math.sqrt(antennas)
    side_real = served_users[:, :, None] * packed_layout[:, 0, :, user_count:] / root_count
    side_imag = served_users[:, :, None] * packed_layout[:, 1, :, user_count:] / root_count
    matrix = jnp.concatenate(
        [jnp.concatenate([sys_real, -sys_imag], 2), jnp.concatenate([sys_imag, sys_real], 2)], 1
    )
    right_side = jnp.concatenate([side_real, side_imag], 1)
    solved = spd_solve(matrix, right_side)
    blocks = solved.shape[0]
    solved = solved.reshape(blocks, 2, user_count, -1, FA, B // FA)
    solved = jnp.transpose(solved, (2, 3, 1, 0, 5, 4))
    return solved.reshape(user_count, solved.shape[1], 2, -1)


def packed_terms(pilot_part, data_part, code_rows):
    channel = jnp.einsum(
        "tcarbm,dktcab->rdkm", pilot_part, code_rows, preferred_element_type=jnp.float32
    ).astype(jnp.bfloat16)
    turned = jnp.stack([-channel[:, 1], channel[:, 0]], 1)
    gram_real = jnp.einsum("rckm,rclm->rkl", channel, channel, preferred_element_type=jnp.float32)
    gram_imag = jnp.einsum("rckm,rclm->rkl", turned, channel, preferred_element_type=jnp.float32)
    user_count = gram_real.shape[1]
    row = lax.broadcasted_iota(jnp.int32, (user_count, user_count), 0)
    col = lax.broadcasted_iota(jnp.int32, (user_count, user_count), 1)
    packed = jnp.where(row <= col, gram_real, gram_imag)
    matched_real = jnp.einsum(
        "rckm,tcarbm->rktab", channel, data_part, preferred_element_type=jnp.float32)
    matched_imag = jnp.einsum(
        "rckm,tcarbm->rktab", turned, data_part, preferred_element_type=jnp.float32)
    blocks = matched_real.shape[0]
    matched_real = matched_real.reshape(blocks, user_count, -1)
    matched_imag = matched_imag.reshape(blocks, user_count, -1)
    return jnp.concatenate([packed, matched_real, matched_imag], 2)


def unpack_terms(terms, user_count):
    packed = terms[:, :, :user_count]
    mirrored = jnp.swapaxes(packed, 1, 2)
    row = lax.broadcasted_iota(jnp.int32, (user_count, user_count), 0)
    col = lax.broadcasted_iota(jnp.int32, (user_count, user_count), 1)
    gram_real = jnp.where(row <= col, packed, mirrored)
    gram_imag = jnp.where(row > col, packed, jnp.where(row < col, -mirrored, 0.0))
    width = (terms.shape[2] - user_count) // 2
    matched_real = terms[:, :, user_count:user_count + width]
    matched_imag = terms[:, :, user_count + width:]
    left_half = jnp.stack([gram_real, gram_imag], 1)
    right_half = jnp.stack([matched_real, matched_imag], 1)
    return jnp.concatenate([left_half, right_half], 3)


def halve(parts, bits, bit, position, fh_size):
    axis = bits.index(bit)
    mine = (position >> bit) & 1
    keep = lax.dynamic_index_in_dim(parts, mine, axis=axis, keepdims=False)
    send = lax.dynamic_index_in_dim(parts, 1 - mine, axis=axis, keepdims=False)
    pairs = [(i, i ^ (1 << bit)) for i in range(fh_size)]
    return keep + lax.ppermute(send, "fh", perm=pairs), bits[:axis] + bits[axis + 1:]


def halving_reduce_scatter(terms, fh_size):
    position = lax.axis_index("fh")
    count = fh_size.bit_length() - 1
    bits = list(reversed(range(count)))
    parts = terms.reshape(*([2] * count), -1, *terms.shape[1:])
    share = parts.shape[count]
    if count < 3 or share % 2:
        for bit in range(count):
            parts, bits = halve(parts, bits, bit, position, fh_size)
        return parts.reshape(-1, *terms.shape[1:])
    parts, bits = halve(parts, bits, 0, position, fh_size)
    first = lax.slice_in_dim(parts, 0, share // 2, axis=count - 1)
    second = lax.slice_in_dim(parts, share // 2, share, axis=count - 1)
    bits_first = bits_second = bits
    order_first = list(range(1, count))
    order_second = [2, 1] + list(range(3, count))
    for bit_first, bit_second in zip(order_first, order_second):
        first, bits_first = halve(first, bits_first, bit_first, position, fh_size)
        second, bits_second = halve(second, bits_second, bit_second, position, fh_size)
    return jnp.concatenate([first, second], axis=0).reshape(-1, *terms.shape[1:])


def on_device(received_time_rows, pilots, active_users, allocation, loading, fh_size):
    spectrum = spectra(received_time_rows)
    code_rows = code_table(pilots)
    terms = packed_terms(split_blocks(spectrum[:PSYM]), split_blocks(spectrum[PSYM:]), code_rows)
    terms = halving_reduce_scatter(terms, fh_size)
    antenna_total = received_time_rows.shape[0] * fh_size
    packed_layout = unpack_terms(terms, pilots.shape[0])
    served_users = active_users.astype(jnp.float32)[None, :] * allocation.astype(jnp.float32)
    result = mmse_equalizer(packed_layout, served_users, loading, antenna_total)
    return lax.all_to_all(result, "fh", split_axis=0, concat_axis=3, tiled=True)


def solution(mesh):
    return jax.shard_map(
        functools.partial(on_device, fh_size=mesh.shape["fh"]),
        mesh=mesh,
        in_specs=(
            P(("cells", "fh"), None, None, None),
            P("cells"),
            P("cells"),
            P(("cells", "fh"), None),
            P("cells"),
        ),
        out_specs=P(("cells", "fh"), None, None, None),
        check_vma=False,
    )
```

```python
import functools
import math

import jax
import jax.numpy as jnp
from jax import lax
from jax.experimental import pallas as pl
from jax.experimental.pallas import tpu as pltpu
from jax.sharding import PartitionSpec as P

SUBCARRIER_COUNT = 4096
PSYM = 2
B = 32
FA = 16
FB = 256

PANEL = 8
PREC = lax.Precision.HIGH


def _solve_body(a_ref, b_ref, x_ref, s_ref, r_ref, lt_ref, y_ref):
    nb, n, _ = a_ref.shape
    panels = n // PANEL
    s_ref[...] = a_ref[...]
    r_ref[...] = b_ref[...]
    lane = lax.broadcasted_iota(jnp.int32, (1, n), 1)
    sub = lax.broadcasted_iota(jnp.int32, (PANEL, 1), 0)

    def forward(p, carry):
        j0 = pl.multiple_of(p * PANEL, PANEL)
        rows = [s_ref[b, pl.ds(j0, PANEL), :] for b in range(nb)]
        sides = [r_ref[b, pl.ds(j0, PANEL), :] for b in range(nb)]
        factors = [[] for _ in range(nb)]
        solved = [[] for _ in range(nb)]
        for t in range(PANEL):
            j = j0 + t
            hit = lane == j
            keep = lane >= j
            for b in range(nb):
                pivot_row = rows[b][t:t + 1, :]
                column = jnp.sum(jnp.where(hit, rows[b], 0.0), axis=1, keepdims=True)
                inv = 1.0 / jnp.sqrt(column[t:t + 1, :])
                l = jnp.where(keep, pivot_row, 0.0) * inv
                col = column * inv
                rows[b] = rows[b] - col * l
                y = sides[b][t:t + 1, :] * inv
                sides[b] = sides[b] - col * y
                factors[b].append(l)
                solved[b].append(y)
        for b in range(nb):
            block = jnp.concatenate(factors[b], axis=0)
            ys = jnp.concatenate(solved[b], axis=0)
            lt_ref[b, pl.ds(j0, PANEL), :] = block
            y_ref[b, pl.ds(j0, PANEL), :] = ys
            update = lax.dot_general(
                block, jnp.concatenate([block, ys], axis=1), (((0,), (0,)), ((), ())),
                precision=PREC, preferred_element_type=jnp.float32)
            s_ref[b] = s_ref[b] - update[:, :n]
            r_ref[b] = r_ref[b] - update[:, n:]
        return carry

    lax.fori_loop(0, panels, forward, 0)
    x_ref[...] = jnp.zeros(x_ref.shape, jnp.float32)

    def backward(q, carry):
        j0 = pl.multiple_of((panels - 1 - q) * PANEL, PANEL)
        blocks = []
        rests = []
        diags = []
        for b in range(nb):
            block = lt_ref[b, pl.ds(j0, PANEL), :]
            rest = y_ref[b, pl.ds(j0, PANEL), :] - jnp.dot(
                block, x_ref[b], precision=PREC, preferred_element_type=jnp.float32)
            blocks.append(block)
            rests.append(rest)
            diags.append(1.0 / jnp.sum(jnp.where(lane == j0 + sub, block, 0.0), axis=1, keepdims=True))
        outs = [[None] * PANEL for _ in range(nb)]
        for t in reversed(range(PANEL)):
            hit = lane == j0 + t
            for b in range(nb):
                xt = rests[b][t:t + 1, :] * diags[b][t:t + 1, :]
                col = jnp.sum(jnp.where(hit, blocks[b], 0.0), axis=1, keepdims=True)
                rests[b] = rests[b] - col * xt
                outs[b][t] = xt
        for b in range(nb):
            x_ref[b, pl.ds(j0, PANEL), :] = jnp.concatenate(outs[b], axis=0)
        return carry

    lax.fori_loop(0, panels, backward, 0)


def spd_solve(matrix, rhs):
    nb, n, _ = matrix.shape
    return pl.pallas_call(
        _solve_body,
        out_shape=jax.ShapeDtypeStruct(rhs.shape, jnp.float32),
        scratch_shapes=[
            pltpu.VMEM((nb, n, n), jnp.float32),
            pltpu.VMEM(rhs.shape, jnp.float32),
            pltpu.VMEM((nb, n, n), jnp.float32),
            pltpu.VMEM(rhs.shape, jnp.float32),
        ],
    )(matrix, rhs)


def dft_table(length):
    indices = jnp.arange(length, dtype=jnp.int32)
    phase_index = indices[:, None] * indices[None, :] % length
    angles = phase_index.astype(jnp.float32) * (2.0 * math.pi / length)
    cos_part = jnp.cos(angles)
    sin_part = jnp.sin(angles)
    layout = jnp.stack([jnp.stack([cos_part, -sin_part], 1), jnp.stack([sin_part, cos_part], 1)], 0)
    return layout.astype(jnp.bfloat16)


def twiddle_parts():
    inner_idx = jnp.arange(FA, dtype=jnp.int32)
    outer_idx = jnp.arange(FB, dtype=jnp.int32)
    phase_index = inner_idx[:, None] * outer_idx[None, :] % SUBCARRIER_COUNT
    angles = phase_index.astype(jnp.float32) * (2.0 * math.pi / SUBCARRIER_COUNT)
    factor = 1.0 / math.sqrt(SUBCARRIER_COUNT)
    return (jnp.cos(angles) * factor, jnp.sin(angles) * factor)


def spectra(samples):
    antennas_here = samples.shape[0]
    symbol_count = samples.shape[1]
    shaped = samples.reshape(antennas_here, symbol_count, 2, FA, FB)
    section_one = jnp.einsum(
        "ascnm,cndk->sdkma", shaped, dft_table(FA), preferred_element_type=jnp.float32
    )
    cos_part, sin_part = twiddle_parts()
    cos_part = cos_part[:, :, None]
    sin_part = sin_part[:, :, None]
    real_part = section_one[:, 0] * cos_part + section_one[:, 1] * sin_part
    imag_part = section_one[:, 1] * cos_part - section_one[:, 0] * sin_part
    section_one = jnp.stack([real_part, imag_part], 1).astype(jnp.bfloat16)
    section_two = jnp.einsum(
        "sckma,cmdj->sdkja", section_one, dft_table(FB), preferred_element_type=jnp.float32
    )
    return section_two.astype(jnp.bfloat16)


def split_blocks(spectrum):
    width_b = B // FA
    shape_in = spectrum.shape
    return spectrum.reshape(shape_in[0], 2, FA, shape_in[3] // width_b, width_b, shape_in[4])


def code_table(pilots):
    width_b = B // FA
    position = (
        jnp.arange(PSYM, dtype=jnp.int32)[:, None, None] * B
        + jnp.arange(FA, dtype=jnp.int32)[None, :, None]
        + FA * jnp.arange(width_b, dtype=jnp.int32)[None, None, :]
    )
    phase_index = pilots[:, None, None, None] * position[None] % (PSYM * B)
    angles = phase_index.astype(jnp.float32) * (2.0 * math.pi / (PSYM * B))
    factor = 1.0 / math.sqrt(PSYM * B)
    cos_part = jnp.cos(angles) * factor
    sin_part = jnp.sin(angles) * factor
    rows_real = jnp.stack([cos_part, sin_part], 2)
    rows_imag = jnp.stack([-sin_part, cos_part], 2)
    return jnp.stack([rows_real, rows_imag], 0).astype(jnp.bfloat16)


def block_terms(pilot_part, data_part, code_rows):
    channel = jnp.einsum(
        "tcarbm,dktcab->rdkm", pilot_part, code_rows, preferred_element_type=jnp.float32
    ).astype(jnp.bfloat16)
    gram = jnp.einsum("rdkm,relm->rdkel", channel, channel, preferred_element_type=jnp.float32)
    gram_real = gram[:, 0, :, 0] + gram[:, 1, :, 1]
    gram_imag = gram[:, 0, :, 1] - gram[:, 1, :, 0]
    matched = jnp.einsum(
        "rdkm,tcarbm->rdktcab", channel, data_part, preferred_element_type=jnp.float32
    )
    matched_real = matched[:, 0, :, :, 0] + matched[:, 1, :, :, 1]
    matched_imag = matched[:, 0, :, :, 1] - matched[:, 1, :, :, 0]
    blocks = matched_real.shape[0]
    user_count = matched_real.shape[1]
    matched_real = matched_real.reshape(blocks, user_count, -1)
    matched_imag = matched_imag.reshape(blocks, user_count, -1)
    left_half = jnp.stack([gram_real, gram_imag], 1)
    right_half = jnp.stack([matched_real, matched_imag], 1)
    return jnp.concatenate([left_half, right_half], 3)


def mmse_equalizer(packed_layout, served_users, loading, antennas):
    user_count = served_users.shape[1]
    pair_mask = served_users[:, :, None] * served_users[:, None, :]
    diagonal = jnp.eye(user_count, dtype=jnp.float32) * loading[None, :]
    sys_real = pair_mask * packed_layout[:, 0, :, :user_count] / antennas + diagonal[None]
    sys_imag = pair_mask * packed_layout[:, 1, :, :user_count] / antennas
    root_count = math.sqrt(antennas)
    side_real = served_users[:, :, None] * packed_layout[:, 0, :, user_count:] / root_count
    side_imag = served_users[:, :, None] * packed_layout[:, 1, :, user_count:] / root_count
    matrix = jnp.concatenate(
        [jnp.concatenate([sys_real, -sys_imag], 2), jnp.concatenate([sys_imag, sys_real], 2)], 1
    )
    right_side = jnp.concatenate([side_real, side_imag], 1)
    solved = spd_solve(matrix, right_side)
    blocks = solved.shape[0]
    solved = solved.reshape(blocks, 2, user_count, -1, FA, B // FA)
    solved = jnp.transpose(solved, (2, 3, 1, 0, 5, 4))
    return solved.reshape(user_count, solved.shape[1], 2, -1)


def packed_terms(pilot_part, data_part, code_rows):
    channel = jnp.einsum(
        "tcarbm,dktcab->rdkm", pilot_part, code_rows, preferred_element_type=jnp.float32
    ).astype(jnp.bfloat16)
    turned = jnp.stack([-channel[:, 1], channel[:, 0]], 1)
    gram_real = jnp.einsum("rckm,rclm->rkl", channel, channel, preferred_element_type=jnp.float32)
    gram_imag = jnp.einsum("rckm,rclm->rkl", turned, channel, preferred_element_type=jnp.float32)
    user_count = gram_real.shape[1]
    row = lax.broadcasted_iota(jnp.int32, (user_count, user_count), 0)
    col = lax.broadcasted_iota(jnp.int32, (user_count, user_count), 1)
    packed = jnp.where(row <= col, gram_real, gram_imag)
    blocks = channel.shape[0]
    data_rows = jnp.transpose(data_part, (3, 1, 0, 2, 4, 5))
    data_rows = data_rows.reshape(blocks, 2, -1, data_rows.shape[-1])
    matched_real = jnp.einsum("rckm,rcum->rku", channel, data_rows, preferred_element_type=jnp.float32)
    matched_imag = jnp.einsum("rckm,rcum->rku", turned, data_rows, preferred_element_type=jnp.float32)
    return jnp.concatenate([packed, matched_real, matched_imag], 2)


def unpack_terms(terms, user_count):
    packed = terms[:, :, :user_count]
    mirrored = jnp.swapaxes(packed, 1, 2)
    row = lax.broadcasted_iota(jnp.int32, (user_count, user_count), 0)
    col = lax.broadcasted_iota(jnp.int32, (user_count, user_count), 1)
    gram_real = jnp.where(row <= col, packed, mirrored)
    gram_imag = jnp.where(row > col, packed, jnp.where(row < col, -mirrored, 0.0))
    width = (terms.shape[2] - user_count) // 2
    matched_real = terms[:, :, user_count:user_count + width]
    matched_imag = terms[:, :, user_count + width:]
    left_half = jnp.stack([gram_real, gram_imag], 1)
    right_half = jnp.stack([matched_real, matched_imag], 1)
    return jnp.concatenate([left_half, right_half], 3)


def halve(parts, bits, bit, position, fh_size):
    axis = bits.index(bit)
    mine = (position >> bit) & 1
    keep = lax.dynamic_index_in_dim(parts, mine, axis=axis, keepdims=False)
    send = lax.dynamic_index_in_dim(parts, 1 - mine, axis=axis, keepdims=False)
    pairs = [(i, i ^ (1 << bit)) for i in range(fh_size)]
    return keep + lax.ppermute(send, "fh", perm=pairs), bits[:axis] + bits[axis + 1:]


def halving_reduce_scatter(terms, fh_size):
    position = lax.axis_index("fh")
    count = fh_size.bit_length() - 1
    bits = list(reversed(range(count)))
    parts = terms.reshape(*([2] * count), -1, *terms.shape[1:])
    share = parts.shape[count]
    if count < 3 or share % 2:
        for bit in range(count):
            parts, bits = halve(parts, bits, bit, position, fh_size)
        return parts.reshape(-1, *terms.shape[1:])
    parts, bits = halve(parts, bits, 0, position, fh_size)
    first = lax.slice_in_dim(parts, 0, share // 2, axis=count - 1)
    second = lax.slice_in_dim(parts, share // 2, share, axis=count - 1)
    bits_first = bits_second = bits
    order_first = list(range(1, count))
    order_second = [2, 1] + list(range(3, count))
    for bit_first, bit_second in zip(order_first, order_second):
        first, bits_first = halve(first, bits_first, bit_first, position, fh_size)
        second, bits_second = halve(second, bits_second, bit_second, position, fh_size)
    return jnp.concatenate([first, second], axis=0).reshape(-1, *terms.shape[1:])


def on_device(received_time_rows, pilots, active_users, allocation, loading, fh_size):
    spectrum = spectra(received_time_rows)
    code_rows = code_table(pilots)
    terms = packed_terms(split_blocks(spectrum[:PSYM]), split_blocks(spectrum[PSYM:]), code_rows)
    terms = halving_reduce_scatter(terms, fh_size)
    antenna_total = received_time_rows.shape[0] * fh_size
    packed_layout = unpack_terms(terms, pilots.shape[0])
    served_users = active_users.astype(jnp.float32)[None, :] * allocation.astype(jnp.float32)
    result = mmse_equalizer(packed_layout, served_users, loading, antenna_total)
    return lax.all_to_all(result, "fh", split_axis=0, concat_axis=3, tiled=True)


def solution(mesh):
    return jax.shard_map(
        functools.partial(on_device, fh_size=mesh.shape["fh"]),
        mesh=mesh,
        in_specs=(
            P(("cells", "fh"), None, None, None),
            P("cells"),
            P("cells"),
            P(("cells", "fh"), None),
            P("cells"),
        ),
        out_specs=P(("cells", "fh"), None, None, None),
        check_vma=False,
    )
```

```python
import functools
import math

import jax
import jax.numpy as jnp
from jax import lax
from jax.experimental import pallas as pl
from jax.experimental.pallas import tpu as pltpu
from jax.sharding import PartitionSpec as P

SUBCARRIER_COUNT = 4096
PSYM = 2
B = 32
FA = 16
FB = 256

PANEL = 8
PREC = lax.Precision.HIGH


def _solve_body(a_ref, b_ref, x_ref, s_ref, r_ref, lt_ref, y_ref):
    nb, n, _ = a_ref.shape
    panels = n // PANEL
    s_ref[...] = a_ref[...]
    r_ref[...] = b_ref[...]
    lane = lax.broadcasted_iota(jnp.int32, (1, n), 1)
    sub = lax.broadcasted_iota(jnp.int32, (PANEL, 1), 0)

    def forward(p, carry):
        j0 = p * PANEL
        rows = [s_ref[b, pl.ds(j0, PANEL), :] for b in range(nb)]
        sides = [r_ref[b, pl.ds(j0, PANEL), :] for b in range(nb)]
        factors = [[] for _ in range(nb)]
        solved = [[] for _ in range(nb)]
        for t in range(PANEL):
            j = j0 + t
            hit = lane == j
            keep = lane >= j
            for b in range(nb):
                pivot_row = rows[b][t:t + 1, :]
                column = rows[b][:, j:j + 1]
                inv = 1.0 / jnp.sqrt(column[t:t + 1, :])
                l = jnp.where(keep, pivot_row, 0.0) * inv
                col = column * inv
                rows[b] = rows[b] - col * l
                y = sides[b][t:t + 1, :] * inv
                sides[b] = sides[b] - col * y
                factors[b].append(l)
                solved[b].append(y)
        for b in range(nb):
            block = jnp.concatenate(factors[b], axis=0)
            ys = jnp.concatenate(solved[b], axis=0)
            lt_ref[b, pl.ds(j0, PANEL), :] = block
            y_ref[b, pl.ds(j0, PANEL), :] = ys
            update = lax.dot_general(
                block, jnp.concatenate([block, ys], axis=1), (((0,), (0,)), ((), ())),
                precision=PREC, preferred_element_type=jnp.float32)
            s_ref[b] = s_ref[b] - update[:, :n]
            r_ref[b] = r_ref[b] - update[:, n:]
        return carry

    for p in range(panels):
        forward(p, 0)
    x_ref[...] = jnp.zeros(x_ref.shape, jnp.float32)

    def backward(q, carry):
        j0 = pl.multiple_of((panels - 1 - q) * PANEL, PANEL)
        blocks = []
        rests = []
        diags = []
        for b in range(nb):
            block = lt_ref[b, pl.ds(j0, PANEL), :]
            rest = y_ref[b, pl.ds(j0, PANEL), :] - jnp.dot(
                block, x_ref[b], precision=PREC, preferred_element_type=jnp.float32)
            blocks.append(block)
            rests.append(rest)
            diags.append(1.0 / jnp.sum(jnp.where(lane == j0 + sub, block, 0.0), axis=1, keepdims=True))
        outs = [[None] * PANEL for _ in range(nb)]
        for t in reversed(range(PANEL)):
            hit = lane == j0 + t
            for b in range(nb):
                xt = rests[b][t:t + 1, :] * diags[b][t:t + 1, :]
                col = jnp.sum(jnp.where(hit, blocks[b], 0.0), axis=1, keepdims=True)
                rests[b] = rests[b] - col * xt
                outs[b][t] = xt
        for b in range(nb):
            x_ref[b, pl.ds(j0, PANEL), :] = jnp.concatenate(outs[b], axis=0)
        return carry

    lax.fori_loop(0, panels, backward, 0)


def spd_solve(matrix, rhs):
    nb, n, _ = matrix.shape
    return pl.pallas_call(
        _solve_body,
        out_shape=jax.ShapeDtypeStruct(rhs.shape, jnp.float32),
        scratch_shapes=[
            pltpu.VMEM((nb, n, n), jnp.float32),
            pltpu.VMEM(rhs.shape, jnp.float32),
            pltpu.VMEM((nb, n, n), jnp.float32),
            pltpu.VMEM(rhs.shape, jnp.float32),
        ],
    )(matrix, rhs)


def dft_table(length):
    indices = jnp.arange(length, dtype=jnp.int32)
    phase_index = indices[:, None] * indices[None, :] % length
    angles = phase_index.astype(jnp.float32) * (2.0 * math.pi / length)
    cos_part = jnp.cos(angles)
    sin_part = jnp.sin(angles)
    layout = jnp.stack([jnp.stack([cos_part, -sin_part], 1), jnp.stack([sin_part, cos_part], 1)], 0)
    return layout.astype(jnp.bfloat16)


def twiddle_parts():
    inner_idx = jnp.arange(FA, dtype=jnp.int32)
    outer_idx = jnp.arange(FB, dtype=jnp.int32)
    phase_index = inner_idx[:, None] * outer_idx[None, :] % SUBCARRIER_COUNT
    angles = phase_index.astype(jnp.float32) * (2.0 * math.pi / SUBCARRIER_COUNT)
    factor = 1.0 / math.sqrt(SUBCARRIER_COUNT)
    return (jnp.cos(angles) * factor, jnp.sin(angles) * factor)


def spectra(samples):
    antennas_here = samples.shape[0]
    symbol_count = samples.shape[1]
    shaped = samples.reshape(antennas_here, symbol_count, 2, FA, FB)
    section_one = jnp.einsum(
        "ascnm,cndk->sdkma", shaped, dft_table(FA), preferred_element_type=jnp.float32
    )
    cos_part, sin_part = twiddle_parts()
    cos_part = cos_part[:, :, None]
    sin_part = sin_part[:, :, None]
    real_part = section_one[:, 0] * cos_part + section_one[:, 1] * sin_part
    imag_part = section_one[:, 1] * cos_part - section_one[:, 0] * sin_part
    section_one = jnp.stack([real_part, imag_part], 1).astype(jnp.bfloat16)
    section_two = jnp.einsum(
        "sckma,cmdj->sdkja", section_one, dft_table(FB), preferred_element_type=jnp.float32
    )
    return section_two.astype(jnp.bfloat16)


def split_blocks(spectrum):
    width_b = B // FA
    shape_in = spectrum.shape
    return spectrum.reshape(shape_in[0], 2, FA, shape_in[3] // width_b, width_b, shape_in[4])


def code_table(pilots):
    width_b = B // FA
    position = (
        jnp.arange(PSYM, dtype=jnp.int32)[:, None, None] * B
        + jnp.arange(FA, dtype=jnp.int32)[None, :, None]
        + FA * jnp.arange(width_b, dtype=jnp.int32)[None, None, :]
    )
    phase_index = pilots[:, None, None, None] * position[None] % (PSYM * B)
    angles = phase_index.astype(jnp.float32) * (2.0 * math.pi / (PSYM * B))
    factor = 1.0 / math.sqrt(PSYM * B)
    cos_part = jnp.cos(angles) * factor
    sin_part = jnp.sin(angles) * factor
    rows_real = jnp.stack([cos_part, sin_part], 2)
    rows_imag = jnp.stack([-sin_part, cos_part], 2)
    return jnp.stack([rows_real, rows_imag], 0).astype(jnp.bfloat16)


def block_terms(pilot_part, data_part, code_rows):
    channel = jnp.einsum(
        "tcarbm,dktcab->rdkm", pilot_part, code_rows, preferred_element_type=jnp.float32
    ).astype(jnp.bfloat16)
    gram = jnp.einsum("rdkm,relm->rdkel", channel, channel, preferred_element_type=jnp.float32)
    gram_real = gram[:, 0, :, 0] + gram[:, 1, :, 1]
    gram_imag = gram[:, 0, :, 1] - gram[:, 1, :, 0]
    matched = jnp.einsum(
        "rdkm,tcarbm->rdktcab", channel, data_part, preferred_element_type=jnp.float32
    )
    matched_real = matched[:, 0, :, :, 0] + matched[:, 1, :, :, 1]
    matched_imag = matched[:, 0, :, :, 1] - matched[:, 1, :, :, 0]
    blocks = matched_real.shape[0]
    user_count = matched_real.shape[1]
    matched_real = matched_real.reshape(blocks, user_count, -1)
    matched_imag = matched_imag.reshape(blocks, user_count, -1)
    left_half = jnp.stack([gram_real, gram_imag], 1)
    right_half = jnp.stack([matched_real, matched_imag], 1)
    return jnp.concatenate([left_half, right_half], 3)


def mmse_equalizer(packed_layout, served_users, loading, antennas):
    user_count = served_users.shape[1]
    pair_mask = served_users[:, :, None] * served_users[:, None, :]
    diagonal = jnp.eye(user_count, dtype=jnp.float32) * loading[None, :]
    sys_real = pair_mask * packed_layout[:, 0, :, :user_count] / antennas + diagonal[None]
    sys_imag = pair_mask * packed_layout[:, 1, :, :user_count] / antennas
    root_count = math.sqrt(antennas)
    side_real = served_users[:, :, None] * packed_layout[:, 0, :, user_count:] / root_count
    side_imag = served_users[:, :, None] * packed_layout[:, 1, :, user_count:] / root_count
    matrix = jnp.concatenate(
        [jnp.concatenate([sys_real, -sys_imag], 2), jnp.concatenate([sys_imag, sys_real], 2)], 1
    )
    right_side = jnp.concatenate([side_real, side_imag], 1)
    solved = spd_solve(matrix, right_side)
    blocks = solved.shape[0]
    solved = solved.reshape(blocks, 2, user_count, -1, FA, B // FA)
    solved = jnp.transpose(solved, (2, 3, 1, 0, 5, 4))
    return solved.reshape(user_count, solved.shape[1], 2, -1)


def packed_terms(pilot_part, data_part, code_rows):
    channel = jnp.einsum(
        "tcarbm,dktcab->rdkm", pilot_part, code_rows, preferred_element_type=jnp.float32
    ).astype(jnp.bfloat16)
    turned = jnp.stack([-channel[:, 1], channel[:, 0]], 1)
    gram_real = jnp.einsum("rckm,rclm->rkl", channel, channel, preferred_element_type=jnp.float32)
    gram_imag = jnp.einsum("rckm,rclm->rkl", turned, channel, preferred_element_type=jnp.float32)
    user_count = gram_real.shape[1]
    row = lax.broadcasted_iota(jnp.int32, (user_count, user_count), 0)
    col = lax.broadcasted_iota(jnp.int32, (user_count, user_count), 1)
    packed = jnp.where(row <= col, gram_real, gram_imag)
    blocks = channel.shape[0]
    data_rows = jnp.transpose(data_part, (3, 1, 0, 2, 4, 5))
    data_rows = data_rows.reshape(blocks, 2, -1, data_rows.shape[-1])
    matched_real = jnp.einsum("rckm,rcum->rku", channel, data_rows, preferred_element_type=jnp.float32)
    matched_imag = jnp.einsum("rckm,rcum->rku", turned, data_rows, preferred_element_type=jnp.float32)
    return jnp.concatenate([packed, matched_real, matched_imag], 2)


def unpack_terms(terms, user_count):
    packed = terms[:, :, :user_count]
    mirrored = jnp.swapaxes(packed, 1, 2)
    row = lax.broadcasted_iota(jnp.int32, (user_count, user_count), 0)
    col = lax.broadcasted_iota(jnp.int32, (user_count, user_count), 1)
    gram_real = jnp.where(row <= col, packed, mirrored)
    gram_imag = jnp.where(row > col, packed, jnp.where(row < col, -mirrored, 0.0))
    width = (terms.shape[2] - user_count) // 2
    matched_real = terms[:, :, user_count:user_count + width]
    matched_imag = terms[:, :, user_count + width:]
    left_half = jnp.stack([gram_real, gram_imag], 1)
    right_half = jnp.stack([matched_real, matched_imag], 1)
    return jnp.concatenate([left_half, right_half], 3)


def halve(parts, bits, bit, position, fh_size):
    axis = bits.index(bit)
    mine = (position >> bit) & 1
    keep = lax.dynamic_index_in_dim(parts, mine, axis=axis, keepdims=False)
    send = lax.dynamic_index_in_dim(parts, 1 - mine, axis=axis, keepdims=False)
    pairs = [(i, i ^ (1 << bit)) for i in range(fh_size)]
    return keep + lax.ppermute(send, "fh", perm=pairs), bits[:axis] + bits[axis + 1:]


def halving_reduce_scatter(terms, fh_size):
    position = lax.axis_index("fh")
    count = fh_size.bit_length() - 1
    bits = list(reversed(range(count)))
    parts = terms.reshape(*([2] * count), -1, *terms.shape[1:])
    share = parts.shape[count]
    if count < 3 or share % 2:
        for bit in range(count):
            parts, bits = halve(parts, bits, bit, position, fh_size)
        return parts.reshape(-1, *terms.shape[1:])
    parts, bits = halve(parts, bits, 0, position, fh_size)
    first = lax.slice_in_dim(parts, 0, share // 2, axis=count - 1)
    second = lax.slice_in_dim(parts, share // 2, share, axis=count - 1)
    bits_first = bits_second = bits
    order_first = list(range(1, count))
    order_second = [2, 1] + list(range(3, count))
    for bit_first, bit_second in zip(order_first, order_second):
        first, bits_first = halve(first, bits_first, bit_first, position, fh_size)
        second, bits_second = halve(second, bits_second, bit_second, position, fh_size)
    return jnp.concatenate([first, second], axis=0).reshape(-1, *terms.shape[1:])


def on_device(received_time_rows, pilots, active_users, allocation, loading, fh_size):
    spectrum = spectra(received_time_rows)
    code_rows = code_table(pilots)
    terms = packed_terms(split_blocks(spectrum[:PSYM]), split_blocks(spectrum[PSYM:]), code_rows)
    terms = halving_reduce_scatter(terms, fh_size)
    antenna_total = received_time_rows.shape[0] * fh_size
    packed_layout = unpack_terms(terms, pilots.shape[0])
    served_users = active_users.astype(jnp.float32)[None, :] * allocation.astype(jnp.float32)
    result = mmse_equalizer(packed_layout, served_users, loading, antenna_total)
    return lax.all_to_all(result, "fh", split_axis=0, concat_axis=3, tiled=True)


def solution(mesh):
    return jax.shard_map(
        functools.partial(on_device, fh_size=mesh.shape["fh"]),
        mesh=mesh,
        in_specs=(
            P(("cells", "fh"), None, None, None),
            P("cells"),
            P("cells"),
            P(("cells", "fh"), None),
            P("cells"),
        ),
        out_specs=P(("cells", "fh"), None, None, None),
        check_vma=False,
    )
```

```python
import functools
import math

import jax
import jax.numpy as jnp
from jax import lax
from jax.experimental import pallas as pl
from jax.experimental.pallas import tpu as pltpu
from jax.sharding import PartitionSpec as P

SUBCARRIER_COUNT = 4096
PSYM = 2
B = 32
FA = 16
FB = 256

PANEL = 8
PREC = lax.Precision.HIGH


def _solve_body(a_ref, b_ref, x_ref, s_ref, r_ref, lt_ref, y_ref):
    nb, n, _ = a_ref.shape
    panels = n // PANEL
    s_ref[...] = a_ref[...]
    r_ref[...] = b_ref[...]
    lane = lax.broadcasted_iota(jnp.int32, (1, n), 1)
    sub = lax.broadcasted_iota(jnp.int32, (PANEL, 1), 0)

    def forward(p, carry, fixed=True):
        j0 = p * PANEL if fixed else pl.multiple_of(p * PANEL, PANEL)
        rows = [s_ref[b, pl.ds(j0, PANEL), :] for b in range(nb)]
        sides = [r_ref[b, pl.ds(j0, PANEL), :] for b in range(nb)]
        factors = [[] for _ in range(nb)]
        solved = [[] for _ in range(nb)]
        for t in range(PANEL):
            j = j0 + t
            hit = lane == j
            keep = lane >= j
            for b in range(nb):
                pivot_row = rows[b][t:t + 1, :]
                if fixed:
                    column = rows[b][:, j:j + 1]
                else:
                    column = jnp.sum(jnp.where(hit, rows[b], 0.0), axis=1, keepdims=True)
                inv = 1.0 / jnp.sqrt(column[t:t + 1, :])
                l = jnp.where(keep, pivot_row, 0.0) * inv
                col = column * inv
                rows[b] = rows[b] - col * l
                y = sides[b][t:t + 1, :] * inv
                sides[b] = sides[b] - col * y
                factors[b].append(l)
                solved[b].append(y)
        for b in range(nb):
            block = jnp.concatenate(factors[b], axis=0)
            ys = jnp.concatenate(solved[b], axis=0)
            lt_ref[b, pl.ds(j0, PANEL), :] = block
            y_ref[b, pl.ds(j0, PANEL), :] = ys
            update = lax.dot_general(
                block, jnp.concatenate([block, ys], axis=1), (((0,), (0,)), ((), ())),
                precision=PREC, preferred_element_type=jnp.float32)
            s_ref[b] = s_ref[b] - update[:, :n]
            r_ref[b] = r_ref[b] - update[:, n:]
        return carry

    looped = panels // 2
    lax.fori_loop(0, looped, functools.partial(forward, fixed=False), 0)
    for p in range(looped, panels):
        forward(p, 0)
    x_ref[...] = jnp.zeros(x_ref.shape, jnp.float32)

    def backward(q, carry):
        j0 = pl.multiple_of((panels - 1 - q) * PANEL, PANEL)
        blocks = []
        rests = []
        diags = []
        for b in range(nb):
            block = lt_ref[b, pl.ds(j0, PANEL), :]
            rest = y_ref[b, pl.ds(j0, PANEL), :] - jnp.dot(
                block, x_ref[b], precision=PREC, preferred_element_type=jnp.float32)
            blocks.append(block)
            rests.append(rest)
            diags.append(1.0 / jnp.sum(jnp.where(lane == j0 + sub, block, 0.0), axis=1, keepdims=True))
        outs = [[None] * PANEL for _ in range(nb)]
        for t in reversed(range(PANEL)):
            hit = lane == j0 + t
            for b in range(nb):
                xt = rests[b][t:t + 1, :] * diags[b][t:t + 1, :]
                col = jnp.sum(jnp.where(hit, blocks[b], 0.0), axis=1, keepdims=True)
                rests[b] = rests[b] - col * xt
                outs[b][t] = xt
        for b in range(nb):
            x_ref[b, pl.ds(j0, PANEL), :] = jnp.concatenate(outs[b], axis=0)
        return carry

    lax.fori_loop(0, panels, backward, 0)


def spd_solve(matrix, rhs):
    nb, n, _ = matrix.shape
    return pl.pallas_call(
        _solve_body,
        out_shape=jax.ShapeDtypeStruct(rhs.shape, jnp.float32),
        scratch_shapes=[
            pltpu.VMEM((nb, n, n), jnp.float32),
            pltpu.VMEM(rhs.shape, jnp.float32),
            pltpu.VMEM((nb, n, n), jnp.float32),
            pltpu.VMEM(rhs.shape, jnp.float32),
        ],
    )(matrix, rhs)


def dft_table(length):
    indices = jnp.arange(length, dtype=jnp.int32)
    phase_index = indices[:, None] * indices[None, :] % length
    angles = phase_index.astype(jnp.float32) * (2.0 * math.pi / length)
    cos_part = jnp.cos(angles)
    sin_part = jnp.sin(angles)
    layout = jnp.stack([jnp.stack([cos_part, -sin_part], 1), jnp.stack([sin_part, cos_part], 1)], 0)
    return layout.astype(jnp.bfloat16)


def twiddle_parts():
    inner_idx = jnp.arange(FA, dtype=jnp.int32)
    outer_idx = jnp.arange(FB, dtype=jnp.int32)
    phase_index = inner_idx[:, None] * outer_idx[None, :] % SUBCARRIER_COUNT
    angles = phase_index.astype(jnp.float32) * (2.0 * math.pi / SUBCARRIER_COUNT)
    factor = 1.0 / math.sqrt(SUBCARRIER_COUNT)
    return (jnp.cos(angles) * factor, jnp.sin(angles) * factor)


def spectra(samples):
    antennas_here = samples.shape[0]
    symbol_count = samples.shape[1]
    shaped = samples.reshape(antennas_here, symbol_count, 2, FA, FB)
    section_one = jnp.einsum(
        "ascnm,cndk->sdkma", shaped, dft_table(FA), preferred_element_type=jnp.float32
    )
    cos_part, sin_part = twiddle_parts()
    cos_part = cos_part[:, :, None]
    sin_part = sin_part[:, :, None]
    real_part = section_one[:, 0] * cos_part + section_one[:, 1] * sin_part
    imag_part = section_one[:, 1] * cos_part - section_one[:, 0] * sin_part
    section_one = jnp.stack([real_part, imag_part], 1).astype(jnp.bfloat16)
    section_two = jnp.einsum(
        "sckma,cmdj->sdkja", section_one, dft_table(FB), preferred_element_type=jnp.float32
    )
    return section_two.astype(jnp.bfloat16)


def split_blocks(spectrum):
    width_b = B // FA
    shape_in = spectrum.shape
    return spectrum.reshape(shape_in[0], 2, FA, shape_in[3] // width_b, width_b, shape_in[4])


def code_table(pilots):
    width_b = B // FA
    position = (
        jnp.arange(PSYM, dtype=jnp.int32)[:, None, None] * B
        + jnp.arange(FA, dtype=jnp.int32)[None, :, None]
        + FA * jnp.arange(width_b, dtype=jnp.int32)[None, None, :]
    )
    phase_index = pilots[:, None, None, None] * position[None] % (PSYM * B)
    angles = phase_index.astype(jnp.float32) * (2.0 * math.pi / (PSYM * B))
    factor = 1.0 / math.sqrt(PSYM * B)
    cos_part = jnp.cos(angles) * factor
    sin_part = jnp.sin(angles) * factor
    rows_real = jnp.stack([cos_part, sin_part], 2)
    rows_imag = jnp.stack([-sin_part, cos_part], 2)
    return jnp.stack([rows_real, rows_imag], 0).astype(jnp.bfloat16)


def block_terms(pilot_part, data_part, code_rows):
    channel = jnp.einsum(
        "tcarbm,dktcab->rdkm", pilot_part, code_rows, preferred_element_type=jnp.float32
    ).astype(jnp.bfloat16)
    gram = jnp.einsum("rdkm,relm->rdkel", channel, channel, preferred_element_type=jnp.float32)
    gram_real = gram[:, 0, :, 0] + gram[:, 1, :, 1]
    gram_imag = gram[:, 0, :, 1] - gram[:, 1, :, 0]
    matched = jnp.einsum(
        "rdkm,tcarbm->rdktcab", channel, data_part, preferred_element_type=jnp.float32
    )
    matched_real = matched[:, 0, :, :, 0] + matched[:, 1, :, :, 1]
    matched_imag = matched[:, 0, :, :, 1] - matched[:, 1, :, :, 0]
    blocks = matched_real.shape[0]
    user_count = matched_real.shape[1]
    matched_real = matched_real.reshape(blocks, user_count, -1)
    matched_imag = matched_imag.reshape(blocks, user_count, -1)
    left_half = jnp.stack([gram_real, gram_imag], 1)
    right_half = jnp.stack([matched_real, matched_imag], 1)
    return jnp.concatenate([left_half, right_half], 3)


def mmse_equalizer(packed_layout, served_users, loading, antennas):
    user_count = served_users.shape[1]
    pair_mask = served_users[:, :, None] * served_users[:, None, :]
    diagonal = jnp.eye(user_count, dtype=jnp.float32) * loading[None, :]
    sys_real = pair_mask * packed_layout[:, 0, :, :user_count] / antennas + diagonal[None]
    sys_imag = pair_mask * packed_layout[:, 1, :, :user_count] / antennas
    root_count = math.sqrt(antennas)
    side_real = served_users[:, :, None] * packed_layout[:, 0, :, user_count:] / root_count
    side_imag = served_users[:, :, None] * packed_layout[:, 1, :, user_count:] / root_count
    matrix = jnp.concatenate(
        [jnp.concatenate([sys_real, -sys_imag], 2), jnp.concatenate([sys_imag, sys_real], 2)], 1
    )
    right_side = jnp.concatenate([side_real, side_imag], 1)
    solved = spd_solve(matrix, right_side)
    blocks = solved.shape[0]
    solved = solved.reshape(blocks, 2, user_count, -1, FA, B // FA)
    solved = jnp.transpose(solved, (2, 3, 1, 0, 5, 4))
    return solved.reshape(user_count, solved.shape[1], 2, -1)


def packed_terms(pilot_part, data_part, code_rows):
    channel = jnp.einsum(
        "tcarbm,dktcab->rdkm", pilot_part, code_rows, preferred_element_type=jnp.float32
    ).astype(jnp.bfloat16)
    turned = jnp.stack([-channel[:, 1], channel[:, 0]], 1)
    gram_real = jnp.einsum("rckm,rclm->rkl", channel, channel, preferred_element_type=jnp.float32)
    gram_imag = jnp.einsum("rckm,rclm->rkl", turned, channel, preferred_element_type=jnp.float32)
    user_count = gram_real.shape[1]
    row = lax.broadcasted_iota(jnp.int32, (user_count, user_count), 0)
    col = lax.broadcasted_iota(jnp.int32, (user_count, user_count), 1)
    packed = jnp.where(row <= col, gram_real, gram_imag)
    blocks = channel.shape[0]
    data_rows = jnp.transpose(data_part, (3, 1, 0, 2, 4, 5))
    data_rows = data_rows.reshape(blocks, 2, -1, data_rows.shape[-1])
    matched_real = jnp.einsum("rckm,rcum->rku", channel, data_rows, preferred_element_type=jnp.float32)
    matched_imag = jnp.einsum("rckm,rcum->rku", turned, data_rows, preferred_element_type=jnp.float32)
    return jnp.concatenate([packed, matched_real, matched_imag], 2)


def unpack_terms(terms, user_count):
    packed = terms[:, :, :user_count]
    mirrored = jnp.swapaxes(packed, 1, 2)
    row = lax.broadcasted_iota(jnp.int32, (user_count, user_count), 0)
    col = lax.broadcasted_iota(jnp.int32, (user_count, user_count), 1)
    gram_real = jnp.where(row <= col, packed, mirrored)
    gram_imag = jnp.where(row > col, packed, jnp.where(row < col, -mirrored, 0.0))
    width = (terms.shape[2] - user_count) // 2
    matched_real = terms[:, :, user_count:user_count + width]
    matched_imag = terms[:, :, user_count + width:]
    left_half = jnp.stack([gram_real, gram_imag], 1)
    right_half = jnp.stack([matched_real, matched_imag], 1)
    return jnp.concatenate([left_half, right_half], 3)


def halve(parts, bits, bit, position, fh_size):
    axis = bits.index(bit)
    mine = (position >> bit) & 1
    keep = lax.dynamic_index_in_dim(parts, mine, axis=axis, keepdims=False)
    send = lax.dynamic_index_in_dim(parts, 1 - mine, axis=axis, keepdims=False)
    pairs = [(i, i ^ (1 << bit)) for i in range(fh_size)]
    return keep + lax.ppermute(send, "fh", perm=pairs), bits[:axis] + bits[axis + 1:]


def halving_reduce_scatter(terms, fh_size):
    position = lax.axis_index("fh")
    count = fh_size.bit_length() - 1
    bits = list(reversed(range(count)))
    parts = terms.reshape(*([2] * count), -1, *terms.shape[1:])
    share = parts.shape[count]
    if count < 3 or share % 2:
        for bit in range(count):
            parts, bits = halve(parts, bits, bit, position, fh_size)
        return parts.reshape(-1, *terms.shape[1:])
    parts, bits = halve(parts, bits, 0, position, fh_size)
    first = lax.slice_in_dim(parts, 0, share // 2, axis=count - 1)
    second = lax.slice_in_dim(parts, share // 2, share, axis=count - 1)
    bits_first = bits_second = bits
    order_first = list(range(1, count))
    order_second = [2, 1] + list(range(3, count))
    for bit_first, bit_second in zip(order_first, order_second):
        first, bits_first = halve(first, bits_first, bit_first, position, fh_size)
        second, bits_second = halve(second, bits_second, bit_second, position, fh_size)
    return jnp.concatenate([first, second], axis=0).reshape(-1, *terms.shape[1:])


def on_device(received_time_rows, pilots, active_users, allocation, loading, fh_size):
    spectrum = spectra(received_time_rows)
    code_rows = code_table(pilots)
    terms = packed_terms(split_blocks(spectrum[:PSYM]), split_blocks(spectrum[PSYM:]), code_rows)
    terms = halving_reduce_scatter(terms, fh_size)
    antenna_total = received_time_rows.shape[0] * fh_size
    packed_layout = unpack_terms(terms, pilots.shape[0])
    served_users = active_users.astype(jnp.float32)[None, :] * allocation.astype(jnp.float32)
    result = mmse_equalizer(packed_layout, served_users, loading, antenna_total)
    return lax.all_to_all(result, "fh", split_axis=0, concat_axis=3, tiled=True)


def solution(mesh):
    return jax.shard_map(
        functools.partial(on_device, fh_size=mesh.shape["fh"]),
        mesh=mesh,
        in_specs=(
            P(("cells", "fh"), None, None, None),
            P("cells"),
            P("cells"),
            P(("cells", "fh"), None),
            P("cells"),
        ),
        out_specs=P(("cells", "fh"), None, None, None),
        check_vma=False,
    )
```

```python
import functools
import math

import jax
import jax.numpy as jnp
from jax import lax
from jax.experimental import pallas as pl
from jax.experimental.pallas import tpu as pltpu
from jax.sharding import PartitionSpec as P

SUBCARRIER_COUNT = 4096
PSYM = 2
B = 32
FA = 16
FB = 256

PANEL = 16
PREC = lax.Precision.HIGH


def _solve_body(a_ref, b_ref, x_ref, s_ref, r_ref, lt_ref, y_ref):
    nb, n, _ = a_ref.shape
    panels = n // PANEL
    s_ref[...] = a_ref[...]
    r_ref[...] = b_ref[...]
    lane = lax.broadcasted_iota(jnp.int32, (1, n), 1)
    sub = lax.broadcasted_iota(jnp.int32, (PANEL, 1), 0)

    def forward(p, carry, fixed=True):
        j0 = p * PANEL if fixed else pl.multiple_of(p * PANEL, PANEL)
        rows = [s_ref[b, pl.ds(j0, PANEL), :] for b in range(nb)]
        sides = [r_ref[b, pl.ds(j0, PANEL), :] for b in range(nb)]
        factors = [[] for _ in range(nb)]
        solved = [[] for _ in range(nb)]
        for t in range(PANEL):
            j = j0 + t
            hit = lane == j
            keep = lane >= j
            for b in range(nb):
                pivot_row = rows[b][t:t + 1, :]
                if fixed:
                    column = rows[b][:, j:j + 1]
                else:
                    column = jnp.sum(jnp.where(hit, rows[b], 0.0), axis=1, keepdims=True)
                inv = 1.0 / jnp.sqrt(column[t:t + 1, :])
                l = jnp.where(keep, pivot_row, 0.0) * inv
                col = column * inv
                rows[b] = rows[b] - col * l
                y = sides[b][t:t + 1, :] * inv
                sides[b] = sides[b] - col * y
                factors[b].append(l)
                solved[b].append(y)
        for b in range(nb):
            block = jnp.concatenate(factors[b], axis=0)
            ys = jnp.concatenate(solved[b], axis=0)
            lt_ref[b, pl.ds(j0, PANEL), :] = block
            y_ref[b, pl.ds(j0, PANEL), :] = ys
            update = lax.dot_general(
                block, jnp.concatenate([block, ys], axis=1), (((0,), (0,)), ((), ())),
                precision=PREC, preferred_element_type=jnp.float32)
            s_ref[b] = s_ref[b] - update[:, :n]
            r_ref[b] = r_ref[b] - update[:, n:]
        return carry

    looped = panels // 2
    lax.fori_loop(0, looped, functools.partial(forward, fixed=False), 0)
    for p in range(looped, panels):
        forward(p, 0)
    x_ref[...] = jnp.zeros(x_ref.shape, jnp.float32)

    def backward(q, carry):
        j0 = pl.multiple_of((panels - 1 - q) * PANEL, PANEL)
        blocks = []
        rests = []
        diags = []
        for b in range(nb):
            block = lt_ref[b, pl.ds(j0, PANEL), :]
            rest = y_ref[b, pl.ds(j0, PANEL), :] - jnp.dot(
                block, x_ref[b], precision=PREC, preferred_element_type=jnp.float32)
            blocks.append(block)
            rests.append(rest)
            diags.append(1.0 / jnp.sum(jnp.where(lane == j0 + sub, block, 0.0), axis=1, keepdims=True))
        outs = [[None] * PANEL for _ in range(nb)]
        for t in reversed(range(PANEL)):
            hit = lane == j0 + t
            for b in range(nb):
                xt = rests[b][t:t + 1, :] * diags[b][t:t + 1, :]
                col = jnp.sum(jnp.where(hit, blocks[b], 0.0), axis=1, keepdims=True)
                rests[b] = rests[b] - col * xt
                outs[b][t] = xt
        for b in range(nb):
            x_ref[b, pl.ds(j0, PANEL), :] = jnp.concatenate(outs[b], axis=0)
        return carry

    lax.fori_loop(0, panels, backward, 0)


def spd_solve(matrix, rhs):
    nb, n, _ = matrix.shape
    return pl.pallas_call(
        _solve_body,
        out_shape=jax.ShapeDtypeStruct(rhs.shape, jnp.float32),
        scratch_shapes=[
            pltpu.VMEM((nb, n, n), jnp.float32),
            pltpu.VMEM(rhs.shape, jnp.float32),
            pltpu.VMEM((nb, n, n), jnp.float32),
            pltpu.VMEM(rhs.shape, jnp.float32),
        ],
    )(matrix, rhs)


def dft_table(length):
    indices = jnp.arange(length, dtype=jnp.int32)
    phase_index = indices[:, None] * indices[None, :] % length
    angles = phase_index.astype(jnp.float32) * (2.0 * math.pi / length)
    cos_part = jnp.cos(angles)
    sin_part = jnp.sin(angles)
    layout = jnp.stack([jnp.stack([cos_part, -sin_part], 1), jnp.stack([sin_part, cos_part], 1)], 0)
    return layout.astype(jnp.bfloat16)


def twiddle_parts():
    inner_idx = jnp.arange(FA, dtype=jnp.int32)
    outer_idx = jnp.arange(FB, dtype=jnp.int32)
    phase_index = inner_idx[:, None] * outer_idx[None, :] % SUBCARRIER_COUNT
    angles = phase_index.astype(jnp.float32) * (2.0 * math.pi / SUBCARRIER_COUNT)
    factor = 1.0 / math.sqrt(SUBCARRIER_COUNT)
    return (jnp.cos(angles) * factor, jnp.sin(angles) * factor)


def spectra(samples):
    antennas_here = samples.shape[0]
    symbol_count = samples.shape[1]
    shaped = samples.reshape(antennas_here, symbol_count, 2, FA, FB)
    section_one = jnp.einsum(
        "ascnm,cndk->sdkma", shaped, dft_table(FA), preferred_element_type=jnp.float32
    )
    cos_part, sin_part = twiddle_parts()
    cos_part = cos_part[:, :, None]
    sin_part = sin_part[:, :, None]
    real_part = section_one[:, 0] * cos_part + section_one[:, 1] * sin_part
    imag_part = section_one[:, 1] * cos_part - section_one[:, 0] * sin_part
    section_one = jnp.stack([real_part, imag_part], 1).astype(jnp.bfloat16)
    section_two = jnp.einsum(
        "sckma,cmdj->sdkja", section_one, dft_table(FB), preferred_element_type=jnp.float32
    )
    return section_two.astype(jnp.bfloat16)


def split_blocks(spectrum):
    width_b = B // FA
    shape_in = spectrum.shape
    return spectrum.reshape(shape_in[0], 2, FA, shape_in[3] // width_b, width_b, shape_in[4])


def code_table(pilots):
    width_b = B // FA
    position = (
        jnp.arange(PSYM, dtype=jnp.int32)[:, None, None] * B
        + jnp.arange(FA, dtype=jnp.int32)[None, :, None]
        + FA * jnp.arange(width_b, dtype=jnp.int32)[None, None, :]
    )
    phase_index = pilots[:, None, None, None] * position[None] % (PSYM * B)
    angles = phase_index.astype(jnp.float32) * (2.0 * math.pi / (PSYM * B))
    factor = 1.0 / math.sqrt(PSYM * B)
    cos_part = jnp.cos(angles) * factor
    sin_part = jnp.sin(angles) * factor
    rows_real = jnp.stack([cos_part, sin_part], 2)
    rows_imag = jnp.stack([-sin_part, cos_part], 2)
    return jnp.stack([rows_real, rows_imag], 0).astype(jnp.bfloat16)


def block_terms(pilot_part, data_part, code_rows):
    channel = jnp.einsum(
        "tcarbm,dktcab->rdkm", pilot_part, code_rows, preferred_element_type=jnp.float32
    ).astype(jnp.bfloat16)
    gram = jnp.einsum("rdkm,relm->rdkel", channel, channel, preferred_element_type=jnp.float32)
    gram_real = gram[:, 0, :, 0] + gram[:, 1, :, 1]
    gram_imag = gram[:, 0, :, 1] - gram[:, 1, :, 0]
    matched = jnp.einsum(
        "rdkm,tcarbm->rdktcab", channel, data_part, preferred_element_type=jnp.float32
    )
    matched_real = matched[:, 0, :, :, 0] + matched[:, 1, :, :, 1]
    matched_imag = matched[:, 0, :, :, 1] - matched[:, 1, :, :, 0]
    blocks = matched_real.shape[0]
    user_count = matched_real.shape[1]
    matched_real = matched_real.reshape(blocks, user_count, -1)
    matched_imag = matched_imag.reshape(blocks, user_count, -1)
    left_half = jnp.stack([gram_real, gram_imag], 1)
    right_half = jnp.stack([matched_real, matched_imag], 1)
    return jnp.concatenate([left_half, right_half], 3)


def mmse_equalizer(packed_layout, served_users, loading, antennas):
    user_count = served_users.shape[1]
    pair_mask = served_users[:, :, None] * served_users[:, None, :]
    diagonal = jnp.eye(user_count, dtype=jnp.float32) * loading[None, :]
    sys_real = pair_mask * packed_layout[:, 0, :, :user_count] / antennas + diagonal[None]
    sys_imag = pair_mask * packed_layout[:, 1, :, :user_count] / antennas
    root_count = math.sqrt(antennas)
    side_real = served_users[:, :, None] * packed_layout[:, 0, :, user_count:] / root_count
    side_imag = served_users[:, :, None] * packed_layout[:, 1, :, user_count:] / root_count
    matrix = jnp.concatenate(
        [jnp.concatenate([sys_real, -sys_imag], 2), jnp.concatenate([sys_imag, sys_real], 2)], 1
    )
    right_side = jnp.concatenate([side_real, side_imag], 1)
    solved = spd_solve(matrix, right_side)
    blocks = solved.shape[0]
    solved = solved.reshape(blocks, 2, user_count, -1, FA, B // FA)
    solved = jnp.transpose(solved, (2, 3, 1, 0, 5, 4))
    return solved.reshape(user_count, solved.shape[1], 2, -1)


def packed_terms(pilot_part, data_part, code_rows):
    channel = jnp.einsum(
        "tcarbm,dktcab->rdkm", pilot_part, code_rows, preferred_element_type=jnp.float32
    ).astype(jnp.bfloat16)
    turned = jnp.stack([-channel[:, 1], channel[:, 0]], 1)
    gram_real = jnp.einsum("rckm,rclm->rkl", channel, channel, preferred_element_type=jnp.float32)
    gram_imag = jnp.einsum("rckm,rclm->rkl", turned, channel, preferred_element_type=jnp.float32)
    user_count = gram_real.shape[1]
    row = lax.broadcasted_iota(jnp.int32, (user_count, user_count), 0)
    col = lax.broadcasted_iota(jnp.int32, (user_count, user_count), 1)
    packed = jnp.where(row <= col, gram_real, gram_imag)
    blocks = channel.shape[0]
    data_rows = jnp.transpose(data_part, (3, 1, 0, 2, 4, 5))
    data_rows = data_rows.reshape(blocks, 2, -1, data_rows.shape[-1])
    matched_real = jnp.einsum("rckm,rcum->rku", channel, data_rows, preferred_element_type=jnp.float32)
    matched_imag = jnp.einsum("rckm,rcum->rku", turned, data_rows, preferred_element_type=jnp.float32)
    return jnp.concatenate([packed, matched_real, matched_imag], 2)


def unpack_terms(terms, user_count):
    packed = terms[:, :, :user_count]
    mirrored = jnp.swapaxes(packed, 1, 2)
    row = lax.broadcasted_iota(jnp.int32, (user_count, user_count), 0)
    col = lax.broadcasted_iota(jnp.int32, (user_count, user_count), 1)
    gram_real = jnp.where(row <= col, packed, mirrored)
    gram_imag = jnp.where(row > col, packed, jnp.where(row < col, -mirrored, 0.0))
    width = (terms.shape[2] - user_count) // 2
    matched_real = terms[:, :, user_count:user_count + width]
    matched_imag = terms[:, :, user_count + width:]
    left_half = jnp.stack([gram_real, gram_imag], 1)
    right_half = jnp.stack([matched_real, matched_imag], 1)
    return jnp.concatenate([left_half, right_half], 3)


def halve(parts, bits, bit, position, fh_size):
    axis = bits.index(bit)
    mine = (position >> bit) & 1
    keep = lax.dynamic_index_in_dim(parts, mine, axis=axis, keepdims=False)
    send = lax.dynamic_index_in_dim(parts, 1 - mine, axis=axis, keepdims=False)
    pairs = [(i, i ^ (1 << bit)) for i in range(fh_size)]
    return keep + lax.ppermute(send, "fh", perm=pairs), bits[:axis] + bits[axis + 1:]


def halving_reduce_scatter(terms, fh_size):
    position = lax.axis_index("fh")
    count = fh_size.bit_length() - 1
    bits = list(reversed(range(count)))
    parts = terms.reshape(*([2] * count), -1, *terms.shape[1:])
    share = parts.shape[count]
    if count < 3 or share % 2:
        for bit in range(count):
            parts, bits = halve(parts, bits, bit, position, fh_size)
        return parts.reshape(-1, *terms.shape[1:])
    parts, bits = halve(parts, bits, 0, position, fh_size)
    first = lax.slice_in_dim(parts, 0, share // 2, axis=count - 1)
    second = lax.slice_in_dim(parts, share // 2, share, axis=count - 1)
    bits_first = bits_second = bits
    order_first = list(range(1, count))
    order_second = [2, 1] + list(range(3, count))
    for bit_first, bit_second in zip(order_first, order_second):
        first, bits_first = halve(first, bits_first, bit_first, position, fh_size)
        second, bits_second = halve(second, bits_second, bit_second, position, fh_size)
    return jnp.concatenate([first, second], axis=0).reshape(-1, *terms.shape[1:])


def on_device(received_time_rows, pilots, active_users, allocation, loading, fh_size):
    spectrum = spectra(received_time_rows)
    code_rows = code_table(pilots)
    terms = packed_terms(split_blocks(spectrum[:PSYM]), split_blocks(spectrum[PSYM:]), code_rows)
    terms = halving_reduce_scatter(terms, fh_size)
    antenna_total = received_time_rows.shape[0] * fh_size
    packed_layout = unpack_terms(terms, pilots.shape[0])
    served_users = active_users.astype(jnp.float32)[None, :] * allocation.astype(jnp.float32)
    result = mmse_equalizer(packed_layout, served_users, loading, antenna_total)
    return lax.all_to_all(result, "fh", split_axis=0, concat_axis=3, tiled=True)


def solution(mesh):
    return jax.shard_map(
        functools.partial(on_device, fh_size=mesh.shape["fh"]),
        mesh=mesh,
        in_specs=(
            P(("cells", "fh"), None, None, None),
            P("cells"),
            P("cells"),
            P(("cells", "fh"), None),
            P("cells"),
        ),
        out_specs=P(("cells", "fh"), None, None, None),
        check_vma=False,
    )
```

```python
import functools
import math

import jax
import jax.numpy as jnp
from jax import lax
from jax.experimental import pallas as pl
from jax.experimental.pallas import tpu as pltpu
from jax.sharding import PartitionSpec as P

SUBCARRIER_COUNT = 4096
PSYM = 2
B = 32
FA = 16
FB = 256

PANEL = 32
PREC = lax.Precision.HIGH


def _solve_body(a_ref, b_ref, x_ref, s_ref, r_ref, lt_ref, y_ref):
    nb, n, _ = a_ref.shape
    panels = n // PANEL
    s_ref[...] = a_ref[...]
    r_ref[...] = b_ref[...]
    lane = lax.broadcasted_iota(jnp.int32, (1, n), 1)
    sub = lax.broadcasted_iota(jnp.int32, (PANEL, 1), 0)

    def forward(p, carry, fixed=True):
        j0 = p * PANEL if fixed else pl.multiple_of(p * PANEL, PANEL)
        rows = [s_ref[b, pl.ds(j0, PANEL), :] for b in range(nb)]
        sides = [r_ref[b, pl.ds(j0, PANEL), :] for b in range(nb)]
        factors = [[] for _ in range(nb)]
        solved = [[] for _ in range(nb)]
        for t in range(PANEL):
            j = j0 + t
            hit = lane == j
            keep = lane >= j
            for b in range(nb):
                pivot_row = rows[b][t:t + 1, :]
                if fixed:
                    column = rows[b][:, j:j + 1]
                else:
                    column = jnp.sum(jnp.where(hit, rows[b], 0.0), axis=1, keepdims=True)
                inv = 1.0 / jnp.sqrt(column[t:t + 1, :])
                l = jnp.where(keep, pivot_row, 0.0) * inv
                col = column * inv
                rows[b] = rows[b] - col * l
                y = sides[b][t:t + 1, :] * inv
                sides[b] = sides[b] - col * y
                factors[b].append(l)
                solved[b].append(y)
        for b in range(nb):
            block = jnp.concatenate(factors[b], axis=0)
            ys = jnp.concatenate(solved[b], axis=0)
            lt_ref[b, pl.ds(j0, PANEL), :] = block
            y_ref[b, pl.ds(j0, PANEL), :] = ys
            update = lax.dot_general(
                block, jnp.concatenate([block, ys], axis=1), (((0,), (0,)), ((), ())),
                precision=PREC, preferred_element_type=jnp.float32)
            s_ref[b] = s_ref[b] - update[:, :n]
            r_ref[b] = r_ref[b] - update[:, n:]
        return carry

    looped = panels - 1
    lax.fori_loop(0, looped, functools.partial(forward, fixed=False), 0)
    for p in range(looped, panels):
        forward(p, 0)
    x_ref[...] = jnp.zeros(x_ref.shape, jnp.float32)

    def backward(q, carry):
        j0 = pl.multiple_of((panels - 1 - q) * PANEL, PANEL)
        blocks = []
        rests = []
        diags = []
        for b in range(nb):
            block = lt_ref[b, pl.ds(j0, PANEL), :]
            rest = y_ref[b, pl.ds(j0, PANEL), :] - jnp.dot(
                block, x_ref[b], precision=PREC, preferred_element_type=jnp.float32)
            blocks.append(block)
            rests.append(rest)
            diags.append(1.0 / jnp.sum(jnp.where(lane == j0 + sub, block, 0.0), axis=1, keepdims=True))
        outs = [[None] * PANEL for _ in range(nb)]
        for t in reversed(range(PANEL)):
            hit = lane == j0 + t
            for b in range(nb):
                xt = rests[b][t:t + 1, :] * diags[b][t:t + 1, :]
                col = jnp.sum(jnp.where(hit, blocks[b], 0.0), axis=1, keepdims=True)
                rests[b] = rests[b] - col * xt
                outs[b][t] = xt
        for b in range(nb):
            x_ref[b, pl.ds(j0, PANEL), :] = jnp.concatenate(outs[b], axis=0)
        return carry

    lax.fori_loop(0, panels, backward, 0)


def spd_solve(matrix, rhs):
    nb, n, _ = matrix.shape
    return pl.pallas_call(
        _solve_body,
        out_shape=jax.ShapeDtypeStruct(rhs.shape, jnp.float32),
        scratch_shapes=[
            pltpu.VMEM((nb, n, n), jnp.float32),
            pltpu.VMEM(rhs.shape, jnp.float32),
            pltpu.VMEM((nb, n, n), jnp.float32),
            pltpu.VMEM(rhs.shape, jnp.float32),
        ],
    )(matrix, rhs)


def dft_table(length):
    indices = jnp.arange(length, dtype=jnp.int32)
    phase_index = indices[:, None] * indices[None, :] % length
    angles = phase_index.astype(jnp.float32) * (2.0 * math.pi / length)
    cos_part = jnp.cos(angles)
    sin_part = jnp.sin(angles)
    layout = jnp.stack([jnp.stack([cos_part, -sin_part], 1), jnp.stack([sin_part, cos_part], 1)], 0)
    return layout.astype(jnp.bfloat16)


def twiddle_parts():
    inner_idx = jnp.arange(FA, dtype=jnp.int32)
    outer_idx = jnp.arange(FB, dtype=jnp.int32)
    phase_index = inner_idx[:, None] * outer_idx[None, :] % SUBCARRIER_COUNT
    angles = phase_index.astype(jnp.float32) * (2.0 * math.pi / SUBCARRIER_COUNT)
    factor = 1.0 / math.sqrt(SUBCARRIER_COUNT)
    return (jnp.cos(angles) * factor, jnp.sin(angles) * factor)


def spectra(samples):
    antennas_here = samples.shape[0]
    symbol_count = samples.shape[1]
    shaped = samples.reshape(antennas_here, symbol_count, 2, FA, FB)
    section_one = jnp.einsum(
        "ascnm,cndk->sdkma", shaped, dft_table(FA), preferred_element_type=jnp.float32
    )
    cos_part, sin_part = twiddle_parts()
    cos_part = cos_part[:, :, None]
    sin_part = sin_part[:, :, None]
    real_part = section_one[:, 0] * cos_part + section_one[:, 1] * sin_part
    imag_part = section_one[:, 1] * cos_part - section_one[:, 0] * sin_part
    section_one = jnp.stack([real_part, imag_part], 1).astype(jnp.bfloat16)
    section_two = jnp.einsum(
        "sckma,cmdj->sdkja", section_one, dft_table(FB), preferred_element_type=jnp.float32
    )
    return section_two.astype(jnp.bfloat16)


def split_blocks(spectrum):
    width_b = B // FA
    shape_in = spectrum.shape
    return spectrum.reshape(shape_in[0], 2, FA, shape_in[3] // width_b, width_b, shape_in[4])


def code_table(pilots):
    width_b = B // FA
    position = (
        jnp.arange(PSYM, dtype=jnp.int32)[:, None, None] * B
        + jnp.arange(FA, dtype=jnp.int32)[None, :, None]
        + FA * jnp.arange(width_b, dtype=jnp.int32)[None, None, :]
    )
    phase_index = pilots[:, None, None, None] * position[None] % (PSYM * B)
    angles = phase_index.astype(jnp.float32) * (2.0 * math.pi / (PSYM * B))
    factor = 1.0 / math.sqrt(PSYM * B)
    cos_part = jnp.cos(angles) * factor
    sin_part = jnp.sin(angles) * factor
    rows_real = jnp.stack([cos_part, sin_part], 2)
    rows_imag = jnp.stack([-sin_part, cos_part], 2)
    return jnp.stack([rows_real, rows_imag], 0).astype(jnp.bfloat16)


def block_terms(pilot_part, data_part, code_rows):
    channel = jnp.einsum(
        "tcarbm,dktcab->rdkm", pilot_part, code_rows, preferred_element_type=jnp.float32
    ).astype(jnp.bfloat16)
    gram = jnp.einsum("rdkm,relm->rdkel", channel, channel, preferred_element_type=jnp.float32)
    gram_real = gram[:, 0, :, 0] + gram[:, 1, :, 1]
    gram_imag = gram[:, 0, :, 1] - gram[:, 1, :, 0]
    matched = jnp.einsum(
        "rdkm,tcarbm->rdktcab", channel, data_part, preferred_element_type=jnp.float32
    )
    matched_real = matched[:, 0, :, :, 0] + matched[:, 1, :, :, 1]
    matched_imag = matched[:, 0, :, :, 1] - matched[:, 1, :, :, 0]
    blocks = matched_real.shape[0]
    user_count = matched_real.shape[1]
    matched_real = matched_real.reshape(blocks, user_count, -1)
    matched_imag = matched_imag.reshape(blocks, user_count, -1)
    left_half = jnp.stack([gram_real, gram_imag], 1)
    right_half = jnp.stack([matched_real, matched_imag], 1)
    return jnp.concatenate([left_half, right_half], 3)


def mmse_equalizer(packed_layout, served_users, loading, antennas):
    user_count = served_users.shape[1]
    pair_mask = served_users[:, :, None] * served_users[:, None, :]
    diagonal = jnp.eye(user_count, dtype=jnp.float32) * loading[None, :]
    sys_real = pair_mask * packed_layout[:, 0, :, :user_count] / antennas + diagonal[None]
    sys_imag = pair_mask * packed_layout[:, 1, :, :user_count] / antennas
    root_count = math.sqrt(antennas)
    side_real = served_users[:, :, None] * packed_layout[:, 0, :, user_count:] / root_count
    side_imag = served_users[:, :, None] * packed_layout[:, 1, :, user_count:] / root_count
    matrix = jnp.concatenate(
        [jnp.concatenate([sys_real, -sys_imag], 2), jnp.concatenate([sys_imag, sys_real], 2)], 1
    )
    right_side = jnp.concatenate([side_real, side_imag], 1)
    solved = spd_solve(matrix, right_side)
    blocks = solved.shape[0]
    solved = solved.reshape(blocks, 2, user_count, -1, FA, B // FA)
    solved = jnp.transpose(solved, (2, 3, 1, 0, 5, 4))
    return solved.reshape(user_count, solved.shape[1], 2, -1)


def packed_terms(pilot_part, data_part, code_rows):
    channel = jnp.einsum(
        "tcarbm,dktcab->rdkm", pilot_part, code_rows, preferred_element_type=jnp.float32
    ).astype(jnp.bfloat16)
    turned = jnp.stack([-channel[:, 1], channel[:, 0]], 1)
    gram_real = jnp.einsum("rckm,rclm->rkl", channel, channel, preferred_element_type=jnp.float32)
    gram_imag = jnp.einsum("rckm,rclm->rkl", turned, channel, preferred_element_type=jnp.float32)
    user_count = gram_real.shape[1]
    row = lax.broadcasted_iota(jnp.int32, (user_count, user_count), 0)
    col = lax.broadcasted_iota(jnp.int32, (user_count, user_count), 1)
    packed = jnp.where(row <= col, gram_real, gram_imag)
    blocks = channel.shape[0]
    data_rows = jnp.transpose(data_part, (3, 1, 0, 2, 4, 5))
    data_rows = data_rows.reshape(blocks, 2, -1, data_rows.shape[-1])
    matched_real = jnp.einsum("rckm,rcum->rku", channel, data_rows, preferred_element_type=jnp.float32)
    matched_imag = jnp.einsum("rckm,rcum->rku", turned, data_rows, preferred_element_type=jnp.float32)
    return jnp.concatenate([packed, matched_real, matched_imag], 2)


def unpack_terms(terms, user_count):
    packed = terms[:, :, :user_count]
    mirrored = jnp.swapaxes(packed, 1, 2)
    row = lax.broadcasted_iota(jnp.int32, (user_count, user_count), 0)
    col = lax.broadcasted_iota(jnp.int32, (user_count, user_count), 1)
    gram_real = jnp.where(row <= col, packed, mirrored)
    gram_imag = jnp.where(row > col, packed, jnp.where(row < col, -mirrored, 0.0))
    width = (terms.shape[2] - user_count) // 2
    matched_real = terms[:, :, user_count:user_count + width]
    matched_imag = terms[:, :, user_count + width:]
    left_half = jnp.stack([gram_real, gram_imag], 1)
    right_half = jnp.stack([matched_real, matched_imag], 1)
    return jnp.concatenate([left_half, right_half], 3)


def halve(parts, bits, bit, position, fh_size):
    axis = bits.index(bit)
    mine = (position >> bit) & 1
    keep = lax.dynamic_index_in_dim(parts, mine, axis=axis, keepdims=False)
    send = lax.dynamic_index_in_dim(parts, 1 - mine, axis=axis, keepdims=False)
    pairs = [(i, i ^ (1 << bit)) for i in range(fh_size)]
    return keep + lax.ppermute(send, "fh", perm=pairs), bits[:axis] + bits[axis + 1:]


def halving_reduce_scatter(terms, fh_size):
    position = lax.axis_index("fh")
    count = fh_size.bit_length() - 1
    bits = list(reversed(range(count)))
    parts = terms.reshape(*([2] * count), -1, *terms.shape[1:])
    share = parts.shape[count]
    if count < 3 or share % 2:
        for bit in range(count):
            parts, bits = halve(parts, bits, bit, position, fh_size)
        return parts.reshape(-1, *terms.shape[1:])
    parts, bits = halve(parts, bits, 0, position, fh_size)
    first = lax.slice_in_dim(parts, 0, share // 2, axis=count - 1)
    second = lax.slice_in_dim(parts, share // 2, share, axis=count - 1)
    bits_first = bits_second = bits
    order_first = list(range(1, count))
    order_second = [2, 1] + list(range(3, count))
    for bit_first, bit_second in zip(order_first, order_second):
        first, bits_first = halve(first, bits_first, bit_first, position, fh_size)
        second, bits_second = halve(second, bits_second, bit_second, position, fh_size)
    return jnp.concatenate([first, second], axis=0).reshape(-1, *terms.shape[1:])


def on_device(received_time_rows, pilots, active_users, allocation, loading, fh_size):
    spectrum = spectra(received_time_rows)
    code_rows = code_table(pilots)
    terms = packed_terms(split_blocks(spectrum[:PSYM]), split_blocks(spectrum[PSYM:]), code_rows)
    terms = halving_reduce_scatter(terms, fh_size)
    antenna_total = received_time_rows.shape[0] * fh_size
    packed_layout = unpack_terms(terms, pilots.shape[0])
    served_users = active_users.astype(jnp.float32)[None, :] * allocation.astype(jnp.float32)
    result = mmse_equalizer(packed_layout, served_users, loading, antenna_total)
    return lax.all_to_all(result, "fh", split_axis=0, concat_axis=3, tiled=True)


def solution(mesh):
    return jax.shard_map(
        functools.partial(on_device, fh_size=mesh.shape["fh"]),
        mesh=mesh,
        in_specs=(
            P(("cells", "fh"), None, None, None),
            P("cells"),
            P("cells"),
            P(("cells", "fh"), None),
            P("cells"),
        ),
        out_specs=P(("cells", "fh"), None, None, None),
        check_vma=False,
    )
```

```python
import functools
import math

import jax
import jax.numpy as jnp
from jax import lax
from jax.experimental import pallas as pl
from jax.experimental.pallas import tpu as pltpu
from jax.sharding import PartitionSpec as P

SUBCARRIER_COUNT = 4096
PSYM = 2
B = 32
FA = 16
FB = 256

PANEL = 32
PREC = lax.Precision.HIGH


def _solve_body(a_ref, b_ref, x_ref, s_ref, r_ref, lt_ref, y_ref):
    nb, n, _ = a_ref.shape
    panels = n // PANEL
    s_ref[...] = a_ref[...]
    r_ref[...] = b_ref[...]
    lane = lax.broadcasted_iota(jnp.int32, (1, n), 1)
    sub = lax.broadcasted_iota(jnp.int32, (PANEL, 1), 0)

    def forward(p, carry, fixed=True):
        j0 = p * PANEL if fixed else pl.multiple_of(p * PANEL, PANEL)
        rows = [s_ref[b, pl.ds(j0, PANEL), :] for b in range(nb)]
        sides = [r_ref[b, pl.ds(j0, PANEL), :] for b in range(nb)]
        factors = [[] for _ in range(nb)]
        solved = [[] for _ in range(nb)]
        for t in range(PANEL):
            j = j0 + t
            hit = lane == j
            keep = lane >= j
            for b in range(nb):
                pivot_row = rows[b][t:t + 1, :]
                if fixed:
                    column = rows[b][:, j:j + 1]
                else:
                    column = jnp.sum(jnp.where(hit, rows[b], 0.0), axis=1, keepdims=True)
                inv = 1.0 / jnp.sqrt(column[t:t + 1, :])
                l = jnp.where(keep, pivot_row, 0.0) * inv
                col = column * inv
                rows[b] = rows[b] - col * l
                y = sides[b][t:t + 1, :] * inv
                sides[b] = sides[b] - col * y
                factors[b].append(l)
                solved[b].append(y)
        for b in range(nb):
            block = jnp.concatenate(factors[b], axis=0)
            ys = jnp.concatenate(solved[b], axis=0)
            lt_ref[b, pl.ds(j0, PANEL), :] = block
            y_ref[b, pl.ds(j0, PANEL), :] = ys
            update = lax.dot_general(
                block, jnp.concatenate([block, ys], axis=1), (((0,), (0,)), ((), ())),
                precision=PREC, preferred_element_type=jnp.float32)
            s_ref[b] = s_ref[b] - update[:, :n]
            r_ref[b] = r_ref[b] - update[:, n:]
        return carry

    looped = panels - 1
    lax.fori_loop(0, looped, functools.partial(forward, fixed=False), 0)
    for p in range(looped, panels):
        forward(p, 0)
    x_ref[...] = jnp.zeros(x_ref.shape, jnp.float32)

    def backward(q, carry):
        j0 = pl.multiple_of((panels - 1 - q) * PANEL, PANEL)
        blocks = []
        rests = []
        diags = []
        for b in range(nb):
            block = lt_ref[b, pl.ds(j0, PANEL), :]
            rest = y_ref[b, pl.ds(j0, PANEL), :] - jnp.dot(
                block, x_ref[b], precision=PREC, preferred_element_type=jnp.float32)
            blocks.append(block)
            rests.append(rest)
            diags.append(1.0 / jnp.sum(jnp.where(lane == j0 + sub, block, 0.0), axis=1, keepdims=True))
        outs = [[None] * PANEL for _ in range(nb)]
        for t in reversed(range(PANEL)):
            hit = lane == j0 + t
            for b in range(nb):
                xt = rests[b][t:t + 1, :] * diags[b][t:t + 1, :]
                col = jnp.sum(jnp.where(hit, blocks[b], 0.0), axis=1, keepdims=True)
                rests[b] = rests[b] - col * xt
                outs[b][t] = xt
        for b in range(nb):
            x_ref[b, pl.ds(j0, PANEL), :] = jnp.concatenate(outs[b], axis=0)
        return carry

    lax.fori_loop(0, panels, backward, 0)


def spd_solve(matrix, rhs):
    nb, n, _ = matrix.shape
    return pl.pallas_call(
        _solve_body,
        out_shape=jax.ShapeDtypeStruct(rhs.shape, jnp.float32),
        scratch_shapes=[
            pltpu.VMEM((nb, n, n), jnp.float32),
            pltpu.VMEM(rhs.shape, jnp.float32),
            pltpu.VMEM((nb, n, n), jnp.float32),
            pltpu.VMEM(rhs.shape, jnp.float32),
        ],
    )(matrix, rhs)


def dft_table(length):
    indices = jnp.arange(length, dtype=jnp.int32)
    phase_index = indices[:, None] * indices[None, :] % length
    angles = phase_index.astype(jnp.float32) * (2.0 * math.pi / length)
    cos_part = jnp.cos(angles)
    sin_part = jnp.sin(angles)
    layout = jnp.stack([jnp.stack([cos_part, -sin_part], 1), jnp.stack([sin_part, cos_part], 1)], 0)
    return layout.astype(jnp.bfloat16)


def twiddle_parts():
    inner_idx = jnp.arange(FA, dtype=jnp.int32)
    outer_idx = jnp.arange(FB, dtype=jnp.int32)
    phase_index = inner_idx[:, None] * outer_idx[None, :] % SUBCARRIER_COUNT
    angles = phase_index.astype(jnp.float32) * (2.0 * math.pi / SUBCARRIER_COUNT)
    factor = 1.0 / math.sqrt(SUBCARRIER_COUNT)
    return (jnp.cos(angles) * factor, jnp.sin(angles) * factor)


def spectra(samples):
    antennas_here = samples.shape[0]
    symbol_count = samples.shape[1]
    shaped = samples.reshape(antennas_here, symbol_count, 2, FA, FB)
    section_one = jnp.einsum(
        "ascnm,cndk->sdkma", shaped, dft_table(FA), preferred_element_type=jnp.float32
    )
    cos_part, sin_part = twiddle_parts()
    cos_part = cos_part[:, :, None]
    sin_part = sin_part[:, :, None]
    signs = jnp.array([1.0, -1.0], jnp.float32)[None, :, None, None, None]
    section_one = (
        section_one * cos_part[None, None] + section_one[:, ::-1] * (signs * sin_part[None, None])
    ).astype(jnp.bfloat16)
    section_two = jnp.einsum(
        "sckma,cmdj->sdkja", section_one, dft_table(FB), preferred_element_type=jnp.float32
    )
    return section_two.astype(jnp.bfloat16)


def split_blocks(spectrum):
    width_b = B // FA
    shape_in = spectrum.shape
    return spectrum.reshape(shape_in[0], 2, FA, shape_in[3] // width_b, width_b, shape_in[4])


def code_table(pilots):
    width_b = B // FA
    position = (
        jnp.arange(PSYM, dtype=jnp.int32)[:, None, None] * B
        + jnp.arange(FA, dtype=jnp.int32)[None, :, None]
        + FA * jnp.arange(width_b, dtype=jnp.int32)[None, None, :]
    )
    phase_index = pilots[:, None, None, None] * position[None] % (PSYM * B)
    angles = phase_index.astype(jnp.float32) * (2.0 * math.pi / (PSYM * B))
    factor = 1.0 / math.sqrt(PSYM * B)
    cos_part = jnp.cos(angles) * factor
    sin_part = jnp.sin(angles) * factor
    rows_real = jnp.stack([cos_part, sin_part], 2)
    rows_imag = jnp.stack([-sin_part, cos_part], 2)
    return jnp.stack([rows_real, rows_imag], 0).astype(jnp.bfloat16)


def block_terms(pilot_part, data_part, code_rows):
    channel = jnp.einsum(
        "tcarbm,dktcab->rdkm", pilot_part, code_rows, preferred_element_type=jnp.float32
    ).astype(jnp.bfloat16)
    gram = jnp.einsum("rdkm,relm->rdkel", channel, channel, preferred_element_type=jnp.float32)
    gram_real = gram[:, 0, :, 0] + gram[:, 1, :, 1]
    gram_imag = gram[:, 0, :, 1] - gram[:, 1, :, 0]
    matched = jnp.einsum(
        "rdkm,tcarbm->rdktcab", channel, data_part, preferred_element_type=jnp.float32
    )
    matched_real = matched[:, 0, :, :, 0] + matched[:, 1, :, :, 1]
    matched_imag = matched[:, 0, :, :, 1] - matched[:, 1, :, :, 0]
    blocks = matched_real.shape[0]
    user_count = matched_real.shape[1]
    matched_real = matched_real.reshape(blocks, user_count, -1)
    matched_imag = matched_imag.reshape(blocks, user_count, -1)
    left_half = jnp.stack([gram_real, gram_imag], 1)
    right_half = jnp.stack([matched_real, matched_imag], 1)
    return jnp.concatenate([left_half, right_half], 3)


def mmse_equalizer(packed_layout, served_users, loading, antennas):
    user_count = served_users.shape[1]
    pair_mask = served_users[:, :, None] * served_users[:, None, :]
    diagonal = jnp.eye(user_count, dtype=jnp.float32) * loading[None, :]
    sys_real = pair_mask * packed_layout[:, 0, :, :user_count] / antennas + diagonal[None]
    sys_imag = pair_mask * packed_layout[:, 1, :, :user_count] / antennas
    root_count = math.sqrt(antennas)
    side_real = served_users[:, :, None] * packed_layout[:, 0, :, user_count:] / root_count
    side_imag = served_users[:, :, None] * packed_layout[:, 1, :, user_count:] / root_count
    matrix = jnp.concatenate(
        [jnp.concatenate([sys_real, -sys_imag], 2), jnp.concatenate([sys_imag, sys_real], 2)], 1
    )
    right_side = jnp.concatenate([side_real, side_imag], 1)
    solved = spd_solve(matrix, right_side)
    blocks = solved.shape[0]
    solved = solved.reshape(blocks, 2, user_count, -1, FA, B // FA)
    solved = jnp.transpose(solved, (2, 3, 1, 0, 5, 4))
    return solved.reshape(user_count, solved.shape[1], 2, -1)


def packed_terms(pilot_part, data_part, code_rows):
    channel = jnp.einsum(
        "tcarbm,dktcab->rdkm", pilot_part, code_rows, preferred_element_type=jnp.float32
    ).astype(jnp.bfloat16)
    turned = jnp.stack([-channel[:, 1], channel[:, 0]], 1)
    gram_real = jnp.einsum("rckm,rclm->rkl", channel, channel, preferred_element_type=jnp.float32)
    gram_imag = jnp.einsum("rckm,rclm->rkl", turned, channel, preferred_element_type=jnp.float32)
    user_count = gram_real.shape[1]
    row = lax.broadcasted_iota(jnp.int32, (user_count, user_count), 0)
    col = lax.broadcasted_iota(jnp.int32, (user_count, user_count), 1)
    packed = jnp.where(row <= col, gram_real, gram_imag)
    blocks = channel.shape[0]
    data_rows = jnp.transpose(data_part, (3, 1, 0, 2, 4, 5))
    data_rows = data_rows.reshape(blocks, 2, -1, data_rows.shape[-1])
    matched_real = jnp.einsum("rckm,rcum->rku", channel, data_rows, preferred_element_type=jnp.float32)
    matched_imag = jnp.einsum("rckm,rcum->rku", turned, data_rows, preferred_element_type=jnp.float32)
    return jnp.concatenate([packed, matched_real, matched_imag], 2)


def unpack_terms(terms, user_count):
    packed = terms[:, :, :user_count]
    mirrored = jnp.swapaxes(packed, 1, 2)
    row = lax.broadcasted_iota(jnp.int32, (user_count, user_count), 0)
    col = lax.broadcasted_iota(jnp.int32, (user_count, user_count), 1)
    gram_real = jnp.where(row <= col, packed, mirrored)
    gram_imag = jnp.where(row > col, packed, jnp.where(row < col, -mirrored, 0.0))
    width = (terms.shape[2] - user_count) // 2
    matched_real = terms[:, :, user_count:user_count + width]
    matched_imag = terms[:, :, user_count + width:]
    left_half = jnp.stack([gram_real, gram_imag], 1)
    right_half = jnp.stack([matched_real, matched_imag], 1)
    return jnp.concatenate([left_half, right_half], 3)


def halve(parts, bits, bit, position, fh_size):
    axis = bits.index(bit)
    mine = (position >> bit) & 1
    keep = lax.dynamic_index_in_dim(parts, mine, axis=axis, keepdims=False)
    send = lax.dynamic_index_in_dim(parts, 1 - mine, axis=axis, keepdims=False)
    pairs = [(i, i ^ (1 << bit)) for i in range(fh_size)]
    return keep + lax.ppermute(send, "fh", perm=pairs), bits[:axis] + bits[axis + 1:]


def halving_reduce_scatter(terms, fh_size):
    position = lax.axis_index("fh")
    count = fh_size.bit_length() - 1
    bits = list(reversed(range(count)))
    parts = terms.reshape(*([2] * count), -1, *terms.shape[1:])
    share = parts.shape[count]
    if count < 3 or share % 2:
        for bit in range(count):
            parts, bits = halve(parts, bits, bit, position, fh_size)
        return parts.reshape(-1, *terms.shape[1:])
    parts, bits = halve(parts, bits, 0, position, fh_size)
    first = lax.slice_in_dim(parts, 0, share // 2, axis=count - 1)
    second = lax.slice_in_dim(parts, share // 2, share, axis=count - 1)
    bits_first = bits_second = bits
    order_first = list(range(1, count))
    order_second = [2, 1] + list(range(3, count))
    for bit_first, bit_second in zip(order_first, order_second):
        first, bits_first = halve(first, bits_first, bit_first, position, fh_size)
        second, bits_second = halve(second, bits_second, bit_second, position, fh_size)
    return jnp.concatenate([first, second], axis=0).reshape(-1, *terms.shape[1:])


def on_device(received_time_rows, pilots, active_users, allocation, loading, fh_size):
    spectrum = spectra(received_time_rows)
    code_rows = code_table(pilots)
    terms = packed_terms(split_blocks(spectrum[:PSYM]), split_blocks(spectrum[PSYM:]), code_rows)
    terms = halving_reduce_scatter(terms, fh_size)
    antenna_total = received_time_rows.shape[0] * fh_size
    packed_layout = unpack_terms(terms, pilots.shape[0])
    served_users = active_users.astype(jnp.float32)[None, :] * allocation.astype(jnp.float32)
    result = mmse_equalizer(packed_layout, served_users, loading, antenna_total)
    return lax.all_to_all(result, "fh", split_axis=0, concat_axis=3, tiled=True)


def solution(mesh):
    return jax.shard_map(
        functools.partial(on_device, fh_size=mesh.shape["fh"]),
        mesh=mesh,
        in_specs=(
            P(("cells", "fh"), None, None, None),
            P("cells"),
            P("cells"),
            P(("cells", "fh"), None),
            P("cells"),
        ),
        out_specs=P(("cells", "fh"), None, None, None),
        check_vma=False,
    )
```

```python
import functools
import math

import jax
import jax.numpy as jnp
from jax import lax
from jax.experimental import pallas as pl
from jax.experimental.pallas import tpu as pltpu
from jax.sharding import PartitionSpec as P

SUBCARRIER_COUNT = 4096
PSYM = 2
B = 32
FA = 16
FB = 256

PANEL = 32
PREC = lax.Precision.HIGH


def _solve_body(a_ref, b_ref, x_ref, s_ref, r_ref, lt_ref, y_ref):
    nb, n, _ = a_ref.shape
    panels = n // PANEL
    s_ref[...] = a_ref[...]
    r_ref[...] = b_ref[...]
    lane = lax.broadcasted_iota(jnp.int32, (1, n), 1)
    sub = lax.broadcasted_iota(jnp.int32, (PANEL, 1), 0)

    def forward(p, carry, fixed=True):
        j0 = p * PANEL if fixed else pl.multiple_of(p * PANEL, PANEL)
        rows = [s_ref[b, pl.ds(j0, PANEL), :] for b in range(nb)]
        sides = [r_ref[b, pl.ds(j0, PANEL), :] for b in range(nb)]
        factors = [[] for _ in range(nb)]
        solved = [[] for _ in range(nb)]
        for t in range(PANEL):
            j = j0 + t
            hit = lane == j
            keep = lane >= j
            for b in range(nb):
                pivot_row = rows[b][t:t + 1, :]
                if fixed:
                    column = rows[b][:, j:j + 1]
                else:
                    column = jnp.sum(jnp.where(hit, rows[b], 0.0), axis=1, keepdims=True)
                inv = 1.0 / jnp.sqrt(column[t:t + 1, :])
                l = jnp.where(keep, pivot_row, 0.0) * inv
                col = column * inv
                rows[b] = rows[b] - col * l
                y = sides[b][t:t + 1, :] * inv
                sides[b] = sides[b] - col * y
                factors[b].append(l)
                solved[b].append(y)
        for b in range(nb):
            block = jnp.concatenate(factors[b], axis=0)
            ys = jnp.concatenate(solved[b], axis=0)
            lt_ref[b, pl.ds(j0, PANEL), :] = block
            y_ref[b, pl.ds(j0, PANEL), :] = ys
            update = lax.dot_general(
                block, jnp.concatenate([block, ys], axis=1), (((0,), (0,)), ((), ())),
                precision=PREC, preferred_element_type=jnp.float32)
            s_ref[b] = s_ref[b] - update[:, :n]
            r_ref[b] = r_ref[b] - update[:, n:]
        return carry

    looped = panels - 1
    lax.fori_loop(0, looped, functools.partial(forward, fixed=False), 0)
    for p in range(looped, panels):
        forward(p, 0)
    x_ref[...] = jnp.zeros(x_ref.shape, jnp.float32)

    def backward(q, carry):
        j0 = pl.multiple_of((panels - 1 - q) * PANEL, PANEL)
        blocks = []
        rests = []
        diags = []
        for b in range(nb):
            block = lt_ref[b, pl.ds(j0, PANEL), :]
            rest = y_ref[b, pl.ds(j0, PANEL), :] - jnp.dot(
                block, x_ref[b], precision=PREC, preferred_element_type=jnp.float32)
            blocks.append(block)
            rests.append(rest)
            diags.append(1.0 / jnp.sum(jnp.where(lane == j0 + sub, block, 0.0), axis=1, keepdims=True))
        outs = [[None] * PANEL for _ in range(nb)]
        for t in reversed(range(PANEL)):
            hit = lane == j0 + t
            for b in range(nb):
                xt = rests[b][t:t + 1, :] * diags[b][t:t + 1, :]
                col = jnp.sum(jnp.where(hit, blocks[b], 0.0), axis=1, keepdims=True)
                rests[b] = rests[b] - col * xt
                outs[b][t] = xt
        for b in range(nb):
            x_ref[b, pl.ds(j0, PANEL), :] = jnp.concatenate(outs[b], axis=0)
        return carry

    lax.fori_loop(0, panels, backward, 0)


def spd_solve(matrix, rhs):
    nb, n, _ = matrix.shape
    return pl.pallas_call(
        _solve_body,
        out_shape=jax.ShapeDtypeStruct(rhs.shape, jnp.float32),
        scratch_shapes=[
            pltpu.VMEM((nb, n, n), jnp.float32),
            pltpu.VMEM(rhs.shape, jnp.float32),
            pltpu.VMEM((nb, n, n), jnp.float32),
            pltpu.VMEM(rhs.shape, jnp.float32),
        ],
    )(matrix, rhs)


def dft_table(length):
    indices = jnp.arange(length, dtype=jnp.int32)
    phase_index = indices[:, None] * indices[None, :] % length
    angles = phase_index.astype(jnp.float32) * (2.0 * math.pi / length)
    cos_part = jnp.cos(angles)
    sin_part = jnp.sin(angles)
    layout = jnp.stack([jnp.stack([cos_part, -sin_part], 1), jnp.stack([sin_part, cos_part], 1)], 0)
    return layout.astype(jnp.bfloat16)


def twiddle_parts():
    inner_idx = jnp.arange(FA, dtype=jnp.int32)
    outer_idx = jnp.arange(FB, dtype=jnp.int32)
    phase_index = inner_idx[:, None] * outer_idx[None, :] % SUBCARRIER_COUNT
    angles = phase_index.astype(jnp.float32) * (2.0 * math.pi / SUBCARRIER_COUNT)
    factor = 1.0 / math.sqrt(SUBCARRIER_COUNT)
    return (jnp.cos(angles) * factor, jnp.sin(angles) * factor)


def spectra(samples):
    antennas_here = samples.shape[0]
    symbol_count = samples.shape[1]
    shaped = samples.reshape(antennas_here, symbol_count, 2, FA, FB)
    section_one = jnp.einsum(
        "ascnm,cndk->sdkma", shaped, dft_table(FA), preferred_element_type=jnp.float32
    )
    cos_part, sin_part = twiddle_parts()
    cos_part = cos_part[:, :, None]
    sin_part = sin_part[:, :, None]
    real_part = section_one[:, 0] * cos_part + section_one[:, 1] * sin_part
    imag_part = section_one[:, 1] * cos_part - section_one[:, 0] * sin_part
    section_one = jnp.stack([real_part, imag_part], 1).astype(jnp.bfloat16)
    section_two = jnp.einsum(
        "sckma,cmdj->sdkja", section_one, dft_table(FB), preferred_element_type=jnp.float32
    )
    return section_two.astype(jnp.bfloat16)


def split_blocks(spectrum):
    width_b = B // FA
    shape_in = spectrum.shape
    return spectrum.reshape(shape_in[0], 2, FA, shape_in[3] // width_b, width_b, shape_in[4])


def code_table(pilots):
    width_b = B // FA
    position = (
        jnp.arange(PSYM, dtype=jnp.int32)[:, None, None] * B
        + jnp.arange(FA, dtype=jnp.int32)[None, :, None]
        + FA * jnp.arange(width_b, dtype=jnp.int32)[None, None, :]
    )
    phase_index = pilots[:, None, None, None] * position[None] % (PSYM * B)
    angles = phase_index.astype(jnp.float32) * (2.0 * math.pi / (PSYM * B))
    factor = 1.0 / math.sqrt(PSYM * B)
    cos_part = jnp.cos(angles) * factor
    sin_part = jnp.sin(angles) * factor
    rows_real = jnp.stack([cos_part, sin_part], 2)
    rows_imag = jnp.stack([-sin_part, cos_part], 2)
    return jnp.stack([rows_real, rows_imag], 0).astype(jnp.bfloat16)


def block_terms(pilot_part, data_part, code_rows):
    channel = jnp.einsum(
        "tcarbm,dktcab->rdkm", pilot_part, code_rows, preferred_element_type=jnp.float32
    ).astype(jnp.bfloat16)
    gram = jnp.einsum("rdkm,relm->rdkel", channel, channel, preferred_element_type=jnp.float32)
    gram_real = gram[:, 0, :, 0] + gram[:, 1, :, 1]
    gram_imag = gram[:, 0, :, 1] - gram[:, 1, :, 0]
    matched = jnp.einsum(
        "rdkm,tcarbm->rdktcab", channel, data_part, preferred_element_type=jnp.float32
    )
    matched_real = matched[:, 0, :, :, 0] + matched[:, 1, :, :, 1]
    matched_imag = matched[:, 0, :, :, 1] - matched[:, 1, :, :, 0]
    blocks = matched_real.shape[0]
    user_count = matched_real.shape[1]
    matched_real = matched_real.reshape(blocks, user_count, -1)
    matched_imag = matched_imag.reshape(blocks, user_count, -1)
    left_half = jnp.stack([gram_real, gram_imag], 1)
    right_half = jnp.stack([matched_real, matched_imag], 1)
    return jnp.concatenate([left_half, right_half], 3)


def mmse_equalizer(packed_layout, served_users, loading, antennas):
    user_count = served_users.shape[1]
    pair_mask = served_users[:, :, None] * served_users[:, None, :]
    diagonal = jnp.eye(user_count, dtype=jnp.float32) * loading[None, :]
    sys_real = pair_mask * packed_layout[:, 0, :, :user_count] / antennas + diagonal[None]
    sys_imag = pair_mask * packed_layout[:, 1, :, :user_count] / antennas
    root_count = math.sqrt(antennas)
    side_real = served_users[:, :, None] * packed_layout[:, 0, :, user_count:] / root_count
    side_imag = served_users[:, :, None] * packed_layout[:, 1, :, user_count:] / root_count
    matrix = jnp.concatenate(
        [jnp.concatenate([sys_real, -sys_imag], 2), jnp.concatenate([sys_imag, sys_real], 2)], 1
    )
    right_side = jnp.concatenate([side_real, side_imag], 1)
    solved = spd_solve(matrix, right_side)
    blocks = solved.shape[0]
    solved = solved.reshape(blocks, 2, user_count, -1, FA, B // FA)
    solved = jnp.transpose(solved, (2, 3, 1, 0, 5, 4))
    return solved.reshape(user_count, solved.shape[1], 2, -1)


def packed_terms(pilot_part, data_part, code_rows):
    channel = jnp.einsum(
        "tcarbm,dktcab->rdkm", pilot_part, code_rows, preferred_element_type=jnp.float32
    ).astype(jnp.bfloat16)
    turned = jnp.stack([-channel[:, 1], channel[:, 0]], 1)
    gram_real = jnp.einsum("rckm,rclm->rkl", channel, channel, preferred_element_type=jnp.float32)
    gram_imag = jnp.einsum("rckm,rclm->rkl", turned, channel, preferred_element_type=jnp.float32)
    user_count = gram_real.shape[1]
    row = lax.broadcasted_iota(jnp.int32, (user_count, user_count), 0)
    col = lax.broadcasted_iota(jnp.int32, (user_count, user_count), 1)
    packed = jnp.where(row <= col, gram_real, gram_imag)
    blocks = channel.shape[0]
    data_rows = jnp.transpose(data_part, (3, 1, 0, 2, 4, 5))
    data_rows = data_rows.reshape(blocks, 2, -1, data_rows.shape[-1])
    data_turned = jnp.stack([data_rows[:, 1], -data_rows[:, 0]], 1)
    data_both = jnp.concatenate([data_rows, data_turned], axis=2)
    matched = jnp.einsum("rckm,rcum->rku", channel, data_both, preferred_element_type=jnp.float32)
    return jnp.concatenate([packed, matched], 2)


def unpack_terms(terms, user_count):
    packed = terms[:, :, :user_count]
    mirrored = jnp.swapaxes(packed, 1, 2)
    row = lax.broadcasted_iota(jnp.int32, (user_count, user_count), 0)
    col = lax.broadcasted_iota(jnp.int32, (user_count, user_count), 1)
    gram_real = jnp.where(row <= col, packed, mirrored)
    gram_imag = jnp.where(row > col, packed, jnp.where(row < col, -mirrored, 0.0))
    width = (terms.shape[2] - user_count) // 2
    matched_real = terms[:, :, user_count:user_count + width]
    matched_imag = terms[:, :, user_count + width:]
    left_half = jnp.stack([gram_real, gram_imag], 1)
    right_half = jnp.stack([matched_real, matched_imag], 1)
    return jnp.concatenate([left_half, right_half], 3)


def halve(parts, bits, bit, position, fh_size):
    axis = bits.index(bit)
    mine = (position >> bit) & 1
    keep = lax.dynamic_index_in_dim(parts, mine, axis=axis, keepdims=False)
    send = lax.dynamic_index_in_dim(parts, 1 - mine, axis=axis, keepdims=False)
    pairs = [(i, i ^ (1 << bit)) for i in range(fh_size)]
    return keep + lax.ppermute(send, "fh", perm=pairs), bits[:axis] + bits[axis + 1:]


def halving_reduce_scatter(terms, fh_size):
    position = lax.axis_index("fh")
    count = fh_size.bit_length() - 1
    bits = list(reversed(range(count)))
    parts = terms.reshape(*([2] * count), -1, *terms.shape[1:])
    share = parts.shape[count]
    if count < 3 or share % 2:
        for bit in range(count):
            parts, bits = halve(parts, bits, bit, position, fh_size)
        return parts.reshape(-1, *terms.shape[1:])
    parts, bits = halve(parts, bits, 0, position, fh_size)
    first = lax.slice_in_dim(parts, 0, share // 2, axis=count - 1)
    second = lax.slice_in_dim(parts, share // 2, share, axis=count - 1)
    bits_first = bits_second = bits
    order_first = list(range(1, count))
    order_second = [2, 1] + list(range(3, count))
    for bit_first, bit_second in zip(order_first, order_second):
        first, bits_first = halve(first, bits_first, bit_first, position, fh_size)
        second, bits_second = halve(second, bits_second, bit_second, position, fh_size)
    return jnp.concatenate([first, second], axis=0).reshape(-1, *terms.shape[1:])


def on_device(received_time_rows, pilots, active_users, allocation, loading, fh_size):
    spectrum = spectra(received_time_rows)
    code_rows = code_table(pilots)
    terms = packed_terms(split_blocks(spectrum[:PSYM]), split_blocks(spectrum[PSYM:]), code_rows)
    terms = halving_reduce_scatter(terms, fh_size)
    antenna_total = received_time_rows.shape[0] * fh_size
    packed_layout = unpack_terms(terms, pilots.shape[0])
    served_users = active_users.astype(jnp.float32)[None, :] * allocation.astype(jnp.float32)
    result = mmse_equalizer(packed_layout, served_users, loading, antenna_total)
    return lax.all_to_all(result, "fh", split_axis=0, concat_axis=3, tiled=True)


def solution(mesh):
    return jax.shard_map(
        functools.partial(on_device, fh_size=mesh.shape["fh"]),
        mesh=mesh,
        in_specs=(
            P(("cells", "fh"), None, None, None),
            P("cells"),
            P("cells"),
            P(("cells", "fh"), None),
            P("cells"),
        ),
        out_specs=P(("cells", "fh"), None, None, None),
        check_vma=False,
    )
```

```python
import functools
import math

import jax
import jax.numpy as jnp
from jax import lax
from jax.experimental import pallas as pl
from jax.experimental.pallas import tpu as pltpu
from jax.sharding import PartitionSpec as P

SUBCARRIER_COUNT = 4096
PSYM = 2
B = 32
FA = 16
FB = 256

PANEL = 32
PREC = lax.Precision.HIGH


def _solve_body(a_ref, b_ref, x_ref, s_ref, r_ref, lt_ref, y_ref):
    nb, n, _ = a_ref.shape
    panels = n // PANEL
    s_ref[...] = a_ref[...]
    r_ref[...] = b_ref[...]
    lane = lax.broadcasted_iota(jnp.int32, (1, n), 1)
    sub = lax.broadcasted_iota(jnp.int32, (PANEL, 1), 0)

    def forward(p, carry, fixed=True):
        j0 = p * PANEL if fixed else pl.multiple_of(p * PANEL, PANEL)
        rows = [s_ref[b, pl.ds(j0, PANEL), :] for b in range(nb)]
        sides = [r_ref[b, pl.ds(j0, PANEL), :] for b in range(nb)]
        factors = [[] for _ in range(nb)]
        solved = [[] for _ in range(nb)]
        for t in range(PANEL):
            j = j0 + t
            hit = lane == j
            keep = lane >= j
            for b in range(nb):
                pivot_row = rows[b][t:t + 1, :]
                if fixed:
                    column = rows[b][:, j:j + 1]
                else:
                    column = jnp.sum(jnp.where(hit, rows[b], 0.0), axis=1, keepdims=True)
                inv = 1.0 / jnp.sqrt(column[t:t + 1, :])
                l = jnp.where(keep, pivot_row, 0.0) * inv
                col = column * inv
                rows[b] = rows[b] - col * l
                y = sides[b][t:t + 1, :] * inv
                sides[b] = sides[b] - col * y
                factors[b].append(l)
                solved[b].append(y)
        for b in range(nb):
            block = jnp.concatenate(factors[b], axis=0)
            ys = jnp.concatenate(solved[b], axis=0)
            lt_ref[b, pl.ds(j0, PANEL), :] = block
            y_ref[b, pl.ds(j0, PANEL), :] = ys
            update = lax.dot_general(
                block, jnp.concatenate([block, ys], axis=1), (((0,), (0,)), ((), ())),
                precision=PREC, preferred_element_type=jnp.float32)
            s_ref[b] = s_ref[b] - update[:, :n]
            r_ref[b] = r_ref[b] - update[:, n:]
        return carry

    looped = panels - 1
    lax.fori_loop(0, looped, functools.partial(forward, fixed=False), 0)
    for p in range(looped, panels):
        forward(p, 0)
    x_ref[...] = jnp.zeros(x_ref.shape, jnp.float32)

    def backward(q, carry):
        j0 = pl.multiple_of((panels - 1 - q) * PANEL, PANEL)
        blocks = []
        rests = []
        diags = []
        for b in range(nb):
            block = lt_ref[b, pl.ds(j0, PANEL), :]
            rest = y_ref[b, pl.ds(j0, PANEL), :] - jnp.dot(
                block, x_ref[b], precision=PREC, preferred_element_type=jnp.float32)
            blocks.append(block)
            rests.append(rest)
            diags.append(1.0 / jnp.sum(jnp.where(lane == j0 + sub, block, 0.0), axis=1, keepdims=True))
        outs = [[None] * PANEL for _ in range(nb)]
        for t in reversed(range(PANEL)):
            hit = lane == j0 + t
            for b in range(nb):
                xt = rests[b][t:t + 1, :] * diags[b][t:t + 1, :]
                col = jnp.sum(jnp.where(hit, blocks[b], 0.0), axis=1, keepdims=True)
                rests[b] = rests[b] - col * xt
                outs[b][t] = xt
        for b in range(nb):
            x_ref[b, pl.ds(j0, PANEL), :] = jnp.concatenate(outs[b], axis=0)
        return carry

    lax.fori_loop(0, panels, backward, 0)


def spd_solve(matrix, rhs):
    nb, n, _ = matrix.shape
    return pl.pallas_call(
        _solve_body,
        out_shape=jax.ShapeDtypeStruct(rhs.shape, jnp.float32),
        scratch_shapes=[
            pltpu.VMEM((nb, n, n), jnp.float32),
            pltpu.VMEM(rhs.shape, jnp.float32),
            pltpu.VMEM((nb, n, n), jnp.float32),
            pltpu.VMEM(rhs.shape, jnp.float32),
        ],
    )(matrix, rhs)


def dft_table(length):
    indices = jnp.arange(length, dtype=jnp.int32)
    phase_index = indices[:, None] * indices[None, :] % length
    angles = phase_index.astype(jnp.float32) * (2.0 * math.pi / length)
    cos_part = jnp.cos(angles)
    sin_part = jnp.sin(angles)
    layout = jnp.stack([jnp.stack([cos_part, -sin_part], 1), jnp.stack([sin_part, cos_part], 1)], 0)
    return layout.astype(jnp.bfloat16)


def twiddle_parts():
    inner_idx = jnp.arange(FA, dtype=jnp.int32)
    outer_idx = jnp.arange(FB, dtype=jnp.int32)
    phase_index = inner_idx[:, None] * outer_idx[None, :] % SUBCARRIER_COUNT
    angles = phase_index.astype(jnp.float32) * (2.0 * math.pi / SUBCARRIER_COUNT)
    factor = 1.0 / math.sqrt(SUBCARRIER_COUNT)
    return (jnp.cos(angles) * factor, jnp.sin(angles) * factor)


def spectra(samples):
    antennas_here = samples.shape[0]
    symbol_count = samples.shape[1]
    shaped = samples.reshape(antennas_here, symbol_count, 2, FA, FB)
    section_one = jnp.einsum(
        "ascnm,cndk->sdkma", shaped, dft_table(FA), preferred_element_type=jnp.float32
    )
    cos_part, sin_part = twiddle_parts()
    cos_part = cos_part[:, :, None]
    sin_part = sin_part[:, :, None]
    real_part = section_one[:, 0] * cos_part + section_one[:, 1] * sin_part
    imag_part = section_one[:, 1] * cos_part - section_one[:, 0] * sin_part
    section_one = jnp.stack([real_part, imag_part], 1).astype(jnp.bfloat16)
    section_two = jnp.einsum(
        "sckma,cmdj->sdkja", section_one, dft_table(FB), preferred_element_type=jnp.float32
    )
    return section_two.astype(jnp.bfloat16)


def split_blocks(spectrum):
    width_b = B // FA
    shape_in = spectrum.shape
    return spectrum.reshape(shape_in[0], 2, FA, shape_in[3] // width_b, width_b, shape_in[4])


def code_table(pilots):
    width_b = B // FA
    position = (
        jnp.arange(PSYM, dtype=jnp.int32)[:, None, None] * B
        + jnp.arange(FA, dtype=jnp.int32)[None, :, None]
        + FA * jnp.arange(width_b, dtype=jnp.int32)[None, None, :]
    )
    phase_index = pilots[:, None, None, None] * position[None] % (PSYM * B)
    angles = phase_index.astype(jnp.float32) * (2.0 * math.pi / (PSYM * B))
    factor = 1.0 / math.sqrt(PSYM * B)
    cos_part = jnp.cos(angles) * factor
    sin_part = jnp.sin(angles) * factor
    rows_real = jnp.stack([cos_part, sin_part], 2)
    rows_imag = jnp.stack([-sin_part, cos_part], 2)
    return jnp.stack([rows_real, rows_imag], 0).astype(jnp.bfloat16)


def block_terms(pilot_part, data_part, code_rows):
    channel = jnp.einsum(
        "tcarbm,dktcab->rdkm", pilot_part, code_rows, preferred_element_type=jnp.float32
    ).astype(jnp.bfloat16)
    gram = jnp.einsum("rdkm,relm->rdkel", channel, channel, preferred_element_type=jnp.float32)
    gram_real = gram[:, 0, :, 0] + gram[:, 1, :, 1]
    gram_imag = gram[:, 0, :, 1] - gram[:, 1, :, 0]
    matched = jnp.einsum(
        "rdkm,tcarbm->rdktcab", channel, data_part, preferred_element_type=jnp.float32
    )
    matched_real = matched[:, 0, :, :, 0] + matched[:, 1, :, :, 1]
    matched_imag = matched[:, 0, :, :, 1] - matched[:, 1, :, :, 0]
    blocks = matched_real.shape[0]
    user_count = matched_real.shape[1]
    matched_real = matched_real.reshape(blocks, user_count, -1)
    matched_imag = matched_imag.reshape(blocks, user_count, -1)
    left_half = jnp.stack([gram_real, gram_imag], 1)
    right_half = jnp.stack([matched_real, matched_imag], 1)
    return jnp.concatenate([left_half, right_half], 3)


def mmse_equalizer(packed_layout, served_users, loading, antennas):
    user_count = served_users.shape[1]
    pair_mask = served_users[:, :, None] * served_users[:, None, :]
    diagonal = jnp.eye(user_count, dtype=jnp.float32) * loading[None, :]
    sys_real = pair_mask * packed_layout[:, 0, :, :user_count] / antennas + diagonal[None]
    sys_imag = pair_mask * packed_layout[:, 1, :, :user_count] / antennas
    root_count = math.sqrt(antennas)
    side_real = served_users[:, :, None] * packed_layout[:, 0, :, user_count:] / root_count
    side_imag = served_users[:, :, None] * packed_layout[:, 1, :, user_count:] / root_count
    matrix = jnp.concatenate(
        [jnp.concatenate([sys_real, -sys_imag], 2), jnp.concatenate([sys_imag, sys_real], 2)], 1
    )
    right_side = jnp.concatenate([side_real, side_imag], 1)
    solved = spd_solve(matrix, right_side)
    blocks = solved.shape[0]
    solved = solved.reshape(blocks, 2, user_count, -1, FA, B // FA)
    solved = jnp.transpose(solved, (2, 3, 1, 0, 5, 4))
    return solved.reshape(user_count, solved.shape[1], 2, -1)


def packed_terms(pilot_part, data_part, code_rows):
    channel = jnp.einsum(
        "tcarbm,dktcab->rdkm", pilot_part, code_rows, preferred_element_type=jnp.float32
    ).astype(jnp.bfloat16)
    mirrored = jnp.stack([channel[:, 1], -channel[:, 0]], 1)
    gram = jnp.einsum(
        "rckm,rclm->rkl", channel, jnp.concatenate([channel, mirrored], axis=2),
        preferred_element_type=jnp.float32)
    user_count = channel.shape[2]
    gram_real = gram[:, :, :user_count]
    gram_imag = gram[:, :, user_count:]
    row = lax.broadcasted_iota(jnp.int32, (user_count, user_count), 0)
    col = lax.broadcasted_iota(jnp.int32, (user_count, user_count), 1)
    packed = jnp.where(row <= col, gram_real, gram_imag)
    blocks = channel.shape[0]
    data_rows = jnp.transpose(data_part, (3, 1, 0, 2, 4, 5))
    data_rows = data_rows.reshape(blocks, 2, -1, data_rows.shape[-1])
    data_turned = jnp.stack([data_rows[:, 1], -data_rows[:, 0]], 1)
    data_both = jnp.concatenate([data_rows, data_turned], axis=2)
    matched = jnp.einsum("rckm,rcum->rku", channel, data_both, preferred_element_type=jnp.float32)
    return jnp.concatenate([packed, matched], 2)


def unpack_terms(terms, user_count):
    packed = terms[:, :, :user_count]
    mirrored = jnp.swapaxes(packed, 1, 2)
    row = lax.broadcasted_iota(jnp.int32, (user_count, user_count), 0)
    col = lax.broadcasted_iota(jnp.int32, (user_count, user_count), 1)
    gram_real = jnp.where(row <= col, packed, mirrored)
    gram_imag = jnp.where(row > col, packed, jnp.where(row < col, -mirrored, 0.0))
    width = (terms.shape[2] - user_count) // 2
    matched_real = terms[:, :, user_count:user_count + width]
    matched_imag = terms[:, :, user_count + width:]
    left_half = jnp.stack([gram_real, gram_imag], 1)
    right_half = jnp.stack([matched_real, matched_imag], 1)
    return jnp.concatenate([left_half, right_half], 3)


def halve(parts, bits, bit, position, fh_size):
    axis = bits.index(bit)
    mine = (position >> bit) & 1
    keep = lax.dynamic_index_in_dim(parts, mine, axis=axis, keepdims=False)
    send = lax.dynamic_index_in_dim(parts, 1 - mine, axis=axis, keepdims=False)
    pairs = [(i, i ^ (1 << bit)) for i in range(fh_size)]
    return keep + lax.ppermute(send, "fh", perm=pairs), bits[:axis] + bits[axis + 1:]


def halving_reduce_scatter(terms, fh_size):
    position = lax.axis_index("fh")
    count = fh_size.bit_length() - 1
    bits = list(reversed(range(count)))
    parts = terms.reshape(*([2] * count), -1, *terms.shape[1:])
    share = parts.shape[count]
    if count < 3 or share % 2:
        for bit in range(count):
            parts, bits = halve(parts, bits, bit, position, fh_size)
        return parts.reshape(-1, *terms.shape[1:])
    parts, bits = halve(parts, bits, 0, position, fh_size)
    first = lax.slice_in_dim(parts, 0, share // 2, axis=count - 1)
    second = lax.slice_in_dim(parts, share // 2, share, axis=count - 1)
    bits_first = bits_second = bits
    order_first = list(range(1, count))
    order_second = [2, 1] + list(range(3, count))
    for bit_first, bit_second in zip(order_first, order_second):
        first, bits_first = halve(first, bits_first, bit_first, position, fh_size)
        second, bits_second = halve(second, bits_second, bit_second, position, fh_size)
    return jnp.concatenate([first, second], axis=0).reshape(-1, *terms.shape[1:])


def on_device(received_time_rows, pilots, active_users, allocation, loading, fh_size):
    spectrum = spectra(received_time_rows)
    code_rows = code_table(pilots)
    terms = packed_terms(split_blocks(spectrum[:PSYM]), split_blocks(spectrum[PSYM:]), code_rows)
    terms = halving_reduce_scatter(terms, fh_size)
    antenna_total = received_time_rows.shape[0] * fh_size
    packed_layout = unpack_terms(terms, pilots.shape[0])
    served_users = active_users.astype(jnp.float32)[None, :] * allocation.astype(jnp.float32)
    result = mmse_equalizer(packed_layout, served_users, loading, antenna_total)
    return lax.all_to_all(result, "fh", split_axis=0, concat_axis=3, tiled=True)


def solution(mesh):
    return jax.shard_map(
        functools.partial(on_device, fh_size=mesh.shape["fh"]),
        mesh=mesh,
        in_specs=(
            P(("cells", "fh"), None, None, None),
            P("cells"),
            P("cells"),
            P(("cells", "fh"), None),
            P("cells"),
        ),
        out_specs=P(("cells", "fh"), None, None, None),
        check_vma=False,
    )
```
